32 devices in a mesh: dp: 8 (over z, core), seq: 4 (over y, x).
Axes of the slice: x: 2, y: 2, z: 4, core: 2. Of those that a mesh axis runs over, the one named last changes fastest.
Arguments:
- layer_input: bfloat16 [16, 2048, 1024], P('dp', 'seq'), may hold values from -6 to 6
- cotangent: bfloat16 [16, 2048, 1024], P('dp', 'seq'), may hold values from -6 to 6
- doc_ids: int32 [16, 2048], P('dp'), may hold values from 0 to 5, never falling along the last dimension, each value on 1 to 1024 neighbouring positions
- resets: int32 [16, 2048], P('dp'), may hold values 0 or 1
- mix_weight: bfloat16 [1024, 4224], P(('dp', 'seq')), may hold values from -0.1875 to 0.1875
- value_weight: bfloat16 [1024, 2048], P(('dp', 'seq')), may hold values from -0.1875 to 0.1875
- head_weight: bfloat16 [2048, 1024], P(('dp', 'seq')), may hold values from -0.5 to 0.5
- expand_weight: bfloat16 [1024, 4096], P(('dp', 'seq')), may hold values from -0.1875 to 0.1875
- shrink_weight: bfloat16 [4096, 1024], P(('dp', 'seq')), may hold values from -0.09375 to 0.09375
- chan_vectors: float32 [3, 1024], replicated, may hold values from 0.25 to 1.75
- ema_logits: float32 [2, 1024, 16], replicated, may hold values from -5 to 0
- ema_beta_eta: float32 [2, 1024, 16], replicated, may hold values from -3 to 3
- z_affine: float32 [3, 128], replicated, may hold values from -6 to 6
Outputs:
- output: bfloat16 [16, 2048, 1024], P('dp', 'seq')
- x_grad: float32 [16, 2048, 1024], P('dp', 'seq')
- mix_grad: float32 [1024, 4224], P(('dp', 'seq'))
- value_grad: float32 [1024, 2048], P(('dp', 'seq'))
- head_grad: float32 [2048, 1024], P(('dp', 'seq'))
- expand_grad: float32 [1024, 4096], P(('dp', 'seq'))
- shrink_grad: float32 [4096, 1024], P(('dp', 'seq'))
- chan_grad: float32 [3, 1024], replicated
- logits_grad: float32 [2, 1024, 16], replicated
- coef_grad: float32 [2, 1024, 16], replicated
- affine_grad: float32 [3, 128], replicated
The draws below stay inside these ranges and needn't reach their ends.
All inputs are finite; a program needn't handle non-finite values. No bound on the sum of `resets` on one device may be relied on, other than what follows from the above.
Results may differ from the reference program's by a relative error of at most 0.023.
The reference program's roundings to bfloat16 on the way count: a program that leaves them out, or rounds other values in their place, can miss the bound.
Values may be sent and summed in bfloat16 or wider, within the bound.
A program may use at most 576 MiB of HBM per device.

```python
import math
import jax
import jax.numpy as jnp
import numpy as np
from jax import lax

D = 1024
Z = 128
V = 2048
EMA_DIM = 16
FF = 4096
SEQ_LEN = 2048
ROWS = 16


def set_ends(array, key, least, largest):
    longest = array.shape.index(max(array.shape))
    spots = []
    for shift in (0, 1):
        where = [jax.random.randint(jax.random.fold_in(key, axis), (), 0, length) for axis, length in enumerate(array.shape)]
        where[longest] = (where[longest] + shift) % array.shape[longest]
        spots.append(tuple(where))
    return array.at[spots[0]].set(least).at[spots[1]].set(largest)


def level_of(key, extent, shards, smallest, largest):
    loudness = 1.0
    for axis_at, blocks in shards:
        draws = jax.random.uniform(jax.random.fold_in(jax.random.fold_in(key, 6), axis_at), (blocks,), jnp.float32, smallest / len(shards), largest / len(shards))
        loudness = loudness * jnp.repeat(jnp.exp(draws), extent[axis_at] // blocks).reshape((-1,) + (1,) * (len(extent) - 1 - axis_at))
    return loudness


def length_profile(amount, total, limit, lean):
    portions = [(1 << 20) // math.isqrt(grade ** lean) + 1 for grade in range(2, amount + 1)]
    surplus, given = total - limit - (amount - 1), [1] * (amount - 1)
    while surplus > 0:
        movable = [i for i in range(amount - 1) if given[i] < limit]
        whole, remaining = sum([portions[i] for i in movable]), surplus
        for i in movable:
            more = min(limit - given[i], max(1, remaining * portions[i] // whole), surplus)
            given[i] = given[i] + more
            surplus = surplus - more
    return np.array([limit] + given)


def uneven_parts(key, number_of, total, reach, skew):
    if number_of == 2:
        one = jax.random.randint(key, (), max(1, total - reach), min(reach, total - 1) + 1)
        return jnp.stack([one, total - one])
    sizes = jnp.asarray(length_profile(number_of, total, reach, skew), jnp.int32)
    pairs = (number_of - 1) // 2
    donor, sink = sizes[1:1 + 2 * pairs:2], sizes[2:2 + 2 * pairs:2]
    slack = jnp.minimum(donor - 1, reach - sink)
    passed = jax.random.randint(jax.random.fold_in(key, 1), (pairs,), 0, 1 << 20) % (slack + 1)
    sizes = sizes.at[1:1 + 2 * pairs:2].set(donor - passed).at[2:2 + 2 * pairs:2].set(sink + passed)
    return sizes[jax.random.permutation(jax.random.fold_in(key, 2), number_of)]


def gaussian(own_key, shape, deviation, limit, pieces=(), held_as=jnp.bfloat16):
    array = deviation * jax.random.normal(own_key, shape, jnp.float32)
    if pieces:
        array = array * level_of(own_key, shape, pieces, -0.22, 0.18)
    return jnp.clip(array, -limit, limit).astype(held_as)


def setup_inputs(seed: int = 0) -> dict:
    streams_of = jax.random.split(jax.random.key(seed), 14)
    layer_input = gaussian(streams_of[0], (ROWS, SEQ_LEN, D), 1.0, 6.0, ((0, 8), (1, 4)))
    cotangent = gaussian(streams_of[1], (ROWS, SEQ_LEN, D), 1.0, 6.0, ((0, 8), (1, 4)))
    doc_ids = jax.vmap(lambda own: jnp.searchsorted(jnp.cumsum(uneven_parts(own, 6, SEQ_LEN, SEQ_LEN // 2, 2)), jnp.arange(SEQ_LEN), side="right"))(jax.random.split(streams_of[2], ROWS)).reshape((ROWS, SEQ_LEN)).astype(jnp.int32)
    resets = set_ends((jax.random.randint(streams_of[3], (ROWS, SEQ_LEN), 0, 128) < 1).astype(jnp.int32), jax.random.fold_in(streams_of[3], 1), 0, 1)
    mix_weight = gaussian(streams_of[4], (D, Z + V + 2 * D), D ** -0.5, 0.1875, ((0, 32),))
    value_weight = gaussian(streams_of[5], (D, V), D ** -0.5, 0.1875, ((0, 32),))
    head_weight = gaussian(streams_of[6], (V, D), (V // 16) ** -0.5, 0.5, ((0, 32),))
    expand_weight = gaussian(streams_of[7], (D, FF), D ** -0.5, 0.1875, ((0, 32),))
    shrink_weight = gaussian(streams_of[8], (FF, D), FF ** -0.5, 0.09375, ((0, 32),))
    chan_vectors = jnp.clip(1.0 + 0.15 * jax.random.normal(streams_of[9], (3, D), jnp.float32), 0.25, 1.75)
    ema_logits = jnp.clip(jax.random.uniform(streams_of[10], (2, D, EMA_DIM), jnp.float32, -5.0, 0.0), -5.0, 0.0)
    ema_beta_eta = gaussian(streams_of[11], (2, D, EMA_DIM), 0.5, 3.0, (), jnp.float32)
    z_affine = gaussian(streams_of[12], (3, Z), 2.0, 6.0, (), jnp.float32)
    return {"layer_input": layer_input, "cotangent": cotangent, "doc_ids": doc_ids, "resets": resets, "mix_weight": mix_weight, "value_weight": value_weight, "head_weight": head_weight, "expand_weight": expand_weight, "shrink_weight": shrink_weight, "chan_vectors": chan_vectors, "ema_logits": ema_logits, "ema_beta_eta": ema_beta_eta, "z_affine": z_affine}


HIGH_MODE = lax.Precision.HIGHEST

@jax.custom_vjp
def low(v):
    return lax.optimization_barrier(v.astype(jnp.bfloat16)).astype(jnp.float32)

@jax.custom_vjp
def low_back(v):
    return v

def low_keep(v):
    return (low(v), None)

def low_pass(kept, grad):
    return (grad,)

def back_keep(v):
    return (v, None)

def back_low(kept, grad):
    return (low(grad),)
low.defvjp(low_keep, low_pass)
low_back.defvjp(back_keep, back_low)

def matmul(left, right):
    return jnp.dot(left, right, precision=HIGH_MODE, preferred_element_type=jnp.float32)

def layer_norm(values):
    center = values - lax.optimization_barrier(jnp.mean(values, axis=-1, keepdims=True))
    spread = lax.optimization_barrier(jnp.mean(center * center, axis=-1, keepdims=True))
    return center * lax.rsqrt(spread + 1e-05)

def ema_scan(inputs, reset_row, ema_logits, ema_beta_eta):
    rate = jax.nn.sigmoid(ema_logits[0])
    damping = jax.nn.sigmoid(ema_logits[1])
    decay = 1.0 - rate * damping
    weight_in = rate * ema_beta_eta[0]
    weight_out = ema_beta_eta[1]

    def advance(state, item):
        current, flag = item
        keep = (1 - flag).astype(jnp.float32)
        state = keep * decay * state + weight_in * current[:, None]
        return (state, lax.optimization_barrier(jnp.sum(weight_out * state, axis=1)))
    start = jnp.zeros(decay.shape, jnp.float32)
    _, result = lax.scan(advance, start, (inputs, reset_row))
    return result

def layer_row(params, input_row, doc_row, reset_row):
    mix_weight, value_weight, head_weight, expand_weight, shrink_weight, chan_vectors, ema_logits, ema_beta_eta, z_affine = params
    normed = layer_norm(input_row) * chan_vectors[0]
    normed_low = low(normed)
    ema_out = ema_scan(low_back(normed_low), reset_row, ema_logits, ema_beta_eta)
    ema_sent = low_back(low(ema_out))
    mixed = jax.nn.silu(ema_sent + chan_vectors[2] * normed)
    projected = low_back(matmul(low(mixed), mix_weight))
    shared = jax.nn.silu(projected[:, :Z])
    reset_gate = jax.nn.silu(projected[:, Z:Z + V])
    head_base = projected[:, Z + V:Z + V + D]
    update_gate = jax.nn.sigmoid(projected[:, Z + V + D:])
    queries = low(shared * z_affine[0] + z_affine[1])
    keys = low_back(low(shared * z_affine[2]))
    values = low_back(low(jax.nn.silu(low_back(matmul(normed_low, value_weight)))))
    scores = low_back(matmul(queries, keys.T) * Z ** (-0.5))
    places = jnp.arange(SEQ_LEN)
    allowed = (places[None, :] <= places[:, None]) & (doc_row[None, :] == doc_row[:, None])
    scores = jnp.where(allowed, scores, -1000000000.0)
    probs = jax.nn.softmax(scores, axis=-1)
    attended = low_back(matmul(low(probs), values))
    gated = low(reset_gate * attended)
    candidate = jax.nn.silu(head_base + low_back(matmul(gated, head_weight)))
    first = input_row + update_gate * (candidate - input_row)
    second = low(layer_norm(first) * chan_vectors[1])
    hidden = low(jax.nn.silu(low_back(matmul(second, expand_weight))))
    return first + matmul(hidden, shrink_weight)

def reference(layer_input, cotangent, doc_ids, resets, mix_weight, value_weight, head_weight, expand_weight, shrink_weight, chan_vectors, ema_logits, ema_beta_eta, z_affine):
    params = tuple((item.astype(jnp.float32) for item in (mix_weight, value_weight, head_weight, expand_weight, shrink_weight, chan_vectors, ema_logits, ema_beta_eta, z_affine)))

    def whole(weights, inputs):

        def step(carry, item):
            input_row, doc_row, reset_row = item
            return (carry, layer_row(weights, input_row, doc_row, reset_row))
        _, outputs = lax.scan(jax.checkpoint(step), jnp.zeros((), jnp.float32), (inputs, doc_ids, resets))
        return outputs
    result, pull = jax.vjp(whole, params, layer_input.astype(jnp.float32))
    grads, x_grad = pull(cotangent.astype(jnp.float32))
    return (result.astype(jnp.bfloat16), x_grad, grads[0], grads[1], grads[2], grads[3], grads[4], grads[5], grads[6], grads[7], grads[8])
```

```python
import functools
import jax
import jax.numpy as jnp
from jax import lax
from jax.experimental import pallas as pl
from jax.experimental.pallas import tpu as pltpu
from jax.sharding import PartitionSpec as P

LANES = 128
EMA_STEP = 16
EMA_WIDTH = 512


def lane(group):
    return slice(group * LANES, (group + 1) * LANES)


def half_of(group, half):
    return (slice(half * 8, half * 8 + 8), lane(group))


def row_of(ref, step, group):
    return ref[group, pl.ds(step, 8, stride=0), :]


def widen(low_ref, wide_ref):
    for group in range(wide_ref.shape[0]):
        wide_ref[group] = low_ref[0, :, lane(group)].astype(jnp.float32)


def fold_rows(part_ref, group):
    halves = []
    for half in range(EMA_STEP // 8):
        base = group * EMA_STEP * 8 + half * 64
        total = part_ref[pl.ds(base, 8, stride=8), :]
        for sub in range(1, 8):
            total = total + part_ref[pl.ds(base + sub, 8, stride=8), :]
        halves.append(total)
    return jnp.concatenate(halves, axis=0)


def ema_last_kernel(reverse, feed_ref, keep_ref, decay_ref, last_ref, feed32):
    length, width = feed_ref.shape[1:]
    groups = width // LANES
    widen(feed_ref, feed32)
    pairs = [(g, h) for g in range(groups) for h in range(2)]

    def body(index, states):
        states = list(states)
        block = (length // EMA_STEP - 1 - index) if reverse else index
        base = pl.multiple_of(block * EMA_STEP, EMA_STEP)
        for offset in range(EMA_STEP):
            step = base + (EMA_STEP - 1 - offset if reverse else offset)
            keep = row_of(keep_ref, step, 0)
            for at, (g, h) in enumerate(pairs):
                feed = row_of(feed32, step, g)
                kept = keep * decay_ref[half_of(g, h)]
                if reverse:
                    states[at] = kept * (states[at] + feed)
                else:
                    states[at] = kept * states[at] + feed
        return tuple(states)

    zero = jnp.zeros((8, LANES), jnp.float32)
    states = lax.fori_loop(0, length // EMA_STEP, body, (zero,) * len(pairs))
    for at, (g, h) in enumerate(pairs):
        last_ref[(0,) + half_of(g, h)] = states[at]


def ema_forward_kernel(feed_ref, keep_ref, decay_ref, gain_ref, start_ref, out_ref, feed32, part_ref):
    length, width = feed_ref.shape[1:]
    groups = width // LANES
    widen(feed_ref, feed32)
    pairs = [(g, h) for g in range(groups) for h in range(2)]

    def body(index, states):
        states = list(states)
        base = pl.multiple_of(index * EMA_STEP, EMA_STEP)
        for offset in range(EMA_STEP):
            keep = row_of(keep_ref, base + offset, 0)
            for g in range(groups):
                feed = row_of(feed32, base + offset, g)
                both = []
                for h in range(2):
                    at = g * 2 + h
                    states[at] = (keep * decay_ref[half_of(g, h)]) * states[at] + feed
                    both.append(gain_ref[half_of(g, h)] * states[at])
                spot = g * EMA_STEP * 8 + offset * 8
                part_ref[spot : spot + 8, :] = both[0] + both[1]
        for g in range(groups):
            out_ref[0, pl.ds(base, EMA_STEP), lane(g)] = fold_rows(part_ref, g).astype(jnp.bfloat16)
        return tuple(states)

    start = tuple(start_ref[(0,) + half_of(g, h)] for g, h in pairs)
    lax.fori_loop(0, length // EMA_STEP, body, start)


def ema_backward_kernel(
    feed_ref, grad_ref, keep_ref, decay_ref, gain_ref, start_ref, end_ref,
    back_ref, gain_grad_ref, decay_grad_ref, feed32, grad32, part_ref, held_ref,
):
    length, width = feed_ref.shape[1:]
    groups = width // LANES
    widen(feed_ref, feed32)
    widen(grad_ref, grad32)
    pairs = [(g, h) for g in range(groups) for h in range(2)]
    blocks = length // EMA_STEP

    def forward(index, states):
        states = list(states)
        base = pl.multiple_of(index * EMA_STEP, EMA_STEP)
        for offset in range(EMA_STEP):
            keep = row_of(keep_ref, base + offset, 0)
            for at, (g, h) in enumerate(pairs):
                kept = keep * states[at]
                held_ref[pl.ds((base + offset) * 16 + h * 8, 8), lane(g)] = kept
                states[at] = decay_ref[half_of(g, h)] * kept + row_of(feed32, base + offset, g)
        return tuple(states)

    start = tuple(start_ref[(0,) + half_of(g, h)] for g, h in pairs)
    lax.fori_loop(0, blocks, forward, start)

    def backward(index, carried):
        pulls, gains, decays = (list(c) for c in carried)
        base = pl.multiple_of((blocks - 1 - index) * EMA_STEP, EMA_STEP)
        for offset in reversed(range(EMA_STEP)):
            step = base + offset
            keep = row_of(keep_ref, step, 0)
            for g in range(groups):
                grad = row_of(grad32, step, g)
                feed = row_of(feed32, step, g)
                both = []
                for h in range(2):
                    at = g * 2 + h
                    local = pulls[at] + grad
                    both.append(gain_ref[half_of(g, h)] * local)
                    gains[at] = gains[at] + local * feed
                    held = held_ref[pl.ds(step * 16 + h * 8, 8), lane(g)]
                    decays[at] = decays[at] + local * held
                    pulls[at] = (keep * decay_ref[half_of(g, h)]) * local
                spot = g * EMA_STEP * 8 + offset * 8
                part_ref[spot : spot + 8, :] = both[0] + both[1]
        for g in range(groups):
            back_ref[0, pl.ds(base, EMA_STEP), lane(g)] = fold_rows(part_ref, g).astype(jnp.bfloat16)
        return (tuple(pulls), tuple(gains), tuple(decays))

    end = tuple(end_ref[(0,) + half_of(g, h)] for g, h in pairs)
    zeros = (jnp.zeros((8, LANES), jnp.float32),) * len(pairs)
    _, gains, decays = lax.fori_loop(0, blocks, backward, (end, zeros, zeros))
    for at, (g, h) in enumerate(pairs):
        gain_grad_ref[(0,) + half_of(g, h)] = gains[at]
        decay_grad_ref[(0,) + half_of(g, h)] = decays[at]


def ema_specs(length, width):
    rows = pl.BlockSpec((1, length, width), lambda r, c: (r, 0, c))
    keep = pl.BlockSpec((1, length, LANES), lambda r, c: (r, 0, 0))
    coef = pl.BlockSpec((16, width), lambda r, c: (0, c))
    state = pl.BlockSpec((1, 16, width), lambda r, c: (r, 0, c))
    return rows, keep, coef, state


def ema_call(kernel, name, ins, outs, args, shapes, scratch, ops):
    rows, length, chans = args[0].shape
    width = min(EMA_WIDTH, chans)
    specs = dict(zip("rkcs", ema_specs(length, width)))
    sizes = {"r": (rows, length, chans), "s": (rows, 16, chans)}
    kinds = {"r": jnp.bfloat16, "s": jnp.float32}
    scratches = [pltpu.VMEM((width // LANES, length, LANES), jnp.float32)] * scratch[0]
    if scratch[1]:
        scratches.append(pltpu.VMEM((width // LANES * EMA_STEP * 8, LANES), jnp.float32))
    if scratch[2]:
        scratches.append(pltpu.VMEM((length * 16, width), jnp.float32))
    return pl.pallas_call(
        kernel,
        out_shape=[jax.ShapeDtypeStruct(sizes[o], kinds[o]) for o in outs],
        grid=(rows, chans // width),
        in_specs=[specs[i] for i in ins],
        out_specs=[specs[o] for o in outs],
        scratch_shapes=scratches,
        compiler_params=pltpu.CompilerParams(vmem_limit_bytes=(40 if scratch[2] else 16) * 2**20),
        cost_estimate=pl.CostEstimate(
            flops=ops * rows * length * chans * 16, bytes_accessed=4 * rows * length * chans, transcendentals=0
        ),
        name=name,
    )(*args)


def ema_last(feed, keep, decay, reverse):
    return ema_call(
        functools.partial(ema_last_kernel, reverse), "ema_back_last" if reverse else "ema_last",
        "rkc", "s", (feed, keep, decay), None, (1, 0, 0), 4)[0]


def ema_forward(feed, keep, decay, gain, start):
    return ema_call(ema_forward_kernel, "ema_forward", "rkccs", "r", (feed, keep, decay, gain, start), None, (1, 1, 0), 6)[0]


def ema_backward(feed, grad, keep, decay, gain, start, end):
    return ema_call(
        ema_backward_kernel, "ema_backward", "rrkccss", "rss",
        (feed, grad, keep, decay, gain, start, end), None, (2, 1, 1), 16)


Z = 128
V = 2048
REACH = 1024
NEG_FILL = -1000000000.0
BOTH = ("dp", "seq")


def layer_norm(values):
    center = values - jnp.mean(values, axis=-1, keepdims=True)
    spread = jnp.mean(center * center, axis=-1, keepdims=True)
    return center * lax.rsqrt(spread + 1e-05)


def scaled_norm(values, gain):
    return layer_norm(values) * gain


def silu_slope(values):
    squash = jax.nn.sigmoid(values)
    return squash * (1.0 + values * (1.0 - squash))


def product(left, right):
    return jnp.dot(left, right, preferred_element_type=jnp.float32)


def against(left, right):
    return lax.dot_general(left, right, (((1,), (1,)), ((), ())), preferred_element_type=jnp.float32)


def transposed(left, right):
    return lax.dot_general(left, right, (((0,), (0,)), ((), ())), preferred_element_type=jnp.float32)


def low(values):
    return values.astype(jnp.bfloat16)


def shift_seq(values, by):
    count = lax.axis_size("seq")
    pairs = [(i, i + by) for i in range(count) if 0 <= i + by < count]
    return lax.ppermute(values, "seq", pairs)


def gather_weight(shard):
    return lax.all_gather(shard, BOTH, axis=0, tiled=True)


def scatter_grad(grad):
    return lax.psum_scatter(low(grad), BOTH, scatter_dimension=0, tiled=True).astype(jnp.float32)


def carried(last, alive, decay_all, forward):
    count = lax.axis_size("seq")
    place = lax.axis_index("seq")
    total = jnp.zeros_like(last)
    through = jnp.ones((last.shape[0], 1, 1), jnp.float32)
    power = None
    for away in range(1, count):
        arrived = shift_seq(last, away if forward else -away)
        factor = through if power is None else through * power
        total = total + factor * arrived
        at = jnp.clip(place - away if forward else place + away, 0, count - 1)
        through = through * lax.dynamic_slice_in_dim(alive, at, 1, 1)[:, :, None]
        power = decay_all if power is None else power * decay_all
    return total


def on_device(
    layer_input,
    cotangent,
    doc_ids,
    resets,
    mix_weight,
    value_weight,
    head_weight,
    expand_weight,
    shrink_weight,
    chan_vectors,
    ema_logits,
    ema_beta_eta,
    z_affine,
):
    seq_count = lax.axis_size("seq")
    seq_place = lax.axis_index("seq")
    rows, places, width = layer_input.shape
    tokens = rows * places
    scale = Z ** (-0.5)
    halo = min(-(-(REACH - 1) // places), seq_count - 1)
    window = (halo + 1) * places

    value_full = gather_weight(value_weight)
    mix_full = gather_weight(mix_weight)
    head_full = gather_weight(head_weight)
    expand_full = gather_weight(expand_weight)
    shrink_full = gather_weight(shrink_weight)

    inputs32 = layer_input.astype(jnp.float32)
    normed, first_pull = jax.vjp(scaled_norm, inputs32, chan_vectors[0])
    normed_low = low(normed)
    normed_parts = [shift_seq(normed_low, by) for by in range(halo, 0, -1)] + [normed_low]
    normed_window = jnp.concatenate(normed_parts, axis=1).reshape(rows * window, width)

    rate = jax.nn.sigmoid(ema_logits[0])
    damping = jax.nn.sigmoid(ema_logits[1])
    decay = (1.0 - rate * damping).T
    weight_in = rate * ema_beta_eta[0]
    weight_out = ema_beta_eta[1]
    gain = (weight_in * weight_out).T
    decay_all = decay
    reach = 1
    while reach < places:
        decay_all = decay_all * decay_all
        reach *= 2
    keep_row = 1.0 - resets.astype(jnp.float32)
    keep_own = lax.dynamic_slice_in_dim(keep_row, seq_place * places, places, 1)
    keep = jnp.broadcast_to(keep_own[:, None, :, None], (rows, 1, places, LANES)).reshape(rows, places, LANES)
    alive = jnp.min(keep_row.reshape(rows, seq_count, places), axis=2)

    last = ema_last(normed_low, keep, decay, False)
    start = carried(last, alive, decay_all, True)
    ema_low = ema_forward(normed_low, keep, decay, gain, start)

    premix = (ema_low.astype(jnp.float32) + chan_vectors[2] * normed).reshape(tokens, width)
    mixed_low = low(jax.nn.silu(premix))
    value_pre = product(normed_window, value_full)
    values_low = low(jax.nn.silu(value_pre)).reshape(rows, window, V)
    projected = product(mixed_low, mix_full)
    shared_pre = projected[:, :Z]
    reset_pre = projected[:, Z : Z + V]
    head_base = projected[:, Z + V : Z + V + width]
    update_pre = projected[:, Z + V + width :]
    shared = jax.nn.silu(shared_pre)
    queries_low = low(shared * z_affine[0] + z_affine[1]).reshape(rows, places, Z)
    keys_low = low(shared * z_affine[2]).reshape(rows, places, Z)
    key_window = jnp.concatenate([shift_seq(keys_low, by) for by in range(halo, 0, -1)] + [keys_low], axis=1)
    reset_gate = jax.nn.silu(reset_pre)
    update_gate = jax.nn.sigmoid(update_pre)

    padded_docs = jnp.pad(doc_ids, ((0, 0), (halo * places, 0)), constant_values=-1)
    key_docs = lax.dynamic_slice_in_dim(padded_docs, seq_place * places, window, 1)
    query_docs = key_docs[:, halo * places :]
    causal = jnp.arange(window)[None, :] <= jnp.arange(places)[:, None] + halo * places
    allowed = causal[None] & (query_docs[:, :, None] == key_docs[:, None, :])
    scores = jnp.einsum("rid,rjd->rij", queries_low, key_window, preferred_element_type=jnp.float32) * scale
    scores = jnp.where(allowed, scores, NEG_FILL)
    peak = jnp.max(scores, axis=-1, keepdims=True)
    expo = jnp.exp(scores - peak)
    total = jnp.sum(expo, axis=-1, keepdims=True)
    probs = expo / total
    probs_low = low(probs)
    attended = jnp.einsum(
        "rij,rjv->riv", probs_low, values_low, preferred_element_type=jnp.float32
    ).reshape(tokens, V)
    gated_low = low(reset_gate * attended)
    head_pre = head_base + product(gated_low, head_full)
    candidate = jax.nn.silu(head_pre)
    residual_in = inputs32.reshape(tokens, width)
    first = residual_in + update_gate * (candidate - residual_in)
    second, second_pull = jax.vjp(scaled_norm, first, chan_vectors[1])
    second_low = low(second)
    expand_pre = product(second_low, expand_full)
    hidden_low = low(jax.nn.silu(expand_pre))
    output = low(first + product(hidden_low, shrink_full)).reshape(rows, places, width)

    cot_low = cotangent.reshape(tokens, width)
    shrink_grad = scatter_grad(transposed(hidden_low, cot_low))
    d_expand = low(against(cot_low, shrink_full) * silu_slope(expand_pre))
    expand_grad = scatter_grad(transposed(second_low, d_expand))
    d_first_norm, d_gain_two = second_pull(against(d_expand, expand_full))
    d_first = cot_low.astype(jnp.float32) + d_first_norm
    d_update = d_first * (candidate - residual_in) * update_gate * (1.0 - update_gate)
    d_direct = d_first * (1.0 - update_gate)
    d_head = d_first * update_gate * silu_slope(head_pre)
    d_head_low = low(d_head)
    head_grad = scatter_grad(transposed(gated_low, d_head_low))
    d_gated = against(d_head_low, head_full)
    d_reset = d_gated * attended * silu_slope(reset_pre)
    d_attended = low(d_gated * reset_gate).reshape(rows, places, V)
    d_probs = jnp.einsum("riv,rjv->rij", d_attended, values_low, preferred_element_type=jnp.float32)
    balance = jnp.sum(probs * d_probs, axis=-1, keepdims=True)
    d_scores = low(probs * (d_probs - balance))
    d_queries = scale * jnp.einsum("rij,rjd->rid", d_scores, key_window, preferred_element_type=jnp.float32)
    key_term = scale * jnp.einsum("rij,rid->rjd", d_scores, queries_low, preferred_element_type=jnp.float32)
    d_keys = key_term[:, halo * places :]
    for by in range(1, halo + 1):
        begin = (halo - by) * places
        d_keys = d_keys + shift_seq(low(key_term[:, begin : begin + places]), -by).astype(jnp.float32)
    d_keys32 = low(d_keys).astype(jnp.float32).reshape(tokens, Z)
    d_values = jnp.einsum("rij,riv->rjv", probs_low, d_attended, preferred_element_type=jnp.float32)
    d_value_pre = low(d_values.reshape(rows * window, V) * silu_slope(value_pre))
    value_grad = scatter_grad(transposed(normed_window, d_value_pre))
    value_term = against(d_value_pre, value_full).reshape(rows, window, width)
    d_normed_value = value_term[:, halo * places :]
    for by in range(1, halo + 1):
        begin = (halo - by) * places
        d_normed_value = d_normed_value + shift_seq(low(value_term[:, begin : begin + places]), -by).astype(jnp.float32)
    d_query_flat = d_queries.reshape(tokens, Z)
    d_shared = d_query_flat * z_affine[0] + d_keys32 * z_affine[2]
    affine_part = jnp.stack(
        [
            jnp.sum(d_query_flat * shared, axis=0),
            jnp.sum(d_query_flat, axis=0),
            jnp.sum(d_keys32 * shared, axis=0),
        ]
    )
    d_projected = low(
        jnp.concatenate([d_shared * silu_slope(shared_pre), d_reset, d_head, d_update], axis=1)
    )
    mix_grad = scatter_grad(transposed(mixed_low, d_projected))
    d_premix = against(d_projected, mix_full) * silu_slope(premix)
    omega_part = jnp.sum(d_premix * normed.reshape(tokens, width), axis=0)
    d_premix = d_premix.reshape(rows, places, width)
    d_ema = low(d_premix)
    back_last = ema_last(d_ema, keep, decay, True)
    end = carried(back_last, alive, decay_all, False)
    d_feed, gain_parts, decay_parts = ema_backward(normed_low, d_ema, keep, decay, gain, start, end)
    d_normed = d_premix * chan_vectors[2] + d_normed_value + d_feed.astype(jnp.float32)
    d_input_norm, d_gain_one = first_pull(d_normed)
    x_grad = d_direct.reshape(rows, places, width) + d_input_norm

    chan_grad, gain_sum, decay_sum, affine_grad = lax.psum(
        (
            jnp.stack([d_gain_one, d_gain_two, omega_part]),
            jnp.sum(gain_parts, axis=0),
            jnp.sum(decay_parts, axis=0),
            affine_part,
        ),
        BOTH,
    )
    d_gain = gain_sum.T
    d_decay = (decay_sum * gain).T
    d_weight_in = d_gain * weight_out
    coef_grad = jnp.stack([d_weight_in * rate, d_gain * weight_in])
    d_rate = d_weight_in * ema_beta_eta[0] - d_decay * damping
    d_damping = -d_decay * rate
    logits_grad = jnp.stack([d_rate * rate * (1.0 - rate), d_damping * damping * (1.0 - damping)])
    return (
        output,
        x_grad,
        mix_grad,
        value_grad,
        head_grad,
        expand_grad,
        shrink_grad,
        chan_grad,
        logits_grad,
        coef_grad,
        affine_grad,
    )


def solution(mesh):
    placed = (
        P("dp", "seq", None),
        P("dp", "seq", None),
        P("dp", None),
        P("dp", None),
        P(BOTH, None),
        P(BOTH, None),
        P(BOTH, None),
        P(BOTH, None),
        P(BOTH, None),
        P(),
        P(),
        P(),
        P(),
    )
    return jax.shard_map(
        on_device,
        mesh=mesh,
        in_specs=placed,
        out_specs=(
            P("dp", "seq", None),
            P("dp", "seq", None),
            P(BOTH, None),
            P(BOTH, None),
            P(BOTH, None),
            P(BOTH, None),
            P(BOTH, None),
            P(),
            P(),
            P(),
            P(),
        ),
        check_vma=False,
    )
```

```python
import functools
import jax
import jax.numpy as jnp
from jax import lax
from jax.experimental import pallas as pl
from jax.experimental.pallas import tpu as pltpu
from jax.sharding import PartitionSpec as P

Z = 128
V = 2048
REACH = 1024
NEG_FILL = -1000000000.0
BOTH = ("dp", "seq")
MESH = pl.DeviceIdType.MESH
LANES = 128
EMA_STEP = 16
FORWARD_WIDTH = 512
BACKWARD_WIDTH = 256


def lanes_at(base, group):
    return pl.ds(pl.multiple_of(base + group * LANES, LANES), LANES)


def row_of(ref, step, group):
    return ref[group, pl.ds(step, 8, stride=0), :]


def widen(source, row, base, wide):
    for group in range(wide.shape[0]):
        wide[group] = source[row, :, lanes_at(base, group)].astype(jnp.float32)


def halves_of(ref, base, groups, row=None):
    spots = [(slice(h * 8, h * 8 + 8), lanes_at(base, g)) for g in range(groups) for h in range(2)]
    return [ref[spot] if row is None else ref[(row,) + spot] for spot in spots]


def put_halves(ref, base, values, row):
    for at, value in enumerate(values):
        g, h = divmod(at, 2)
        ref[row, h * 8 : h * 8 + 8, lanes_at(base, g)] = value


def add_halves(ref, first, base, values):
    for at, value in enumerate(values):
        g, h = divmod(at, 2)
        spot = (slice(first + h * 8, first + h * 8 + 8), lanes_at(base, g))
        ref[spot] = ref[spot] + value


def fold_rows(part, group):
    halves = []
    for half in range(EMA_STEP // 8):
        base = group * EMA_STEP * 8 + half * 64
        total = part[pl.ds(base, 8, stride=8), :]
        for sub in range(1, 8):
            total = total + part[pl.ds(base + sub, 8, stride=8), :]
        halves.append(total)
    return jnp.concatenate(halves, axis=0).astype(jnp.bfloat16)


def unit_of(index, width, chans):
    across = chans // width
    return lax.div(index, across), pl.multiple_of(lax.rem(index, across) * width, width)


def ema_last(reverse, row, base, feed, keep, decay, last, wide):
    length, groups = feed.shape[1], wide.shape[0]
    widen(feed, row, base, wide)
    decays = halves_of(decay, base, groups)

    def body(index, states):
        states = list(states)
        block = (length // EMA_STEP - 1 - index) if reverse else index
        first = pl.multiple_of(block * EMA_STEP, EMA_STEP)
        for offset in range(EMA_STEP):
            step = first + (EMA_STEP - 1 - offset if reverse else offset)
            kept = row_of(keep, step, row)
            for at in range(2 * groups):
                fed = row_of(wide, step, at // 2)
                if reverse:
                    states[at] = (kept * decays[at]) * (states[at] + fed)
                else:
                    states[at] = (kept * decays[at]) * states[at] + fed
        return tuple(states)

    zero = jnp.zeros((8, LANES), jnp.float32)
    put_halves(last, base, lax.fori_loop(0, length // EMA_STEP, body, (zero,) * (2 * groups)), row)


def ema_forward(row, base, feed, keep, decay, gain, start, out, wide, part):
    length, groups = feed.shape[1], wide.shape[0]
    widen(feed, row, base, wide)
    decays, gains = halves_of(decay, base, groups), halves_of(gain, base, groups)

    def body(index, states):
        states = list(states)
        first = pl.multiple_of(index * EMA_STEP, EMA_STEP)
        for offset in range(EMA_STEP):
            kept = row_of(keep, first + offset, row)
            for g in range(groups):
                fed = row_of(wide, first + offset, g)
                both = []
                for at in (2 * g, 2 * g + 1):
                    states[at] = (kept * decays[at]) * states[at] + fed
                    both.append(gains[at] * states[at])
                spot = g * EMA_STEP * 8 + offset * 8
                part[spot : spot + 8, :] = both[0] + both[1]
        for g in range(groups):
            out[row, pl.ds(first, EMA_STEP), lanes_at(base, g)] = fold_rows(part, g)
        return tuple(states)

    lax.fori_loop(0, length // EMA_STEP, body, tuple(halves_of(start, base, groups, row)))


def ema_backward(row, base, feed, grad, keep, decay, gain, start, end, back, sums, wide, wide_grad, part, held):
    length, groups = feed.shape[1], wide.shape[0]
    widen(feed, row, base, wide)
    widen(grad, row, base, wide_grad)
    decays, gains = halves_of(decay, base, groups), halves_of(gain, base, groups)
    blocks = length // EMA_STEP

    def forward(index, states):
        states = list(states)
        first = pl.multiple_of(index * EMA_STEP, EMA_STEP)
        for offset in range(EMA_STEP):
            kept = row_of(keep, first + offset, row)
            for at in range(2 * groups):
                g, h = divmod(at, 2)
                held[pl.ds((first + offset) * 16 + h * 8, 8), g * LANES : (g + 1) * LANES] = kept * states[at]
                states[at] = (kept * decays[at]) * states[at] + row_of(wide, first + offset, g)
        return tuple(states)

    lax.fori_loop(0, blocks, forward, tuple(halves_of(start, base, groups, row)))

    def backward(index, carried):
        pulls, gain_sums, decay_sums = (list(c) for c in carried)
        first = pl.multiple_of((blocks - 1 - index) * EMA_STEP, EMA_STEP)
        for offset in reversed(range(EMA_STEP)):
            step = first + offset
            kept = row_of(keep, step, row)
            for g in range(groups):
                pulled, fed = row_of(wide_grad, step, g), row_of(wide, step, g)
                both = []
                for h in range(2):
                    at = 2 * g + h
                    local = pulls[at] + pulled
                    both.append(gains[at] * local)
                    gain_sums[at] = gain_sums[at] + local * fed
                    before = held[pl.ds(step * 16 + h * 8, 8), g * LANES : (g + 1) * LANES]
                    decay_sums[at] = decay_sums[at] + local * before
                    pulls[at] = (kept * decays[at]) * local
                spot = g * EMA_STEP * 8 + offset * 8
                part[spot : spot + 8, :] = both[0] + both[1]
        for g in range(groups):
            back[row, pl.ds(first, EMA_STEP), lanes_at(base, g)] = fold_rows(part, g)
        return (tuple(pulls), tuple(gain_sums), tuple(decay_sums))

    zeros = (jnp.zeros((8, LANES), jnp.float32),) * (2 * groups)
    _, gain_sums, decay_sums = lax.fori_loop(
        0, blocks, backward, (tuple(halves_of(end, base, groups, row)), zeros, zeros)
    )
    add_halves(sums, 0, base, gain_sums)
    add_halves(sums, 16, base, decay_sums)


def layer_norm(values):
    center = values - jnp.mean(values, axis=-1, keepdims=True)
    spread = jnp.mean(center * center, axis=-1, keepdims=True)
    return center * lax.rsqrt(spread + 1e-05)


def scaled_norm(values, gain):
    return layer_norm(values) * gain


def silu_slope(values):
    squash = jax.nn.sigmoid(values)
    return squash * (1.0 + values * (1.0 - squash))


def product(left, right):
    return jnp.dot(left, right, preferred_element_type=jnp.float32)


def against(left, right):
    return lax.dot_general(left, right, (((1,), (1,)), ((), ())), preferred_element_type=jnp.float32)


def transposed(left, right):
    return lax.dot_general(left, right, (((0,), (0,)), ((), ())), preferred_element_type=jnp.float32)


def low(values):
    return values.astype(jnp.bfloat16)


def shift_seq(values, by):
    count = lax.axis_size("seq")
    pairs = [(i, i + by) for i in range(count) if 0 <= i + by < count]
    return lax.ppermute(values, "seq", pairs)


def side_of(count):
    side = 1
    while side * side < count:
        side *= 2
    return side


def shape_of():
    depth = lax.axis_size("dp") // 2
    seqs = lax.axis_size("seq")
    down = side_of(seqs)
    return depth, 2, down, seqs // down


def place_of():
    depth, cores, down, across = shape_of()
    dp, seq = lax.axis_index("dp"), lax.axis_index("seq")
    return lax.div(dp, cores), lax.rem(dp, cores), lax.div(seq, across), lax.rem(seq, across)


def peer_of(sizes, spot, axis, by):
    spot = list(spot)
    spot[axis] = lax.rem(spot[axis] + by, sizes[axis])
    return {"dp": spot[0] * sizes[1] + spot[1], "seq": spot[2] * sizes[3] + spot[3]}


def along(count, by):
    return {"dp": lax.axis_index("dp"), "seq": lax.rem(lax.axis_index("seq") + by, count)}


def greet(sizes, spot):
    barrier = pltpu.get_barrier_semaphore()
    seqs = sizes[2] * sizes[3]
    peers = [peer_of(sizes, spot, axis, by) for axis in (0, 1) for by in range(1, sizes[axis])]
    peers += [along(seqs, by) for by in range(1, seqs)]
    for peer in peers:
        pl.semaphore_signal(barrier, inc=1, device_id=peer, device_id_type=MESH)
    pl.semaphore_wait(barrier, len(peers))


def piece_shape(rows, columns):
    return (rows, columns) if rows % 16 == 0 else (rows * columns // LANES, LANES)


def share(total, parts, at):
    return total * at // parts, total * (at + 1) // parts


def spread_edge(seqs, edge, arrived, send, recv, forward):
    return [
        pltpu.make_async_remote_copy(
            src_ref=edge,
            dst_ref=arrived.at[by - 1],
            send_sem=send.at[by - 1],
            recv_sem=recv.at[by - 1],
            device_id=along(seqs, by if forward else seqs - by),
            device_id_type=MESH,
        )
        for by in range(1, seqs)
    ]


def join_edges(arrived, reach, power, entry):
    rows, _, chans = entry.shape

    def body(row, carry):
        for group in range(chans // LANES):
            spot = slice(group * LANES, (group + 1) * LANES)
            total = None
            for at in range(arrived.shape[0]):
                term = reach[at, row] * power[at, :, spot] * arrived[at, row, :, spot]
                total = term if total is None else total + term
            entry[row, :, spot] = total
        return carry

    lax.fori_loop(0, rows, body, 0)


class Halo:
    def __init__(self, count, seqs, feed, window, zero, send, recv, local, hand_send):
        place = lax.axis_index("seq")
        relay = seqs == 4 and count == 2
        self.items = []

        def copy(source, by, towards, sent):
            return pltpu.make_async_remote_copy(
                src_ref=source,
                dst_ref=window.at[:, count - by],
                send_sem=sent,
                recv_sem=recv.at[by - 1],
                device_id=along(seqs, towards),
                device_id_type=MESH,
            )

        for by in range(1, count + 1):
            gives = place + by < seqs
            if relay and by == 1:
                gives = jnp.logical_and(gives, place != 1)
            blank = pltpu.make_async_copy(zero, window.at[:, count - by], local.at[by - 1])
            self.items.append((gives, place >= by, copy(feed, by, by, send.at[by - 1]), blank))
        self.hands = (place == 3, copy(window.at[:, 0], 1, 3, hand_send.at[0])) if relay else None

    def start(self):
        for gives, takes, remote, blank in self.items:
            pl.when(gives)(remote.start)
            pl.when(jnp.logical_not(takes))(blank.start)

    def hand_on(self):
        if self.hands:
            at_hand, hand = self.hands

            @pl.when(at_hand)
            def _():
                self.items[1][2].wait_recv()
                hand.start()

    def wait(self):
        for at, (gives, takes, remote, blank) in enumerate(self.items):
            waits = takes
            if self.hands and at == 1:
                waits = jnp.logical_and(takes, jnp.logical_not(self.hands[0]))
            pl.when(waits)(remote.wait_recv)
            pl.when(jnp.logical_not(takes))(blank.wait)
            pl.when(gives)(remote.wait_send)
        if self.hands:
            pl.when(self.hands[0])(self.hands[1].wait_send)


def gather_kernel(sizes, count, halo, *refs):
    shards, (feed, keep, decay, gain, reach, power) = refs[:count], refs[count : count + 6]
    wholes, (window, entry, out) = refs[count + 6 : 2 * count + 6], refs[2 * count + 6 : 2 * count + 9]
    (
        send_sem, recv_sem, local_sem, edge, arrived, edge_send, edge_recv,
        zero, halo_send, halo_recv, halo_local, hand_send, wide_feed, part,
    ) = refs[2 * count + 9 :]
    rows, length, chans = feed.shape
    width = wide_feed.shape[0] * LANES
    seqs = sizes[2] * sizes[3]
    depth, cores, down, across = sizes
    spot = place_of()
    z, c, a, b = spot
    half = depth // 2
    greet(sizes, spot)
    slots = {}

    def copy(w, kind, source, target, axis, by):
        slot = slots.setdefault(kind, len(slots))
        return pltpu.make_async_remote_copy(
            src_ref=source,
            dst_ref=target,
            send_sem=send_sem.at[w, slot],
            recv_sem=recv_sem.at[w, slot],
            device_id=peer_of(sizes, spot, axis, by),
            device_id_type=MESH,
        )

    def block(w, a_by=0, b_by=0, part=None):
        at = pl.ds(0, depth) if part is None else part
        return wholes[w].at[at, c, lax.rem(a - a_by + down, down), lax.rem(b - b_by + across, across)]

    front, back = pl.ds(0, half), pl.ds(half, depth - half)
    local, line, wide, tall, cross, twin = [], [], [], [], [], []
    for w in range(count):
        own = wholes[w].at[z, c, a, b]
        local.append(pltpu.make_async_copy(shards[w], own, local_sem.at[w]))
        line.append([copy(w, ("z", k), shards[w], own, 0, k) for k in range(1, depth)])
        wide.append([copy(w, ("x", k), block(w), block(w), 3, k) for k in range(1, across)])
        tall.append([copy(w, ("y", l), block(w), block(w), 2, l) for l in range(1, down)])
        pairs = [(k, l) for k in range(1, across) for l in range(1, down)]
        cross.append(
            {
                (k, l): (
                    copy(w, ("f", k, l), block(w, 0, k, front), block(w, 0, k, front), 2, l),
                    copy(w, ("g", k, l), block(w, l, 0, back), block(w, l, 0, back), 3, k),
                )
                for k, l in pairs
            }
        )
        twin.append(
            {
                (l, k): copy(w, ("c", l, k), block(w, l, k), block(w, l, k), 1, 1)
                for l in range(down)
                for k in range(across)
            }
        )
    zero[...] = jnp.zeros_like(zero)
    around = Halo(halo, seqs, feed, window, zero, halo_send, halo_recv, halo_local, hand_send)
    own = pltpu.make_async_copy(feed, window.at[:, halo], local_sem.at[count])
    edges = spread_edge(seqs, edge, arrived, edge_send, edge_recv, True)
    for w in range(count):
        local[w].start()
    for item in line[0]:
        item.start()
    own.start()
    around.start()
    for w in range(1, min(2, count)):
        for item in line[w]:
            item.start()
    units = rows * (chans // width)

    def last_unit(index, carry):
        row, base = unit_of(index, width, chans)
        ema_last(False, row, base, feed, keep, decay, edge, wide_feed)
        return carry

    def forward_unit(index, carry):
        row, base = unit_of(index, width, chans)
        ema_forward(row, base, feed, keep, decay, gain, entry, out, wide_feed, part)
        return carry

    lax.fori_loop(0, units, last_unit, 0)
    for item in edges:
        item.start()
    for step in range(count + 2):
        if step < count:
            w = step
            local[w].wait()
            for item in line[w]:
                item.wait_recv()
            for item in wide[w] + tall[w]:
                item.start()
            twin[w][0, 0].start()
            if w + 2 < count:
                for item in line[w + 2]:
                    item.start()
        if 1 <= step <= count:
            w = step - 1
            for k in range(1, across):
                wide[w][k - 1].wait_recv()
                for l in range(1, down):
                    cross[w][k, l][0].start()
                twin[w][0, k].start()
            for l in range(1, down):
                tall[w][l - 1].wait_recv()
                for k in range(1, across):
                    cross[w][k, l][1].start()
                twin[w][l, 0].start()
        if step >= 2:
            w = step - 2
            for (k, l), both in cross[w].items():
                both[0].wait_recv()
                both[1].wait_recv()
                twin[w][l, k].start()
        if step == 0:
            for item in edges:
                item.wait()
            join_edges(arrived, reach, power, entry)
        if step == 1:
            around.hand_on()
        lax.fori_loop(*share(units, count + 2, step), forward_unit, 0)
    for w in range(count):
        for item in twin[w].values():
            item.wait()
        for item in line[w] + wide[w] + tall[w]:
            item.wait_send()
        for both in cross[w].values():
            both[0].wait_send()
            both[1].wait_send()
    own.wait()
    around.wait()


def vmem(count):
    return [pl.BlockSpec(memory_space=pltpu.VMEM)] * count


def anywhere(count):
    return [pl.BlockSpec(memory_space=pl.ANY)] * count


def gather_weights(shards, feed, keep, decay, gain, reach, power, halo):
    sizes = shape_of()
    depth, cores, down, across = sizes
    seqs = down * across
    count = len(shards)
    pieces = [piece_shape(*shard.shape) for shard in shards]
    slots = (depth - 1) + (across - 1) + (down - 1) + 2 * (across - 1) * (down - 1) + across * down
    rows, length, chans = feed.shape
    state = (rows, 16, chans)
    width = min(FORWARD_WIDTH, chans)
    results = pl.pallas_call(
        functools.partial(gather_kernel, sizes, count, halo),
        out_shape=[jax.ShapeDtypeStruct(sizes + piece, jnp.bfloat16) for piece in pieces]
        + [
            jax.ShapeDtypeStruct((rows, halo + 1, length, chans), jnp.bfloat16),
            jax.ShapeDtypeStruct(state, jnp.float32),
            jax.ShapeDtypeStruct(feed.shape, jnp.bfloat16),
        ],
        in_specs=anywhere(count) + vmem(6),
        out_specs=anywhere(count + 1) + vmem(2),
        scratch_shapes=[
            pltpu.SemaphoreType.DMA((count, slots)),
            pltpu.SemaphoreType.DMA((count, slots)),
            pltpu.SemaphoreType.DMA((count + 1,)),
            pltpu.VMEM(state, jnp.float32),
            pltpu.VMEM((seqs - 1,) + state, jnp.float32),
            pltpu.SemaphoreType.DMA((seqs - 1,)),
            pltpu.SemaphoreType.DMA((seqs - 1,)),
            pltpu.VMEM(feed.shape, jnp.bfloat16),
            pltpu.SemaphoreType.DMA((halo,)),
            pltpu.SemaphoreType.DMA((halo,)),
            pltpu.SemaphoreType.DMA((halo,)),
            pltpu.SemaphoreType.DMA((1,)),
            pltpu.VMEM((width // LANES, length, LANES), jnp.float32),
            pltpu.VMEM((width // LANES * EMA_STEP * 8, LANES), jnp.float32),
        ],
        compiler_params=pltpu.CompilerParams(collective_id=0, has_side_effects=True, vmem_limit_bytes=48 * 2**20),
        name="gather_weights",
    )(*[shard.reshape(piece) for shard, piece in zip(shards, pieces)], feed, keep, decay, gain, reach, power)
    total = depth * cores * down * across
    wholes = [whole.reshape(total * shard.shape[0], shard.shape[1]) for whole, shard in zip(results, shards)]
    return wholes, *results[count:]


def add_rows(target, total, others):
    rows = total.shape[0]
    chunk = 16 if rows % 16 == 0 else rows

    def body(index, carry):
        at = pl.ds(pl.multiple_of(index * chunk, chunk), chunk)
        result = total[at, :].astype(jnp.float32)
        for other in others:
            result = result + other[at, :].astype(jnp.float32)
        target[at, :] = result.astype(target.dtype)
        return carry

    lax.fori_loop(0, rows // chunk, body, 0)


def scatter_kernel(sizes, count, *refs):
    grads, small = refs[:count], refs[count]
    feed, grad, keep, decay, gain, start, reach, power = refs[count + 1 : count + 9]
    refs = refs[count + 9 :]
    outs, (small_out, back_out) = refs[:count], refs[count : count + 2]
    rest = refs[count + 2 :]
    rest, (
        edge, arrived, end, edge_send, edge_recv, wide, wide_grad, part, kept_states,
    ) = rest[:-9], rest[-9:]
    rows, length, chans = feed.shape
    width = wide.shape[0] * LANES
    seqs = sizes[2] * sizes[3]
    names = ("arrive", "own", "first_a", "first_b", "second_a", "second_b", "third")
    held = {name: rest[at * count : (at + 1) * count] for at, name in enumerate(names)}
    small_parts, send_sem, recv_sem, own_sem, small_send, small_recv = rest[len(names) * count :]
    depth, cores, down, across = sizes
    spot = place_of()
    z, c, a, b = spot
    half = depth // 2
    front, back = pl.ds(0, half), pl.ds(half, depth - half)
    greet(sizes, spot)
    slots = {}

    def copy(w, kind, source, target, axis, by):
        slot = slots.setdefault(kind, len(slots))
        return pltpu.make_async_remote_copy(
            src_ref=source,
            dst_ref=target,
            send_sem=send_sem.at[w, slot],
            recv_sem=recv_sem.at[w, slot],
            device_id=peer_of(sizes, spot, axis, by),
            device_id_type=MESH,
        )

    def at_a(by):
        return lax.rem(a + by, down)

    def at_b(by):
        return lax.rem(b + by, across)

    twin, first, second, third = [], [], [], []
    for w in range(count):
        arrive = held["arrive"][w]
        twin.append(copy(w, "c", grads[w].at[:, 1 - c], arrive, 1, 1))
        first.append(
            [
                copy(w, ("a1", k), arrive.at[front, :, at_b(k)], held["first_a"][w].at[k - 1], 3, k)
                for k in range(1, across)
            ]
            + [
                copy(w, ("b1", l), arrive.at[back, at_a(l)], held["first_b"][w].at[l - 1], 2, l)
                for l in range(1, down)
            ]
        )
        second.append(
            [
                copy(w, ("a2", l), arrive.at[front, at_a(l), b], held["second_a"][w].at[l - 1], 2, l)
                for l in range(1, down)
            ]
            + [
                copy(w, ("b2", k), arrive.at[back, a, at_b(k)], held["second_b"][w].at[k - 1], 3, k)
                for k in range(1, across)
            ]
        )
        third.append(
            [
                copy(w, ("z", k), arrive.at[lax.rem(z + k, depth), a, b], held["third"][w].at[k - 1], 0, k)
                for k in range(1, depth)
            ]
        )

    stages = [(axis, 1 << bit) for axis in (1, 2, 3, 0) for bit in range(sizes[axis].bit_length() - 1)]

    def small_copy(at):
        axis, bit = stages[at]
        mine = spot[axis]
        towards = jnp.where(lax.rem(mine // bit, 2) == 0, bit, sizes[axis] - bit)
        return pltpu.make_async_remote_copy(
            src_ref=small_out,
            dst_ref=small_parts.at[at],
            send_sem=small_send.at[at],
            recv_sem=small_recv.at[at],
            device_id=peer_of(sizes, spot, axis, towards),
            device_id_type=MESH,
        )

    def own_load(w, at):
        return pltpu.make_async_copy(grads[w].at[at, c], held["own"][w].at[lax.rem(at, 2)], own_sem.at[w, lax.rem(at, 2)])

    def add_own(w):
        own_load(w, 0).start()

        def body(at, carry):
            @pl.when(at + 1 < depth)
            def _():
                own_load(w, at + 1).start()

            own_load(w, at).wait()
            for down_at in range(down):
                for across_at in range(across):
                    spot_ref = held["arrive"][w].at[at, down_at, across_at]
                    add_rows(spot_ref, spot_ref, [held["own"][w].at[lax.rem(at, 2), down_at, across_at]])
            return carry

        lax.fori_loop(0, depth, body, 0)

    small_out[...] = small[...]
    edges = spread_edge(seqs, edge, arrived, edge_send, edge_recv, False)
    units = rows * (chans // width)

    def last_unit(index, carry):
        row, base = unit_of(index, width, chans)
        ema_last(True, row, base, grad, keep, decay, edge, wide)
        return carry

    def backward_unit(index, carry):
        row, base = unit_of(index, width, chans)
        ema_backward(
            row, base, feed, grad, keep, decay, gain, start, end, back_out, small_out, wide, wide_grad, part, kept_states
        )
        return carry

    for w in range(min(2, count)):
        twin[w].start()
    lax.fori_loop(0, units, last_unit, 0)
    for item in edges:
        item.start()
    busy = count - 1
    for step in range(max(count + 3, busy + len(stages))):
        if step < count:
            w = step
            twin[w].wait_recv()
            if w + 2 < count:
                twin[w + 2].start()
            add_own(w)
            for item in first[w]:
                item.start()
        if 1 <= step <= count:
            w = step - 1
            arrive = held["arrive"][w]
            for item in first[w]:
                item.wait_recv()
            for at in range(half):
                for l in range(down):
                    spot_ref = arrive.at[at, l, b]
                    add_rows(spot_ref, spot_ref, [held["first_a"][w].at[k, at, l] for k in range(across - 1)])
            for at in range(half, depth):
                for k in range(across):
                    spot_ref = arrive.at[at, a, k]
                    add_rows(spot_ref, spot_ref, [held["first_b"][w].at[l, at - half, k] for l in range(down - 1)])
            for item in second[w]:
                item.start()
        if 2 <= step <= count + 1:
            w = step - 2
            arrive = held["arrive"][w]
            for item in second[w]:
                item.wait_recv()
            for at in range(half):
                spot_ref = arrive.at[at, a, b]
                add_rows(spot_ref, spot_ref, [held["second_a"][w].at[l, at] for l in range(down - 1)])
            for at in range(half, depth):
                spot_ref = arrive.at[at, a, b]
                add_rows(spot_ref, spot_ref, [held["second_b"][w].at[k, at - half] for k in range(across - 1)])
            for item in third[w]:
                item.start()
        if 3 <= step <= count + 2:
            w = step - 3
            for item in third[w]:
                item.wait_recv()
            add_rows(outs[w], held["arrive"][w].at[z, a, b], [held["third"][w].at[k] for k in range(depth - 1)])
        if step == 0:
            for item in edges:
                item.wait()
            join_edges(arrived, reach, power, end)
        if step < busy:
            lax.fori_loop(*share(units, busy, step), backward_unit, 0)
        stage = step - busy
        if stage == -1:
            small_copy(0).start()
        if 0 <= stage < len(stages):
            small_copy(stage).wait()
            small_out[...] = small_out[...] + small_parts[stage]
            if stage + 1 < len(stages):
                small_copy(stage + 1).start()
    for w in range(count):
        for item in [twin[w]] + first[w] + second[w] + third[w]:
            item.wait_send()


def scatter_grads(grads, small, feed, grad, keep, decay, gain, start, reach, power):
    sizes = shape_of()
    depth, cores, down, across = sizes
    total = depth * cores * down * across
    count = len(grads)
    half = depth // 2
    pieces = [piece_shape(g.shape[0] // total, g.shape[1]) for g in grads]
    leads = (
        (depth, down, across),
        (2, down, across),
        (across - 1, half, down),
        (down - 1, depth - half, across),
        (down - 1, half),
        (across - 1, depth - half),
        (depth - 1,),
    )
    slots = 1 + 2 * (across - 1 + down - 1) + depth - 1
    stages = sum(size.bit_length() - 1 for size in sizes)
    rows, length, chans = feed.shape
    state = (rows, 16, chans)
    width = min(BACKWARD_WIDTH, chans)
    seqs = down * across
    results = pl.pallas_call(
        functools.partial(scatter_kernel, sizes, count),
        out_shape=[jax.ShapeDtypeStruct(piece, jnp.float32) for piece in pieces]
        + [
            jax.ShapeDtypeStruct(small.shape, jnp.float32),
            jax.ShapeDtypeStruct(feed.shape, jnp.bfloat16),
        ],
        in_specs=anywhere(count) + vmem(9),
        out_specs=vmem(count + 2),
        scratch_shapes=[pltpu.VMEM(lead + piece, jnp.bfloat16) for lead in leads for piece in pieces]
        + [
            pltpu.VMEM((stages,) + small.shape, jnp.float32),
            pltpu.SemaphoreType.DMA((count, slots)),
            pltpu.SemaphoreType.DMA((count, slots)),
            pltpu.SemaphoreType.DMA((count, 2)),
            pltpu.SemaphoreType.DMA((stages,)),
            pltpu.SemaphoreType.DMA((stages,)),
            pltpu.VMEM(state, jnp.float32),
            pltpu.VMEM((seqs - 1,) + state, jnp.float32),
            pltpu.VMEM(state, jnp.float32),
            pltpu.SemaphoreType.DMA((seqs - 1,)),
            pltpu.SemaphoreType.DMA((seqs - 1,)),
            pltpu.VMEM((width // LANES, length, LANES), jnp.float32),
            pltpu.VMEM((width // LANES, length, LANES), jnp.float32),
            pltpu.VMEM((width // LANES * EMA_STEP * 8, LANES), jnp.float32),
            pltpu.VMEM((length * 16, width), jnp.float32),
        ],
        compiler_params=pltpu.CompilerParams(collective_id=1, has_side_effects=True, vmem_limit_bytes=62 * 2**20),
        name="scatter_grads",
    )(
        *[g.reshape(sizes + piece) for g, piece in zip(grads, pieces)],
        small, feed, grad, keep, decay, gain, start, reach, power,
    )
    sums = [result.reshape(g.shape[0] // total, g.shape[1]) for result, g in zip(results[:count], grads)]
    return sums, *results[count:]


def passed_on(alive, forward):
    count = lax.axis_size("seq")
    place = lax.axis_index("seq")
    through = jnp.ones((alive.shape[0], 1, 1), jnp.float32)
    factors = []
    for away in range(1, count):
        exists = place >= away if forward else place + away < count
        factors.append(jnp.broadcast_to(jnp.where(exists, through, 0.0), (alive.shape[0], 16, LANES)))
        at = jnp.clip(place - away if forward else place + away, 0, count - 1)
        through = through * lax.dynamic_slice_in_dim(alive, at, 1, 1)[:, :, None]
    return jnp.stack(factors)


def on_device(
    layer_input,
    cotangent,
    doc_ids,
    resets,
    mix_weight,
    value_weight,
    head_weight,
    expand_weight,
    shrink_weight,
    chan_vectors,
    ema_logits,
    ema_beta_eta,
    z_affine,
):
    seq_count = lax.axis_size("seq")
    seq_place = lax.axis_index("seq")
    rows, places, width = layer_input.shape
    tokens = rows * places
    scale = Z ** (-0.5)
    halo = min(-(-(REACH - 1) // places), seq_count - 1)
    window = (halo + 1) * places

    inputs32 = layer_input.astype(jnp.float32)
    center = inputs32 - jnp.mean(inputs32, axis=-1, keepdims=True)
    unit = lax.rsqrt(jnp.mean(center * center, axis=-1, keepdims=True) + 1e-05)
    plain = center * unit
    normed = plain * chan_vectors[0]
    normed_low = low(normed)

    rate = jax.nn.sigmoid(ema_logits[0])
    damping = jax.nn.sigmoid(ema_logits[1])
    decay = (1.0 - rate * damping).T
    weight_in = rate * ema_beta_eta[0]
    weight_out = ema_beta_eta[1]
    gain = (weight_in * weight_out).T
    decay_all = decay
    reach = 1
    while reach < places:
        decay_all = decay_all * decay_all
        reach *= 2
    powers = [jnp.ones_like(decay)]
    while len(powers) < seq_count - 1:
        powers.append(powers[-1] * decay_all)
    power = jnp.stack(powers)
    keep_row = 1.0 - resets.astype(jnp.float32)
    keep_own = lax.dynamic_slice_in_dim(keep_row, seq_place * places, places, 1)
    keep = jnp.broadcast_to(keep_own[:, None, :, None], (rows, 1, places, LANES)).reshape(rows, places, LANES)
    alive = jnp.min(keep_row.reshape(rows, seq_count, places), axis=2)

    (value_full, mix_full, head_full), normed_window, start, ema_low = gather_weights(
        (value_weight, mix_weight, head_weight),
        normed_low,
        keep,
        decay,
        gain,
        passed_on(alive, True),
        power,
        halo,
    )
    normed_window = normed_window.reshape(rows * window, width)
    value_full, mix_full, head_full, expand_late, shrink_late = lax.optimization_barrier(
        (value_full, mix_full, head_full, expand_weight, shrink_weight)
    )
    expand_full = lax.all_gather(expand_late, BOTH, axis=0, tiled=True)
    shrink_full = lax.all_gather(shrink_late, BOTH, axis=0, tiled=True)

    premix = (ema_low.astype(jnp.float32) + chan_vectors[2] * normed).reshape(tokens, width)
    mixed_low = low(jax.nn.silu(premix))
    value_pre = product(normed_window, value_full)
    values_low = low(jax.nn.silu(value_pre)).reshape(rows, window, V)
    projected = product(mixed_low, mix_full)
    shared_pre = projected[:, :Z]
    reset_pre = projected[:, Z : Z + V]
    head_base = projected[:, Z + V : Z + V + width]
    update_pre = projected[:, Z + V + width :]
    shared = jax.nn.silu(shared_pre)
    queries_low = low(shared * z_affine[0] + z_affine[1]).reshape(rows, places, Z)
    keys_low = low(shared * z_affine[2]).reshape(rows, places, Z)
    key_window = jnp.concatenate([shift_seq(keys_low, by) for by in range(halo, 0, -1)] + [keys_low], axis=1)
    reset_gate = jax.nn.silu(reset_pre)
    update_gate = jax.nn.sigmoid(update_pre)

    padded_docs = jnp.pad(doc_ids, ((0, 0), (halo * places, 0)), constant_values=-1)
    key_docs = lax.dynamic_slice_in_dim(padded_docs, seq_place * places, window, 1)
    query_docs = key_docs[:, halo * places :]
    causal = jnp.arange(window)[None, :] <= jnp.arange(places)[:, None] + halo * places
    allowed = causal[None] & (query_docs[:, :, None] == key_docs[:, None, :])
    scores = jnp.einsum("rid,rjd->rij", queries_low, key_window, preferred_element_type=jnp.float32) * scale
    scores = jnp.where(allowed, scores, NEG_FILL)
    peak = jnp.max(scores, axis=-1, keepdims=True)
    expo = jnp.exp(scores - peak)
    total = jnp.sum(expo, axis=-1, keepdims=True)
    probs = expo / total
    probs_low = low(probs)
    attended = jnp.einsum(
        "rij,rjv->riv", probs_low, values_low, preferred_element_type=jnp.float32
    ).reshape(tokens, V)
    gated_low = low(reset_gate * attended)
    head_pre = head_base + product(gated_low, head_full)
    candidate = jax.nn.silu(head_pre)
    residual_in = inputs32.reshape(tokens, width)
    first = residual_in + update_gate * (candidate - residual_in)
    second, second_pull = jax.vjp(scaled_norm, first, chan_vectors[1])
    second_low = low(second)
    expand_pre = product(second_low, expand_full)
    hidden_low = low(jax.nn.silu(expand_pre))
    output = low(first + product(hidden_low, shrink_full)).reshape(rows, places, width)

    cot_low = cotangent.reshape(tokens, width)
    shrink_part = low(transposed(hidden_low, cot_low))
    d_expand = low(against(cot_low, shrink_full) * silu_slope(expand_pre))
    expand_part = low(transposed(second_low, d_expand))
    d_first_norm, d_gain_two = second_pull(against(d_expand, expand_full))
    d_first = cot_low.astype(jnp.float32) + d_first_norm
    d_update = d_first * (candidate - residual_in) * update_gate * (1.0 - update_gate)
    d_direct = d_first * (1.0 - update_gate)
    d_head = d_first * update_gate * silu_slope(head_pre)
    d_head_low = low(d_head)
    head_part = low(transposed(gated_low, d_head_low))
    d_gated = against(d_head_low, head_full)
    d_reset = d_gated * attended * silu_slope(reset_pre)
    d_attended = low(d_gated * reset_gate).reshape(rows, places, V)
    d_probs = jnp.einsum("riv,rjv->rij", d_attended, values_low, preferred_element_type=jnp.float32)
    balance = jnp.sum(probs * d_probs, axis=-1, keepdims=True)
    d_scores = low(probs * (d_probs - balance))
    d_queries = scale * jnp.einsum("rij,rjd->rid", d_scores, key_window, preferred_element_type=jnp.float32)
    key_term = scale * jnp.einsum("rij,rid->rjd", d_scores, queries_low, preferred_element_type=jnp.float32)
    d_keys = key_term[:, halo * places :]
    for by in range(1, halo + 1):
        begin = (halo - by) * places
        d_keys = d_keys + shift_seq(low(key_term[:, begin : begin + places]), -by).astype(jnp.float32)
    d_keys32 = low(d_keys).astype(jnp.float32).reshape(tokens, Z)
    d_values = jnp.einsum("rij,riv->rjv", probs_low, d_attended, preferred_element_type=jnp.float32)
    d_value_pre = low(d_values.reshape(rows * window, V) * silu_slope(value_pre))
    value_part = low(transposed(normed_window, d_value_pre))
    value_term = against(d_value_pre, value_full).reshape(rows, halo + 1, places, width)
    terms = low(value_term[:, :halo])
    d_normed_value = value_term[:, halo]
    for by in range(1, halo + 1):
        d_normed_value = d_normed_value + shift_seq(terms[:, halo - by], -by).astype(jnp.float32)
    d_query_flat = d_queries.reshape(tokens, Z)
    d_shared = d_query_flat * z_affine[0] + d_keys32 * z_affine[2]
    affine_part = jnp.stack(
        [
            jnp.sum(d_query_flat * shared, axis=0),
            jnp.sum(d_query_flat, axis=0),
            jnp.sum(d_keys32 * shared, axis=0),
        ]
    )
    d_projected = low(
        jnp.concatenate([d_shared * silu_slope(shared_pre), d_reset, d_head, d_update], axis=1)
    )
    mix_part = low(transposed(mixed_low, d_projected))
    d_premix = against(d_projected, mix_full) * silu_slope(premix)
    omega_part = jnp.sum(d_premix * normed.reshape(tokens, width), axis=0)
    d_premix = d_premix.reshape(rows, places, width)
    d_ema = low(d_premix)
    known = d_premix * chan_vectors[2] + d_normed_value
    d_gain_one = jnp.sum(known * plain, axis=(0, 1))
    small_part = jnp.concatenate(
        [
            jnp.zeros((32, width), jnp.float32),
            jnp.stack([d_gain_one, d_gain_two, omega_part]),
            jnp.pad(affine_part.reshape(1, 3 * Z), ((0, 4), (0, width - 3 * Z))),
        ],
        axis=0,
    )
    (shrink_grad, expand_grad, head_grad, value_grad, mix_grad), small_sum, d_feed = scatter_grads(
        (shrink_part, expand_part, head_part, value_part, mix_part),
        small_part,
        normed_low,
        d_ema,
        keep,
        decay,
        gain,
        start,
        passed_on(alive, False),
        power,
    )
    d_normed = known + d_feed.astype(jnp.float32)
    pulled = d_normed * chan_vectors[0]
    pulled = pulled - jnp.mean(pulled, axis=-1, keepdims=True) - plain * jnp.mean(pulled * plain, axis=-1, keepdims=True)
    x_grad = d_direct.reshape(rows, places, width) + pulled * unit
    gain_sum = small_sum[:16]
    decay_sum = small_sum[16:32]
    chan_grad = small_sum[32:35].at[0].add(jnp.sum(gain * gain_sum, axis=0) / chan_vectors[0])
    affine_grad = small_sum[35, : 3 * Z].reshape(3, Z)
    d_gain = gain_sum.T
    d_decay = (decay_sum * gain).T
    d_weight_in = d_gain * weight_out
    coef_grad = jnp.stack([d_weight_in * rate, d_gain * weight_in])
    d_rate = d_weight_in * ema_beta_eta[0] - d_decay * damping
    d_damping = -d_decay * rate
    logits_grad = jnp.stack([d_rate * rate * (1.0 - rate), d_damping * damping * (1.0 - damping)])
    return (
        output,
        x_grad,
        mix_grad,
        value_grad,
        head_grad,
        expand_grad,
        shrink_grad,
        chan_grad,
        logits_grad,
        coef_grad,
        affine_grad,
    )


def solution(mesh):
    placed = (
        P("dp", "seq", None),
        P("dp", "seq", None),
        P("dp", None),
        P("dp", None),
        P(BOTH, None),
        P(BOTH, None),
        P(BOTH, None),
        P(BOTH, None),
        P(BOTH, None),
        P(),
        P(),
        P(),
        P(),
    )
    return jax.shard_map(
        on_device,
        mesh=mesh,
        in_specs=placed,
        out_specs=(
            P("dp", "seq", None),
            P("dp", "seq", None),
            P(BOTH, None),
            P(BOTH, None),
            P(BOTH, None),
            P(BOTH, None),
            P(BOTH, None),
            P(),
            P(),
            P(),
            P(),
        ),
        check_vma=False,
    )
```

```python
import functools
import jax
import jax.numpy as jnp
from jax import lax
from jax.experimental import pallas as pl
from jax.experimental.pallas import tpu as pltpu
from jax.sharding import PartitionSpec as P

Z = 128
V = 2048
REACH = 1024
NEG_FILL = -1000000000.0
BOTH = ("dp", "seq")
MESH = pl.DeviceIdType.MESH
LANES = 128
EMA_STEP = 16
FORWARD_WIDTH = 512
BACKWARD_WIDTH = 256


def lanes_at(base, group):
    return pl.ds(pl.multiple_of(base + group * LANES, LANES), LANES)


def row_of(ref, step, group):
    return ref[group, pl.ds(step, 8, stride=0), :]


def widen(source, row, base, wide):
    for group in range(wide.shape[0]):
        wide[group] = source[row, :, lanes_at(base, group)].astype(jnp.float32)


def halves_of(ref, base, groups, row=None):
    spots = [(slice(h * 8, h * 8 + 8), lanes_at(base, g)) for g in range(groups) for h in range(2)]
    return [ref[spot] if row is None else ref[(row,) + spot] for spot in spots]


def put_halves(ref, base, values, row):
    for at, value in enumerate(values):
        g, h = divmod(at, 2)
        ref[row, h * 8 : h * 8 + 8, lanes_at(base, g)] = value


def add_halves(ref, first, base, values):
    for at, value in enumerate(values):
        g, h = divmod(at, 2)
        spot = (slice(first + h * 8, first + h * 8 + 8), lanes_at(base, g))
        ref[spot] = ref[spot] + value


def fold_rows(part, group):
    halves = []
    for half in range(EMA_STEP // 8):
        base = group * EMA_STEP * 8 + half * 64
        total = part[pl.ds(base, 8, stride=8), :]
        for sub in range(1, 8):
            total = total + part[pl.ds(base + sub, 8, stride=8), :]
        halves.append(total)
    return jnp.concatenate(halves, axis=0).astype(jnp.bfloat16)


def unit_of(index, width, chans):
    across = chans // width
    return lax.div(index, across), pl.multiple_of(lax.rem(index, across) * width, width)


def ema_last(reverse, row, base, feed, keep, decay, last, wide):
    length, groups = feed.shape[1], wide.shape[0]
    widen(feed, row, base, wide)
    decays = halves_of(decay, base, groups)

    def body(index, states):
        states = list(states)
        block = (length // EMA_STEP - 1 - index) if reverse else index
        first = pl.multiple_of(block * EMA_STEP, EMA_STEP)
        for offset in range(EMA_STEP):
            step = first + (EMA_STEP - 1 - offset if reverse else offset)
            kept = row_of(keep, step, row)
            for at in range(2 * groups):
                fed = row_of(wide, step, at // 2)
                if reverse:
                    states[at] = (kept * decays[at]) * (states[at] + fed)
                else:
                    states[at] = (kept * decays[at]) * states[at] + fed
        return tuple(states)

    zero = jnp.zeros((8, LANES), jnp.float32)
    put_halves(last, base, lax.fori_loop(0, length // EMA_STEP, body, (zero,) * (2 * groups)), row)


def ema_forward(row, base, feed, keep, decay, gain, start, out, wide, part):
    length, groups = feed.shape[1], wide.shape[0]
    widen(feed, row, base, wide)
    decays, gains = halves_of(decay, base, groups), halves_of(gain, base, groups)

    def body(index, states):
        states = list(states)
        first = pl.multiple_of(index * EMA_STEP, EMA_STEP)
        for offset in range(EMA_STEP):
            kept = row_of(keep, first + offset, row)
            for g in range(groups):
                fed = row_of(wide, first + offset, g)
                both = []
                for at in (2 * g, 2 * g + 1):
                    states[at] = (kept * decays[at]) * states[at] + fed
                    both.append(gains[at] * states[at])
                spot = g * EMA_STEP * 8 + offset * 8
                part[spot : spot + 8, :] = both[0] + both[1]
        for g in range(groups):
            out[row, pl.ds(first, EMA_STEP), lanes_at(base, g)] = fold_rows(part, g)
        return tuple(states)

    lax.fori_loop(0, length // EMA_STEP, body, tuple(halves_of(start, base, groups, row)))


def ema_backward(row, base, feed, grad, keep, decay, gain, start, end, back, sums, wide, wide_grad, part, held):
    length, groups = feed.shape[1], wide.shape[0]
    widen(feed, row, base, wide)
    widen(grad, row, base, wide_grad)
    decays, gains = halves_of(decay, base, groups), halves_of(gain, base, groups)
    blocks = length // EMA_STEP

    def forward(index, states):
        states = list(states)
        first = pl.multiple_of(index * EMA_STEP, EMA_STEP)
        for offset in range(EMA_STEP):
            kept = row_of(keep, first + offset, row)
            for at in range(2 * groups):
                g, h = divmod(at, 2)
                held[pl.ds((first + offset) * 16 + h * 8, 8), g * LANES : (g + 1) * LANES] = kept * states[at]
                states[at] = (kept * decays[at]) * states[at] + row_of(wide, first + offset, g)
        return tuple(states)

    lax.fori_loop(0, blocks, forward, tuple(halves_of(start, base, groups, row)))

    def backward(index, carried):
        pulls, gain_sums, decay_sums = (list(c) for c in carried)
        first = pl.multiple_of((blocks - 1 - index) * EMA_STEP, EMA_STEP)
        for offset in reversed(range(EMA_STEP)):
            step = first + offset
            kept = row_of(keep, step, row)
            for g in range(groups):
                pulled, fed = row_of(wide_grad, step, g), row_of(wide, step, g)
                both = []
                for h in range(2):
                    at = 2 * g + h
                    local = pulls[at] + pulled
                    both.append(gains[at] * local)
                    gain_sums[at] = gain_sums[at] + local * fed
                    before = held[pl.ds(step * 16 + h * 8, 8), g * LANES : (g + 1) * LANES]
                    decay_sums[at] = decay_sums[at] + local * before
                    pulls[at] = (kept * decays[at]) * local
                spot = g * EMA_STEP * 8 + offset * 8
                part[spot : spot + 8, :] = both[0] + both[1]
        for g in range(groups):
            back[row, pl.ds(first, EMA_STEP), lanes_at(base, g)] = fold_rows(part, g)
        return (tuple(pulls), tuple(gain_sums), tuple(decay_sums))

    zeros = (jnp.zeros((8, LANES), jnp.float32),) * (2 * groups)
    _, gain_sums, decay_sums = lax.fori_loop(
        0, blocks, backward, (tuple(halves_of(end, base, groups, row)), zeros, zeros)
    )
    add_halves(sums, 0, base, gain_sums)
    add_halves(sums, 16, base, decay_sums)


def layer_norm(values):
    center = values - jnp.mean(values, axis=-1, keepdims=True)
    spread = jnp.mean(center * center, axis=-1, keepdims=True)
    return center * lax.rsqrt(spread + 1e-05)


def scaled_norm(values, gain):
    return layer_norm(values) * gain


def silu_slope(values):
    squash = jax.nn.sigmoid(values)
    return squash * (1.0 + values * (1.0 - squash))


def product(left, right):
    return jnp.dot(left, right, preferred_element_type=jnp.float32)


def against(left, right):
    return lax.dot_general(left, right, (((1,), (1,)), ((), ())), preferred_element_type=jnp.float32)


def transposed(left, right):
    return lax.dot_general(left, right, (((0,), (0,)), ((), ())), preferred_element_type=jnp.float32)


def low(values):
    return values.astype(jnp.bfloat16)


def shift_seq(values, by):
    count = lax.axis_size("seq")
    pairs = [(i, i + by) for i in range(count) if 0 <= i + by < count]
    return lax.ppermute(values, "seq", pairs)


def side_of(count):
    side = 1
    while side * side < count:
        side *= 2
    return side


def shape_of():
    depth = lax.axis_size("dp") // 2
    seqs = lax.axis_size("seq")
    down = side_of(seqs)
    return depth, 2, down, seqs // down


def place_of():
    depth, cores, down, across = shape_of()
    dp, seq = lax.axis_index("dp"), lax.axis_index("seq")
    return lax.div(dp, cores), lax.rem(dp, cores), lax.div(seq, across), lax.rem(seq, across)


def peer_of(sizes, spot, axis, by):
    spot = list(spot)
    spot[axis] = lax.rem(spot[axis] + by, sizes[axis])
    return {"dp": spot[0] * sizes[1] + spot[1], "seq": spot[2] * sizes[3] + spot[3]}


def along(count, by):
    return {"dp": lax.axis_index("dp"), "seq": lax.rem(lax.axis_index("seq") + by, count)}


def greet(sizes, spot):
    barrier = pltpu.get_barrier_semaphore()
    seqs = sizes[2] * sizes[3]
    peers = [peer_of(sizes, spot, axis, by) for axis in (0, 1) for by in range(1, sizes[axis])]
    peers += [along(seqs, by) for by in range(1, seqs)]
    for peer in peers:
        pl.semaphore_signal(barrier, inc=1, device_id=peer, device_id_type=MESH)
    pl.semaphore_wait(barrier, len(peers))


def piece_shape(rows, columns):
    return (rows, columns) if rows % 16 == 0 else (rows * columns // LANES, LANES)


def share(total, parts, at):
    return total * at // parts, total * (at + 1) // parts


def spread_edge(seqs, edge, arrived, send, recv, forward):
    return [
        pltpu.make_async_remote_copy(
            src_ref=edge,
            dst_ref=arrived.at[by - 1],
            send_sem=send.at[by - 1],
            recv_sem=recv.at[by - 1],
            device_id=along(seqs, by if forward else seqs - by),
            device_id_type=MESH,
        )
        for by in range(1, seqs)
    ]


def join_edges(arrived, reach, power, entry):
    rows, _, chans = entry.shape

    def body(row, carry):
        for group in range(chans // LANES):
            spot = slice(group * LANES, (group + 1) * LANES)
            total = None
            for at in range(arrived.shape[0]):
                term = reach[at, row] * power[at, :, spot] * arrived[at, row, :, spot]
                total = term if total is None else total + term
            entry[row, :, spot] = total
        return carry

    lax.fori_loop(0, rows, body, 0)


class Halo:
    def __init__(self, count, seqs, feed, window, zero, send, recv, local, hand_send):
        place = lax.axis_index("seq")
        relay = seqs == 4 and count == 2
        self.items = []

        def copy(source, by, towards, sent):
            return pltpu.make_async_remote_copy(
                src_ref=source,
                dst_ref=window.at[:, count - by],
                send_sem=sent,
                recv_sem=recv.at[by - 1],
                device_id=along(seqs, towards),
                device_id_type=MESH,
            )

        for by in range(1, count + 1):
            gives = place + by < seqs
            if relay and by == 1:
                gives = jnp.logical_and(gives, place != 1)
            blank = pltpu.make_async_copy(zero, window.at[:, count - by], local.at[by - 1])
            self.items.append((gives, place >= by, copy(feed, by, by, send.at[by - 1]), blank))
        self.hands = (place == 3, copy(window.at[:, 0], 1, 3, hand_send.at[0])) if relay else None

    def start(self):
        for gives, takes, remote, blank in self.items:
            pl.when(gives)(remote.start)
            pl.when(jnp.logical_not(takes))(blank.start)

    def hand_on(self):
        if self.hands:
            at_hand, hand = self.hands

            @pl.when(at_hand)
            def _():
                self.items[1][2].wait_recv()
                hand.start()

    def wait(self):
        for at, (gives, takes, remote, blank) in enumerate(self.items):
            waits = takes
            if self.hands and at == 1:
                waits = jnp.logical_and(takes, jnp.logical_not(self.hands[0]))
            pl.when(waits)(remote.wait_recv)
            pl.when(jnp.logical_not(takes))(blank.wait)
            pl.when(gives)(remote.wait_send)
        if self.hands:
            pl.when(self.hands[0])(self.hands[1].wait_send)


def gather_kernel(sizes, count, halo, *refs):
    shards, (feed, keep, decay, gain, reach, power) = refs[:count], refs[count : count + 6]
    wholes, (window, entry, out) = refs[count + 6 : 2 * count + 6], refs[2 * count + 6 : 2 * count + 9]
    (
        send_sem, recv_sem, local_sem, edge, arrived, edge_send, edge_recv,
        zero, halo_send, halo_recv, halo_local, hand_send, wide_feed, part,
    ) = refs[2 * count + 9 :]
    rows, length, chans = feed.shape
    width = wide_feed.shape[0] * LANES
    seqs = sizes[2] * sizes[3]
    depth, cores, down, across = sizes
    spot = place_of()
    z, c, a, b = spot
    half = depth // 2
    greet(sizes, spot)
    slots = {}

    def copy(w, kind, source, target, axis, by):
        slot = slots.setdefault(kind, len(slots))
        return pltpu.make_async_remote_copy(
            src_ref=source,
            dst_ref=target,
            send_sem=send_sem.at[w, slot],
            recv_sem=recv_sem.at[w, slot],
            device_id=peer_of(sizes, spot, axis, by),
            device_id_type=MESH,
        )

    def block(w, a_by=0, b_by=0, part=None):
        at = pl.ds(0, depth) if part is None else part
        return wholes[w].at[at, c, lax.rem(a - a_by + down, down), lax.rem(b - b_by + across, across)]

    front, back = pl.ds(0, half), pl.ds(half, depth - half)
    local, line, wide, tall, cross, twin = [], [], [], [], [], []
    for w in range(count):
        own = wholes[w].at[z, c, a, b]
        local.append(pltpu.make_async_copy(shards[w], own, local_sem.at[w]))
        line.append([copy(w, ("z", k), shards[w], own, 0, k) for k in range(1, depth)])
        wide.append([copy(w, ("x", k), block(w), block(w), 3, k) for k in range(1, across)])
        tall.append([copy(w, ("y", l), block(w), block(w), 2, l) for l in range(1, down)])
        pairs = [(k, l) for k in range(1, across) for l in range(1, down)]
        cross.append(
            {
                (k, l): (
                    copy(w, ("f", k, l), block(w, 0, k, front), block(w, 0, k, front), 2, l),
                    copy(w, ("g", k, l), block(w, l, 0, back), block(w, l, 0, back), 3, k),
                )
                for k, l in pairs
            }
        )
        twin.append(
            {
                (l, k): copy(w, ("c", l, k), block(w, l, k), block(w, l, k), 1, 1)
                for l in range(down)
                for k in range(across)
            }
        )
    zero[...] = jnp.zeros_like(zero)
    around = Halo(halo, seqs, feed, window, zero, halo_send, halo_recv, halo_local, hand_send)
    own = pltpu.make_async_copy(feed, window.at[:, halo], local_sem.at[count])
    edges = spread_edge(seqs, edge, arrived, edge_send, edge_recv, True)
    for w in range(count):
        local[w].start()
    for item in line[0]:
        item.start()
    own.start()
    around.start()
    for w in range(1, min(2, count)):
        for item in line[w]:
            item.start()
    units = rows * (chans // width)

    def last_unit(index, carry):
        row, base = unit_of(index, width, chans)
        ema_last(False, row, base, feed, keep, decay, edge, wide_feed)
        return carry

    def forward_unit(index, carry):
        row, base = unit_of(index, width, chans)
        ema_forward(row, base, feed, keep, decay, gain, entry, out, wide_feed, part)
        return carry

    lax.fori_loop(0, units, last_unit, 0)
    for item in edges:
        item.start()
    for step in range(count + 2):
        if step < count:
            w = step
            local[w].wait()
            for item in line[w]:
                item.wait_recv()
            for item in wide[w] + tall[w]:
                item.start()
            twin[w][0, 0].start()
            if w + 2 < count:
                for item in line[w + 2]:
                    item.start()
        if 1 <= step <= count:
            w = step - 1
            for k in range(1, across):
                wide[w][k - 1].wait_recv()
                for l in range(1, down):
                    cross[w][k, l][0].start()
                twin[w][0, k].start()
            for l in range(1, down):
                tall[w][l - 1].wait_recv()
                for k in range(1, across):
                    cross[w][k, l][1].start()
                twin[w][l, 0].start()
        if step >= 2:
            w = step - 2
            for (k, l), both in cross[w].items():
                both[0].wait_recv()
                both[1].wait_recv()
                twin[w][l, k].start()
        if step == 0:
            for item in edges:
                item.wait()
            join_edges(arrived, reach, power, entry)
        if step == 1:
            around.hand_on()
        lax.fori_loop(*share(units, count + 2, step), forward_unit, 0)
    for w in range(count):
        for item in twin[w].values():
            item.wait()
        for item in line[w] + wide[w] + tall[w]:
            item.wait_send()
        for both in cross[w].values():
            both[0].wait_send()
            both[1].wait_send()
    own.wait()
    around.wait()


def vmem(count):
    return [pl.BlockSpec(memory_space=pltpu.VMEM)] * count


def anywhere(count):
    return [pl.BlockSpec(memory_space=pl.ANY)] * count


def gather_weights(shards, feed, keep, decay, gain, reach, power, halo):
    sizes = shape_of()
    depth, cores, down, across = sizes
    seqs = down * across
    count = len(shards)
    pieces = [piece_shape(*shard.shape) for shard in shards]
    slots = (depth - 1) + (across - 1) + (down - 1) + 2 * (across - 1) * (down - 1) + across * down
    rows, length, chans = feed.shape
    state = (rows, 16, chans)
    width = min(FORWARD_WIDTH, chans)
    results = pl.pallas_call(
        functools.partial(gather_kernel, sizes, count, halo),
        out_shape=[jax.ShapeDtypeStruct(sizes + piece, jnp.bfloat16) for piece in pieces]
        + [
            jax.ShapeDtypeStruct((rows, halo + 1, length, chans), jnp.bfloat16),
            jax.ShapeDtypeStruct(state, jnp.float32),
            jax.ShapeDtypeStruct(feed.shape, jnp.bfloat16),
        ],
        in_specs=anywhere(count) + vmem(6),
        out_specs=anywhere(count + 1) + vmem(2),
        scratch_shapes=[
            pltpu.SemaphoreType.DMA((count, slots)),
            pltpu.SemaphoreType.DMA((count, slots)),
            pltpu.SemaphoreType.DMA((count + 1,)),
            pltpu.VMEM(state, jnp.float32),
            pltpu.VMEM((seqs - 1,) + state, jnp.float32),
            pltpu.SemaphoreType.DMA((seqs - 1,)),
            pltpu.SemaphoreType.DMA((seqs - 1,)),
            pltpu.VMEM(feed.shape, jnp.bfloat16),
            pltpu.SemaphoreType.DMA((halo,)),
            pltpu.SemaphoreType.DMA((halo,)),
            pltpu.SemaphoreType.DMA((halo,)),
            pltpu.SemaphoreType.DMA((1,)),
            pltpu.VMEM((width // LANES, length, LANES), jnp.float32),
            pltpu.VMEM((width // LANES * EMA_STEP * 8, LANES), jnp.float32),
        ],
        compiler_params=pltpu.CompilerParams(collective_id=0, has_side_effects=True, vmem_limit_bytes=48 * 2**20),
        name="gather_weights",
    )(*[shard.reshape(piece) for shard, piece in zip(shards, pieces)], feed, keep, decay, gain, reach, power)
    total = depth * cores * down * across
    wholes = [whole.reshape(total * shard.shape[0], shard.shape[1]) for whole, shard in zip(results, shards)]
    return wholes, *results[count:]


def add_rows(target, total, others):
    rows = total.shape[0]
    chunk = 16 if rows % 16 == 0 else rows

    def body(index, carry):
        at = pl.ds(pl.multiple_of(index * chunk, chunk), chunk)
        result = total[at, :].astype(jnp.float32)
        for other in others:
            result = result + other[at, :].astype(jnp.float32)
        target[at, :] = result.astype(target.dtype)
        return carry

    lax.fori_loop(0, rows // chunk, body, 0)


def scatter_kernel(sizes, count, *refs):
    grads, small = refs[:count], refs[count]
    feed, grad, keep, decay, gain, start, reach, power = refs[count + 1 : count + 9]
    refs = refs[count + 9 :]
    outs, (small_out, back_out) = refs[:count], refs[count : count + 2]
    rest = refs[count + 2 :]
    rest, (
        edge, arrived, end, edge_send, edge_recv, wide, wide_grad, part, kept_states,
    ) = rest[:-9], rest[-9:]
    rows, length, chans = feed.shape
    width = wide.shape[0] * LANES
    seqs = sizes[2] * sizes[3]
    names = ("arrive", "own", "first_a", "first_b", "second_a", "second_b", "third")
    held = {name: rest[at * count : (at + 1) * count] for at, name in enumerate(names)}
    small_parts, send_sem, recv_sem, own_sem, small_send, small_recv = rest[len(names) * count :]
    depth, cores, down, across = sizes
    spot = place_of()
    z, c, a, b = spot
    half = depth // 2
    front, back = pl.ds(0, half), pl.ds(half, depth - half)
    greet(sizes, spot)
    slots = {}

    def copy(w, kind, source, target, axis, by):
        slot = slots.setdefault(kind, len(slots))
        return pltpu.make_async_remote_copy(
            src_ref=source,
            dst_ref=target,
            send_sem=send_sem.at[w, slot],
            recv_sem=recv_sem.at[w, slot],
            device_id=peer_of(sizes, spot, axis, by),
            device_id_type=MESH,
        )

    def at_a(by):
        return lax.rem(a + by, down)

    def at_b(by):
        return lax.rem(b + by, across)

    twin, first, second, third = [], [], [], []
    for w in range(count):
        arrive = held["arrive"][w]
        twin.append(copy(w, "c", grads[w].at[:, 1 - c], arrive, 1, 1))
        first.append(
            [
                copy(w, ("a1", k), arrive.at[front, :, at_b(k)], held["first_a"][w].at[k - 1], 3, k)
                for k in range(1, across)
            ]
            + [
                copy(w, ("b1", l), arrive.at[back, at_a(l)], held["first_b"][w].at[l - 1], 2, l)
                for l in range(1, down)
            ]
        )
        second.append(
            [
                copy(w, ("a2", l), arrive.at[front, at_a(l), b], held["second_a"][w].at[l - 1], 2, l)
                for l in range(1, down)
            ]
            + [
                copy(w, ("b2", k), arrive.at[back, a, at_b(k)], held["second_b"][w].at[k - 1], 3, k)
                for k in range(1, across)
            ]
        )
        third.append(
            [
                copy(w, ("z", k), arrive.at[lax.rem(z + k, depth), a, b], held["third"][w].at[k - 1], 0, k)
                for k in range(1, depth)
            ]
        )

    stages = [(axis, 1 << bit) for axis in (1, 2, 3, 0) for bit in range(sizes[axis].bit_length() - 1)]

    def small_copy(at):
        axis, bit = stages[at]
        mine = spot[axis]
        towards = jnp.where(lax.rem(mine // bit, 2) == 0, bit, sizes[axis] - bit)
        return pltpu.make_async_remote_copy(
            src_ref=small_out,
            dst_ref=small_parts.at[at],
            send_sem=small_send.at[at],
            recv_sem=small_recv.at[at],
            device_id=peer_of(sizes, spot, axis, towards),
            device_id_type=MESH,
        )

    def own_load(w, at):
        return pltpu.make_async_copy(grads[w].at[at, c], held["own"][w].at[lax.rem(at, 2)], own_sem.at[w, lax.rem(at, 2)])

    def add_own(w):
        own_load(w, 0).start()

        def body(at, carry):
            @pl.when(at + 1 < depth)
            def _():
                own_load(w, at + 1).start()

            own_load(w, at).wait()
            for down_at in range(down):
                for across_at in range(across):
                    spot_ref = held["arrive"][w].at[at, down_at, across_at]
                    add_rows(spot_ref, spot_ref, [held["own"][w].at[lax.rem(at, 2), down_at, across_at]])
            return carry

        lax.fori_loop(0, depth, body, 0)

    small_out[...] = small[...]
    edges = spread_edge(seqs, edge, arrived, edge_send, edge_recv, False)
    units = rows * (chans // width)

    def last_unit(index, carry):
        row, base = unit_of(index, width, chans)
        ema_last(True, row, base, grad, keep, decay, edge, wide)
        return carry

    def backward_unit(index, carry):
        row, base = unit_of(index, width, chans)
        ema_backward(
            row, base, feed, grad, keep, decay, gain, start, end, back_out, small_out, wide, wide_grad, part, kept_states
        )
        return carry

    for w in range(min(2, count)):
        twin[w].start()
    lax.fori_loop(0, units, last_unit, 0)
    for item in edges:
        item.start()
    busy = count - 1
    for step in range(max(count + 3, busy + len(stages))):
        if step < count:
            w = step
            twin[w].wait_recv()
            if w + 2 < count:
                twin[w + 2].start()
            add_own(w)
            for item in first[w]:
                item.start()
        if 1 <= step <= count:
            w = step - 1
            arrive = held["arrive"][w]
            for item in first[w]:
                item.wait_recv()
            for at in range(half):
                for l in range(down):
                    spot_ref = arrive.at[at, l, b]
                    add_rows(spot_ref, spot_ref, [held["first_a"][w].at[k, at, l] for k in range(across - 1)])
            for at in range(half, depth):
                for k in range(across):
                    spot_ref = arrive.at[at, a, k]
                    add_rows(spot_ref, spot_ref, [held["first_b"][w].at[l, at - half, k] for l in range(down - 1)])
            for item in second[w]:
                item.start()
        if 2 <= step <= count + 1:
            w = step - 2
            arrive = held["arrive"][w]
            for item in second[w]:
                item.wait_recv()
            for at in range(half):
                spot_ref = arrive.at[at, a, b]
                add_rows(spot_ref, spot_ref, [held["second_a"][w].at[l, at] for l in range(down - 1)])
            for at in range(half, depth):
                spot_ref = arrive.at[at, a, b]
                add_rows(spot_ref, spot_ref, [held["second_b"][w].at[k, at - half] for k in range(across - 1)])
            for item in third[w]:
                item.start()
        if 3 <= step <= count + 2:
            w = step - 3
            for item in third[w]:
                item.wait_recv()
            add_rows(outs[w], held["arrive"][w].at[z, a, b], [held["third"][w].at[k] for k in range(depth - 1)])
        if step == 0:
            for item in edges:
                item.wait()
            join_edges(arrived, reach, power, end)
        if step < busy:
            lax.fori_loop(*share(units, busy, step), backward_unit, 0)
        stage = step - busy
        if stage == -1:
            small_copy(0).start()
        if 0 <= stage < len(stages):
            small_copy(stage).wait()
            small_out[...] = small_out[...] + small_parts[stage]
            if stage + 1 < len(stages):
                small_copy(stage + 1).start()
    for w in range(count):
        for item in [twin[w]] + first[w] + second[w] + third[w]:
            item.wait_send()


def scatter_grads(grads, small, feed, grad, keep, decay, gain, start, reach, power):
    sizes = shape_of()
    depth, cores, down, across = sizes
    total = depth * cores * down * across
    count = len(grads)
    half = depth // 2
    pieces = [piece_shape(g.shape[0] // total, g.shape[1]) for g in grads]
    leads = (
        (depth, down, across),
        (2, down, across),
        (across - 1, half, down),
        (down - 1, depth - half, across),
        (down - 1, half),
        (across - 1, depth - half),
        (depth - 1,),
    )
    slots = 1 + 2 * (across - 1 + down - 1) + depth - 1
    stages = sum(size.bit_length() - 1 for size in sizes)
    rows, length, chans = feed.shape
    state = (rows, 16, chans)
    width = min(BACKWARD_WIDTH, chans)
    seqs = down * across
    results = pl.pallas_call(
        functools.partial(scatter_kernel, sizes, count),
        out_shape=[jax.ShapeDtypeStruct(piece, jnp.float32) for piece in pieces]
        + [
            jax.ShapeDtypeStruct(small.shape, jnp.float32),
            jax.ShapeDtypeStruct(feed.shape, jnp.bfloat16),
        ],
        in_specs=anywhere(count) + vmem(9),
        out_specs=vmem(count + 2),
        scratch_shapes=[pltpu.VMEM(lead + piece, jnp.bfloat16) for lead in leads for piece in pieces]
        + [
            pltpu.VMEM((stages,) + small.shape, jnp.float32),
            pltpu.SemaphoreType.DMA((count, slots)),
            pltpu.SemaphoreType.DMA((count, slots)),
            pltpu.SemaphoreType.DMA((count, 2)),
            pltpu.SemaphoreType.DMA((stages,)),
            pltpu.SemaphoreType.DMA((stages,)),
            pltpu.VMEM(state, jnp.float32),
            pltpu.VMEM((seqs - 1,) + state, jnp.float32),
            pltpu.VMEM(state, jnp.float32),
            pltpu.SemaphoreType.DMA((seqs - 1,)),
            pltpu.SemaphoreType.DMA((seqs - 1,)),
            pltpu.VMEM((width // LANES, length, LANES), jnp.float32),
            pltpu.VMEM((width // LANES, length, LANES), jnp.float32),
            pltpu.VMEM((width // LANES * EMA_STEP * 8, LANES), jnp.float32),
            pltpu.VMEM((length * 16, width), jnp.float32),
        ],
        compiler_params=pltpu.CompilerParams(collective_id=1, has_side_effects=True, vmem_limit_bytes=62 * 2**20),
        name="scatter_grads",
    )(
        *[g.reshape(sizes + piece) for g, piece in zip(grads, pieces)],
        small, feed, grad, keep, decay, gain, start, reach, power,
    )
    sums = [result.reshape(g.shape[0] // total, g.shape[1]) for result, g in zip(results[:count], grads)]
    return sums, *results[count:]


def passed_on(alive, forward):
    count = lax.axis_size("seq")
    place = lax.axis_index("seq")
    through = jnp.ones((alive.shape[0], 1, 1), jnp.float32)
    factors = []
    for away in range(1, count):
        exists = place >= away if forward else place + away < count
        factors.append(jnp.broadcast_to(jnp.where(exists, through, 0.0), (alive.shape[0], 16, LANES)))
        at = jnp.clip(place - away if forward else place + away, 0, count - 1)
        through = through * lax.dynamic_slice_in_dim(alive, at, 1, 1)[:, :, None]
    return jnp.stack(factors)


QUERY_BLOCK = 256
KEY_BLOCK = 512
VALUE_BLOCK = 1024


def attend_kernel(halo_span, query, key, value, key_docs, query_docs, out, probs):
    size, span = probs.shape
    first = pl.program_id(1) * size
    keys = pl.ds(pl.multiple_of(first, LANES), span)
    scores = against(query[0], key[0, keys, :]) * Z ** (-0.5)
    query_at = lax.broadcasted_iota(jnp.int32, (size, span), 0) + halo_span
    key_at = lax.broadcasted_iota(jnp.int32, (size, span), 1)
    allowed = (key_at <= query_at) & (key_docs[0, :, keys] == query_docs[0])
    scores = jnp.where(allowed, scores, NEG_FILL)
    expo = jnp.exp(scores - jnp.max(scores, axis=1, keepdims=True))
    probs[...] = low(expo / jnp.sum(expo, axis=1, keepdims=True))

    def body(at, carry):
        columns = pl.ds(pl.multiple_of(at * VALUE_BLOCK, VALUE_BLOCK), VALUE_BLOCK)
        out[0, :, columns] = product(probs[...], value[0, keys, columns])
        return carry

    lax.fori_loop(0, out.shape[2] // VALUE_BLOCK, body, 0)


def attend(query, key, value, docs_row, docs_column, halo):
    rows, places, _ = query.shape
    window, wide = value.shape[1:]
    size = min(QUERY_BLOCK, places)
    span = halo * places + size
    return pl.pallas_call(
        functools.partial(attend_kernel, halo * places),
        out_shape=jax.ShapeDtypeStruct((rows, places, wide), jnp.float32),
        grid=(rows, places // size),
        in_specs=[
            pl.BlockSpec((1, size, Z), lambda r, i: (r, i, 0)),
            pl.BlockSpec((1, window, Z), lambda r, i: (r, 0, 0)),
            pl.BlockSpec((1, window, wide), lambda r, i: (r, 0, 0)),
            pl.BlockSpec((1, 1, window), lambda r, i: (r, 0, 0)),
            pl.BlockSpec((1, size, 1), lambda r, i: (r, i, 0)),
        ],
        out_specs=pl.BlockSpec((1, size, wide), lambda r, i: (r, i, 0)),
        scratch_shapes=[pltpu.VMEM((size, span), jnp.bfloat16)],
        compiler_params=pltpu.CompilerParams(vmem_limit_bytes=40 * 2**20),
        cost_estimate=pl.CostEstimate(
            flops=2 * rows * places * span * (wide + Z),
            bytes_accessed=rows * (window * wide * 2 + places * wide * 4),
            transcendentals=rows * places * span,
        ),
        name="attend",
    )(query, key, value, docs_row, docs_column[:, halo * places :])


def attend_back_kernel(
    halo_span, query, key, value, slope, pulled, key_docs, query_docs, d_query, d_key, d_value, chances, pulls, balance
):
    window, places = chances.shape
    step = d_value.shape[1]
    chunk = pl.program_id(1)

    @pl.when(chunk == 0)
    def _():
        peak = jnp.full((1, places), NEG_FILL, jnp.float32)

        def score(at, peak):
            keys = pl.ds(pl.multiple_of(at * step, step), step)
            scores = against(key[0, keys, :], query[0]) * Z ** (-0.5)
            key_at = lax.broadcasted_iota(jnp.int32, (step, places), 0) + at * step
            query_at = lax.broadcasted_iota(jnp.int32, (step, places), 1) + halo_span
            allowed = (key_at <= query_at) & (key_docs[0, keys, :] == query_docs[0])
            scores = jnp.where(allowed, scores, NEG_FILL)
            chances[keys, :] = scores
            return jnp.maximum(peak, jnp.max(scores, axis=0, keepdims=True))

        peak = lax.fori_loop(0, window // step, score, peak)

        def weigh(at, total):
            keys = pl.ds(pl.multiple_of(at * step, step), step)
            expo = jnp.exp(chances[keys, :] - peak)
            chances[keys, :] = expo
            return total + jnp.sum(expo, axis=0, keepdims=True)

        total = lax.fori_loop(0, window // step, weigh, jnp.zeros((1, places), jnp.float32))

        def pull(at, held):
            keys = pl.ds(pl.multiple_of(at * step, step), step)
            probs = chances[keys, :] / total
            chances[keys, :] = probs
            local = against(value[0, keys, :], pulled[0])
            pulls[keys, :] = local
            return held + jnp.sum(probs * local, axis=0, keepdims=True)

        balance[...] = lax.fori_loop(0, window // step, pull, jnp.zeros((1, places), jnp.float32))
        d_query[...] = jnp.zeros_like(d_query)

    keys = pl.ds(pl.multiple_of(chunk * step, step), step)
    probs = chances[keys, :]
    d_scores = low(probs * (pulls[keys, :] - balance[...]))
    d_key[0] = product(d_scores, query[0]) * Z ** (-0.5)
    d_query[0] = d_query[0] + transposed(d_scores, key[0, keys, :]) * Z ** (-0.5)
    probs_low = low(probs)

    def body(at, carry):
        columns = pl.ds(pl.multiple_of(at * VALUE_BLOCK, VALUE_BLOCK), VALUE_BLOCK)
        local = product(probs_low, pulled[0, :, columns])
        d_value[0, :, columns] = low(local * slope[0, :, columns].astype(jnp.float32))
        return carry

    lax.fori_loop(0, d_value.shape[2] // VALUE_BLOCK, body, 0)


def attend_back(query, key, value, slope, pulled, docs_row, docs_column, halo):
    rows, places, _ = query.shape
    window, wide = value.shape[1:]
    step = min(KEY_BLOCK, places)
    return pl.pallas_call(
        functools.partial(attend_back_kernel, halo * places),
        out_shape=[
            jax.ShapeDtypeStruct((rows, places, Z), jnp.float32),
            jax.ShapeDtypeStruct((rows, window, Z), jnp.float32),
            jax.ShapeDtypeStruct((rows, window, wide), jnp.bfloat16),
        ],
        grid=(rows, window // step),
        in_specs=[
            pl.BlockSpec((1, places, Z), lambda r, i: (r, 0, 0)),
            pl.BlockSpec((1, window, Z), lambda r, i: (r, 0, 0)),
            pl.BlockSpec((1, window, wide), lambda r, i: (r, 0, 0)),
            pl.BlockSpec((1, step, wide), lambda r, i: (r, i, 0)),
            pl.BlockSpec((1, places, wide), lambda r, i: (r, 0, 0)),
            pl.BlockSpec((1, window, 1), lambda r, i: (r, 0, 0)),
            pl.BlockSpec((1, 1, places), lambda r, i: (r, 0, 0)),
        ],
        out_specs=[
            pl.BlockSpec((1, places, Z), lambda r, i: (r, 0, 0)),
            pl.BlockSpec((1, step, Z), lambda r, i: (r, i, 0)),
            pl.BlockSpec((1, step, wide), lambda r, i: (r, i, 0)),
        ],
        scratch_shapes=[
            pltpu.VMEM((window, places), jnp.float32),
            pltpu.VMEM((window, places), jnp.float32),
            pltpu.VMEM((1, places), jnp.float32),
        ],
        compiler_params=pltpu.CompilerParams(vmem_limit_bytes=48 * 2**20),
        cost_estimate=pl.CostEstimate(
            flops=4 * rows * places * window * (wide + Z),
            bytes_accessed=rows * (window * wide * 6 + places * wide * 2),
            transcendentals=rows * places * window,
        ),
        name="attend_back",
    )(query, key, value, slope, pulled, docs_column, docs_row[:, :, halo * places :])


def on_device(
    layer_input,
    cotangent,
    doc_ids,
    resets,
    mix_weight,
    value_weight,
    head_weight,
    expand_weight,
    shrink_weight,
    chan_vectors,
    ema_logits,
    ema_beta_eta,
    z_affine,
):
    seq_count = lax.axis_size("seq")
    seq_place = lax.axis_index("seq")
    rows, places, width = layer_input.shape
    tokens = rows * places
    halo = min(-(-(REACH - 1) // places), seq_count - 1)
    window = (halo + 1) * places

    inputs32 = layer_input.astype(jnp.float32)
    center = inputs32 - jnp.mean(inputs32, axis=-1, keepdims=True)
    unit = lax.rsqrt(jnp.mean(center * center, axis=-1, keepdims=True) + 1e-05)
    plain = center * unit
    normed = plain * chan_vectors[0]
    normed_low = low(normed)

    rate = jax.nn.sigmoid(ema_logits[0])
    damping = jax.nn.sigmoid(ema_logits[1])
    decay = (1.0 - rate * damping).T
    weight_in = rate * ema_beta_eta[0]
    weight_out = ema_beta_eta[1]
    gain = (weight_in * weight_out).T
    decay_all = decay
    reach = 1
    while reach < places:
        decay_all = decay_all * decay_all
        reach *= 2
    powers = [jnp.ones_like(decay)]
    while len(powers) < seq_count - 1:
        powers.append(powers[-1] * decay_all)
    power = jnp.stack(powers)
    keep_row = 1.0 - resets.astype(jnp.float32)
    keep_own = lax.dynamic_slice_in_dim(keep_row, seq_place * places, places, 1)
    keep = jnp.broadcast_to(keep_own[:, None, :, None], (rows, 1, places, LANES)).reshape(rows, places, LANES)
    alive = jnp.min(keep_row.reshape(rows, seq_count, places), axis=2)

    (value_full, mix_full, head_full, expand_full), normed_window, start, ema_low = gather_weights(
        (value_weight, mix_weight, head_weight, expand_weight),
        normed_low,
        keep,
        decay,
        gain,
        passed_on(alive, True),
        power,
        halo,
    )
    normed_window = normed_window.reshape(rows * window, width)
    value_full, mix_full, head_full, expand_full, shrink_late = lax.optimization_barrier(
        (value_full, mix_full, head_full, expand_full, shrink_weight)
    )
    shrink_full = lax.all_gather(shrink_late, BOTH, axis=0, tiled=True)

    premix = (ema_low.astype(jnp.float32) + chan_vectors[2] * normed).reshape(tokens, width)
    mixed_low = low(jax.nn.silu(premix))
    value_pre = product(normed_window, value_full)
    values_low = low(jax.nn.silu(value_pre)).reshape(rows, window, V)
    value_slope = low(silu_slope(value_pre)).reshape(rows, window, V)
    projected = product(mixed_low, mix_full)
    shared_pre = projected[:, :Z]
    reset_pre = projected[:, Z : Z + V]
    head_base = projected[:, Z + V : Z + V + width]
    update_pre = projected[:, Z + V + width :]
    shared = jax.nn.silu(shared_pre)
    queries_low = low(shared * z_affine[0] + z_affine[1]).reshape(rows, places, Z)
    keys_low = low(shared * z_affine[2]).reshape(rows, places, Z)
    key_window = jnp.concatenate([shift_seq(keys_low, by) for by in range(halo, 0, -1)] + [keys_low], axis=1)
    reset_gate = jax.nn.silu(reset_pre)
    update_gate = jax.nn.sigmoid(update_pre)

    padded_docs = jnp.pad(doc_ids, ((0, 0), (halo * places, 0)), constant_values=-1)
    key_docs = lax.dynamic_slice_in_dim(padded_docs, seq_place * places, window, 1)
    docs_row, docs_column = key_docs[:, None, :], key_docs[:, :, None]
    attended = attend(queries_low, key_window, values_low, docs_row, docs_column, halo).reshape(tokens, V)
    gated_low = low(reset_gate * attended)
    head_pre = head_base + product(gated_low, head_full)
    candidate = jax.nn.silu(head_pre)
    residual_in = inputs32.reshape(tokens, width)
    first = residual_in + update_gate * (candidate - residual_in)
    second, second_pull = jax.vjp(scaled_norm, first, chan_vectors[1])
    second_low = low(second)
    expand_pre = product(second_low, expand_full)
    expand_slope = silu_slope(expand_pre)
    hidden_low, expand_slope = lax.optimization_barrier((low(jax.nn.silu(expand_pre)), expand_slope))
    output = low(first + product(hidden_low, shrink_full)).reshape(rows, places, width)

    cot_low = cotangent.reshape(tokens, width)
    shrink_part = low(transposed(hidden_low, cot_low))
    d_expand = low(against(cot_low, shrink_full) * expand_slope)
    expand_part = low(transposed(second_low, d_expand))
    d_first_norm, d_gain_two = second_pull(against(d_expand, expand_full))
    d_first = cot_low.astype(jnp.float32) + d_first_norm
    d_update = d_first * (candidate - residual_in) * update_gate * (1.0 - update_gate)
    d_direct = d_first * (1.0 - update_gate)
    d_head = d_first * update_gate * silu_slope(head_pre)
    d_head_low = low(d_head)
    head_part = low(transposed(gated_low, d_head_low))
    d_gated = against(d_head_low, head_full)
    d_reset = d_gated * attended * silu_slope(reset_pre)
    d_attended = low(d_gated * reset_gate).reshape(rows, places, V)
    d_queries, key_term, d_value_pre = attend_back(
        queries_low, key_window, values_low, value_slope, d_attended, docs_row, docs_column, halo
    )
    d_value_pre = d_value_pre.reshape(rows * window, V)
    d_keys = key_term[:, halo * places :]
    for by in range(1, halo + 1):
        begin = (halo - by) * places
        d_keys = d_keys + shift_seq(low(key_term[:, begin : begin + places]), -by).astype(jnp.float32)
    d_keys32 = low(d_keys).astype(jnp.float32).reshape(tokens, Z)
    value_part = low(transposed(normed_window, d_value_pre))
    value_term = against(d_value_pre, value_full).reshape(rows, halo + 1, places, width)
    terms = low(value_term[:, :halo])
    d_normed_value = value_term[:, halo]
    for by in range(1, halo + 1):
        d_normed_value = d_normed_value + shift_seq(terms[:, halo - by], -by).astype(jnp.float32)
    d_query_flat = d_queries.reshape(tokens, Z)
    d_shared = d_query_flat * z_affine[0] + d_keys32 * z_affine[2]
    affine_part = jnp.stack(
        [
            jnp.sum(d_query_flat * shared, axis=0),
            jnp.sum(d_query_flat, axis=0),
            jnp.sum(d_keys32 * shared, axis=0),
        ]
    )
    d_projected = low(
        jnp.concatenate([d_shared * silu_slope(shared_pre), d_reset, d_head, d_update], axis=1)
    )
    mix_part = low(transposed(mixed_low, d_projected))
    d_premix = against(d_projected, mix_full) * silu_slope(premix)
    omega_part = jnp.sum(d_premix * normed.reshape(tokens, width), axis=0)
    d_premix = d_premix.reshape(rows, places, width)
    d_ema = low(d_premix)
    known = d_premix * chan_vectors[2] + d_normed_value
    d_gain_one = jnp.sum(known * plain, axis=(0, 1))
    small_part = jnp.concatenate(
        [
            jnp.zeros((32, width), jnp.float32),
            jnp.stack([d_gain_one, d_gain_two, omega_part]),
            jnp.pad(affine_part.reshape(1, 3 * Z), ((0, 4), (0, width - 3 * Z))),
        ],
        axis=0,
    )
    (shrink_grad, expand_grad, head_grad, value_grad, mix_grad), small_sum, d_feed = scatter_grads(
        (shrink_part, expand_part, head_part, value_part, mix_part),
        small_part,
        normed_low,
        d_ema,
        keep,
        decay,
        gain,
        start,
        passed_on(alive, False),
        power,
    )
    d_normed = known + d_feed.astype(jnp.float32)
    pulled = d_normed * chan_vectors[0]
    pulled = pulled - jnp.mean(pulled, axis=-1, keepdims=True) - plain * jnp.mean(pulled * plain, axis=-1, keepdims=True)
    x_grad = d_direct.reshape(rows, places, width) + pulled * unit
    gain_sum = small_sum[:16]
    decay_sum = small_sum[16:32]
    chan_grad = small_sum[32:35].at[0].add(jnp.sum(gain * gain_sum, axis=0) / chan_vectors[0])
    affine_grad = small_sum[35, : 3 * Z].reshape(3, Z)
    d_gain = gain_sum.T
    d_decay = (decay_sum * gain).T
    d_weight_in = d_gain * weight_out
    coef_grad = jnp.stack([d_weight_in * rate, d_gain * weight_in])
    d_rate = d_weight_in * ema_beta_eta[0] - d_decay * damping
    d_damping = -d_decay * rate
    logits_grad = jnp.stack([d_rate * rate * (1.0 - rate), d_damping * damping * (1.0 - damping)])
    return (
        output,
        x_grad,
        mix_grad,
        value_grad,
        head_grad,
        expand_grad,
        shrink_grad,
        chan_grad,
        logits_grad,
        coef_grad,
        affine_grad,
    )


def solution(mesh):
    placed = (
        P("dp", "seq", None),
        P("dp", "seq", None),
        P("dp", None),
        P("dp", None),
        P(BOTH, None),
        P(BOTH, None),
        P(BOTH, None),
        P(BOTH, None),
        P(BOTH, None),
        P(),
        P(),
        P(),
        P(),
    )
    return jax.shard_map(
        on_device,
        mesh=mesh,
        in_specs=placed,
        out_specs=(
            P("dp", "seq", None),
            P("dp", "seq", None),
            P(BOTH, None),
            P(BOTH, None),
            P(BOTH, None),
            P(BOTH, None),
            P(BOTH, None),
            P(),
            P(),
            P(),
            P(),
        ),
        check_vma=False,
    )
```

```python
import functools
import jax
import jax.numpy as jnp
from jax import lax
from jax.experimental import pallas as pl
from jax.experimental.pallas import tpu as pltpu
from jax.sharding import PartitionSpec as P

Z = 128
V = 2048
REACH = 1024
NEG_FILL = -1000000000.0
BOTH = ("dp", "seq")
MESH = pl.DeviceIdType.MESH
LANES = 128
EMA_STEP = 16
FORWARD_WIDTH = 512
BACKWARD_WIDTH = 256
HOST_TILE = 512


def lanes_at(base, group):
    return pl.ds(pl.multiple_of(base + group * LANES, LANES), LANES)


def row_of(ref, step, group):
    return ref[group, pl.ds(step, 8, stride=0), :]


def widen(source, row, base, wide):
    for group in range(wide.shape[0]):
        wide[group] = source[row, :, lanes_at(base, group)].astype(jnp.float32)


def halves_of(ref, base, groups, row=None):
    spots = [(slice(h * 8, h * 8 + 8), lanes_at(base, g)) for g in range(groups) for h in range(2)]
    return [ref[spot] if row is None else ref[(row,) + spot] for spot in spots]


def put_halves(ref, base, values, row):
    for at, value in enumerate(values):
        g, h = divmod(at, 2)
        ref[row, h * 8 : h * 8 + 8, lanes_at(base, g)] = value


def add_halves(ref, first, base, values):
    for at, value in enumerate(values):
        g, h = divmod(at, 2)
        spot = (slice(first + h * 8, first + h * 8 + 8), lanes_at(base, g))
        ref[spot] = ref[spot] + value


def fold_rows(part, group):
    halves = []
    for half in range(EMA_STEP // 8):
        base = group * EMA_STEP * 8 + half * 64
        total = part[pl.ds(base, 8, stride=8), :]
        for sub in range(1, 8):
            total = total + part[pl.ds(base + sub, 8, stride=8), :]
        halves.append(total)
    return jnp.concatenate(halves, axis=0).astype(jnp.bfloat16)


def unit_of(index, width, chans):
    across = chans // width
    return lax.div(index, across), pl.multiple_of(lax.rem(index, across) * width, width)


def ema_last(reverse, row, base, feed, keep, decay, last, wide):
    length, groups = feed.shape[1], wide.shape[0]
    widen(feed, row, base, wide)
    decays = halves_of(decay, base, groups)

    def body(index, states):
        states = list(states)
        block = (length // EMA_STEP - 1 - index) if reverse else index
        first = pl.multiple_of(block * EMA_STEP, EMA_STEP)
        for offset in range(EMA_STEP):
            step = first + (EMA_STEP - 1 - offset if reverse else offset)
            kept = row_of(keep, step, row)
            for at in range(2 * groups):
                fed = row_of(wide, step, at // 2)
                if reverse:
                    states[at] = (kept * decays[at]) * (states[at] + fed)
                else:
                    states[at] = (kept * decays[at]) * states[at] + fed
        return tuple(states)

    zero = jnp.zeros((8, LANES), jnp.float32)
    put_halves(last, base, lax.fori_loop(0, length // EMA_STEP, body, (zero,) * (2 * groups)), row)


def ema_forward(row, base, feed, keep, decay, gain, start, out, wide, part):
    length, groups = feed.shape[1], wide.shape[0]
    widen(feed, row, base, wide)
    decays, gains = halves_of(decay, base, groups), halves_of(gain, base, groups)

    def body(index, states):
        states = list(states)
        first = pl.multiple_of(index * EMA_STEP, EMA_STEP)
        for offset in range(EMA_STEP):
            kept = row_of(keep, first + offset, row)
            for g in range(groups):
                fed = row_of(wide, first + offset, g)
                both = []
                for at in (2 * g, 2 * g + 1):
                    states[at] = (kept * decays[at]) * states[at] + fed
                    both.append(gains[at] * states[at])
                spot = g * EMA_STEP * 8 + offset * 8
                part[spot : spot + 8, :] = both[0] + both[1]
        for g in range(groups):
            out[row, pl.ds(first, EMA_STEP), lanes_at(base, g)] = fold_rows(part, g)
        return tuple(states)

    lax.fori_loop(0, length // EMA_STEP, body, tuple(halves_of(start, base, groups, row)))


def ema_backward(row, base, feed, grad, keep, decay, gain, start, end, back, sums, wide, wide_grad, part, held):
    length, groups = feed.shape[1], wide.shape[0]
    widen(feed, row, base, wide)
    widen(grad, row, base, wide_grad)
    decays, gains = halves_of(decay, base, groups), halves_of(gain, base, groups)
    blocks = length // EMA_STEP

    def forward(index, states):
        states = list(states)
        first = pl.multiple_of(index * EMA_STEP, EMA_STEP)
        for offset in range(EMA_STEP):
            kept = row_of(keep, first + offset, row)
            for at in range(2 * groups):
                g, h = divmod(at, 2)
                held[pl.ds((first + offset) * 16 + h * 8, 8), g * LANES : (g + 1) * LANES] = kept * states[at]
                states[at] = (kept * decays[at]) * states[at] + row_of(wide, first + offset, g)
        return tuple(states)

    lax.fori_loop(0, blocks, forward, tuple(halves_of(start, base, groups, row)))

    def backward(index, carried):
        pulls, gain_sums, decay_sums = (list(c) for c in carried)
        first = pl.multiple_of((blocks - 1 - index) * EMA_STEP, EMA_STEP)
        for offset in reversed(range(EMA_STEP)):
            step = first + offset
            kept = row_of(keep, step, row)
            for g in range(groups):
                pulled, fed = row_of(wide_grad, step, g), row_of(wide, step, g)
                both = []
                for h in range(2):
                    at = 2 * g + h
                    local = pulls[at] + pulled
                    both.append(gains[at] * local)
                    gain_sums[at] = gain_sums[at] + local * fed
                    before = held[pl.ds(step * 16 + h * 8, 8), g * LANES : (g + 1) * LANES]
                    decay_sums[at] = decay_sums[at] + local * before
                    pulls[at] = (kept * decays[at]) * local
                spot = g * EMA_STEP * 8 + offset * 8
                part[spot : spot + 8, :] = both[0] + both[1]
        for g in range(groups):
            back[row, pl.ds(first, EMA_STEP), lanes_at(base, g)] = fold_rows(part, g)
        return (tuple(pulls), tuple(gain_sums), tuple(decay_sums))

    zeros = (jnp.zeros((8, LANES), jnp.float32),) * (2 * groups)
    _, gain_sums, decay_sums = lax.fori_loop(
        0, blocks, backward, (tuple(halves_of(end, base, groups, row)), zeros, zeros)
    )
    add_halves(sums, 0, base, gain_sums)
    add_halves(sums, 16, base, decay_sums)


def layer_norm(values):
    center = values - jnp.mean(values, axis=-1, keepdims=True)
    spread = jnp.mean(center * center, axis=-1, keepdims=True)
    return center * lax.rsqrt(spread + 1e-05)


def scaled_norm(values, gain):
    return layer_norm(values) * gain


def silu_slope(values):
    squash = jax.nn.sigmoid(values)
    return squash * (1.0 + values * (1.0 - squash))


def product(left, right):
    return jnp.dot(left, right, preferred_element_type=jnp.float32)


def against(left, right):
    return lax.dot_general(left, right, (((1,), (1,)), ((), ())), preferred_element_type=jnp.float32)


def transposed(left, right):
    return lax.dot_general(left, right, (((0,), (0,)), ((), ())), preferred_element_type=jnp.float32)


def low(values):
    return values.astype(jnp.bfloat16)


def shift_seq(values, by):
    count = lax.axis_size("seq")
    pairs = [(i, i + by) for i in range(count) if 0 <= i + by < count]
    return lax.ppermute(values, "seq", pairs)


def side_of(count):
    side = 1
    while side * side < count:
        side *= 2
    return side


def shape_of():
    depth = lax.axis_size("dp") // 2
    seqs = lax.axis_size("seq")
    down = side_of(seqs)
    return depth, 2, down, seqs // down


def place_of():
    depth, cores, down, across = shape_of()
    dp, seq = lax.axis_index("dp"), lax.axis_index("seq")
    return lax.div(dp, cores), lax.rem(dp, cores), lax.div(seq, across), lax.rem(seq, across)


def peer_of(sizes, spot, axis, by):
    spot = list(spot)
    spot[axis] = lax.rem(spot[axis] + by, sizes[axis])
    return {"dp": spot[0] * sizes[1] + spot[1], "seq": spot[2] * sizes[3] + spot[3]}


def along(count, by):
    return {"dp": lax.axis_index("dp"), "seq": lax.rem(lax.axis_index("seq") + by, count)}


def greet(sizes, spot):
    barrier = pltpu.get_barrier_semaphore()
    seqs = sizes[2] * sizes[3]
    peers = [peer_of(sizes, spot, axis, by) for axis in (0, 1) for by in range(1, sizes[axis])]
    peers += [along(seqs, by) for by in range(1, seqs)]
    for peer in peers:
        pl.semaphore_signal(barrier, inc=1, device_id=peer, device_id_type=MESH)
    pl.semaphore_wait(barrier, len(peers))


def piece_shape(rows, columns):
    return (rows, columns) if rows % 16 == 0 else (rows * columns // LANES, LANES)


def share(total, parts, at):
    return total * at // parts, total * (at + 1) // parts


def spread_edge(seqs, edge, arrived, send, recv, forward):
    return [
        pltpu.make_async_remote_copy(
            src_ref=edge,
            dst_ref=arrived.at[by - 1],
            send_sem=send.at[by - 1],
            recv_sem=recv.at[by - 1],
            device_id=along(seqs, by if forward else seqs - by),
            device_id_type=MESH,
        )
        for by in range(1, seqs)
    ]


def join_edges(arrived, reach, power, entry):
    rows, _, chans = entry.shape

    def body(row, carry):
        for group in range(chans // LANES):
            spot = slice(group * LANES, (group + 1) * LANES)
            total = None
            for at in range(arrived.shape[0]):
                term = reach[at, row] * power[at, :, spot] * arrived[at, row, :, spot]
                total = term if total is None else total + term
            entry[row, :, spot] = total
        return carry

    lax.fori_loop(0, rows, body, 0)


class Halo:
    def __init__(self, count, seqs, feed, window, zero, send, recv, local, hand_send):
        place = lax.axis_index("seq")
        relay = seqs == 4 and count == 2
        self.items = []

        def copy(source, by, towards, sent):
            return pltpu.make_async_remote_copy(
                src_ref=source,
                dst_ref=window.at[:, count - by],
                send_sem=sent,
                recv_sem=recv.at[by - 1],
                device_id=along(seqs, towards),
                device_id_type=MESH,
            )

        for by in range(1, count + 1):
            gives = place + by < seqs
            if relay and by == 1:
                gives = jnp.logical_and(gives, place != 1)
            blank = pltpu.make_async_copy(zero, window.at[:, count - by], local.at[by - 1])
            self.items.append((gives, place >= by, copy(feed, by, by, send.at[by - 1]), blank))
        self.hands = (place == 3, copy(window.at[:, 0], 1, 3, hand_send.at[0])) if relay else None

    def start(self):
        for gives, takes, remote, blank in self.items:
            pl.when(gives)(remote.start)
            pl.when(jnp.logical_not(takes))(blank.start)

    def hand_on(self):
        if self.hands:
            at_hand, hand = self.hands

            @pl.when(at_hand)
            def _():
                self.items[1][2].wait_recv()
                hand.start()

    def wait(self):
        for at, (gives, takes, remote, blank) in enumerate(self.items):
            waits = takes
            if self.hands and at == 1:
                waits = jnp.logical_and(takes, jnp.logical_not(self.hands[0]))
            pl.when(waits)(remote.wait_recv)
            pl.when(jnp.logical_not(takes))(blank.wait)
            pl.when(gives)(remote.wait_send)
        if self.hands:
            pl.when(self.hands[0])(self.hands[1].wait_send)


def gather_kernel(sizes, count, halo, hosts, *refs):
    shards, (feed, keep, decay, gain, reach, power) = refs[:count], refs[count : count + 6]
    wholes, (window, entry, out) = refs[count + 6 : 2 * count + 6], refs[2 * count + 6 : 2 * count + 9]
    if hosts:
        values, slopes = refs[2 * count + 9 : 2 * count + 11]
        weight, block_in, value_tile, slope_tile, weight_sem, in_sem, out_sem = refs[-7:]
        refs = refs[: 2 * count + 9] + refs[2 * count + 11 : -7]
    (
        send_sem, recv_sem, local_sem, edge, arrived, edge_send, edge_recv,
        zero, halo_send, halo_recv, halo_local, hand_send, wide_feed, part,
    ) = refs[2 * count + 9 :]
    rows, length, chans = feed.shape
    width = wide_feed.shape[0] * LANES
    seqs = sizes[2] * sizes[3]
    depth, cores, down, across = sizes
    spot = place_of()
    z, c, a, b = spot
    half = depth // 2
    greet(sizes, spot)
    slots = {}

    def copy(w, kind, source, target, axis, by):
        slot = slots.setdefault(kind, len(slots))
        return pltpu.make_async_remote_copy(
            src_ref=source,
            dst_ref=target,
            send_sem=send_sem.at[w, slot],
            recv_sem=recv_sem.at[w, slot],
            device_id=peer_of(sizes, spot, axis, by),
            device_id_type=MESH,
        )

    def block(w, a_by=0, b_by=0, part=None):
        at = pl.ds(0, depth) if part is None else part
        return wholes[w].at[at, c, lax.rem(a - a_by + down, down), lax.rem(b - b_by + across, across)]

    front, back = pl.ds(0, half), pl.ds(half, depth - half)
    local, line, wide, tall, cross, twin = [], [], [], [], [], []
    for w in range(count):
        own = wholes[w].at[z, c, a, b]
        local.append(pltpu.make_async_copy(shards[w], own, local_sem.at[w]))
        line.append([copy(w, ("z", k), shards[w], own, 0, k) for k in range(1, depth)])
        wide.append([copy(w, ("x", k), block(w), block(w), 3, k) for k in range(1, across)])
        tall.append([copy(w, ("y", l), block(w), block(w), 2, l) for l in range(1, down)])
        pairs = [(k, l) for k in range(1, across) for l in range(1, down)]
        cross.append(
            {
                (k, l): (
                    copy(w, ("f", k, l), block(w, 0, k, front), block(w, 0, k, front), 2, l),
                    copy(w, ("g", k, l), block(w, l, 0, back), block(w, l, 0, back), 3, k),
                )
                for k, l in pairs
            }
        )
        twin.append(
            {
                (l, k): copy(w, ("c", l, k), block(w, l, k), block(w, l, k), 1, 1)
                for l in range(down)
                for k in range(across)
            }
        )
    zero[...] = jnp.zeros_like(zero)
    around = Halo(halo, seqs, feed, window, zero, halo_send, halo_recv, halo_local, hand_send)
    own = pltpu.make_async_copy(feed, window.at[:, halo], local_sem.at[count])
    edges = spread_edge(seqs, edge, arrived, edge_send, edge_recv, True)
    for w in range(count):
        local[w].start()
    for item in line[0]:
        item.start()
    own.start()
    around.start()
    for w in range(1, min(2, count)):
        for item in line[w]:
            item.start()
    units = rows * (chans // width)

    def last_unit(index, carry):
        row, base = unit_of(index, width, chans)
        ema_last(False, row, base, feed, keep, decay, edge, wide_feed)
        return carry

    def forward_unit(index, carry):
        row, base = unit_of(index, width, chans)
        ema_forward(row, base, feed, keep, decay, gain, entry, out, wide_feed, part)
        return carry

    def block_place(index):
        return lax.rem(index, rows), halo - lax.div(index, rows)

    def load_block(index):
        slot = lax.rem(index, 2)
        return pltpu.make_async_copy(window.at[block_place(index)], block_in.at[slot], in_sem.at[slot])

    def store_tiles(index):
        slot = lax.rem(index, 2)
        row, back_by = block_place(lax.div(index, tiles))
        columns = pl.ds(pl.multiple_of(lax.rem(index, tiles) * HOST_TILE, HOST_TILE), HOST_TILE)
        return [
            pltpu.make_async_copy(tile.at[slot], whole.at[row, back_by, :, columns], out_sem.at[at, slot])
            for at, (tile, whole) in enumerate(((value_tile, values), (slope_tile, slopes)))
        ]

    blocks = rows * (halo + 1)
    tiles = wholes[0].shape[-1] // HOST_TILE

    def value_unit(index, carry):
        block, slot = lax.div(index, tiles), lax.rem(index, 2)

        @pl.when(lax.rem(index, tiles) == 0)
        def _():
            load_block(block).wait()

            @pl.when(block + 1 < blocks)
            def _():
                load_block(block + 1).start()

        columns = pl.ds(pl.multiple_of(lax.rem(index, tiles) * HOST_TILE, HOST_TILE), HOST_TILE)
        part_weight = weight[:, :, :, :, :, columns].reshape(chans, HOST_TILE)
        before = product(block_in[lax.rem(block, 2)], part_weight)
        squash = jax.nn.sigmoid(before)

        @pl.when(index >= 2)
        def _():
            for item in store_tiles(index - 2):
                item.wait()

        value_tile[slot] = low(before * squash)
        slope_tile[slot] = low(squash * (1.0 + before * (1.0 - squash)))
        for item in store_tiles(index):
            item.start()
        return carry

    lax.fori_loop(0, units, last_unit, 0)
    for item in edges:
        item.start()
    for step in range(count + 2):
        if step < count:
            w = step
            local[w].wait()
            for item in line[w]:
                item.wait_recv()
            for item in wide[w] + tall[w]:
                item.start()
            twin[w][0, 0].start()
            if w + 2 < count:
                for item in line[w + 2]:
                    item.start()
        if 1 <= step <= count:
            w = step - 1
            for k in range(1, across):
                wide[w][k - 1].wait_recv()
                for l in range(1, down):
                    cross[w][k, l][0].start()
                twin[w][0, k].start()
            for l in range(1, down):
                tall[w][l - 1].wait_recv()
                for k in range(1, across):
                    cross[w][k, l][1].start()
                twin[w][l, 0].start()
        if step >= 2:
            w = step - 2
            for (k, l), both in cross[w].items():
                both[0].wait_recv()
                both[1].wait_recv()
                twin[w][l, k].start()
        if step == 0:
            for item in edges:
                item.wait()
            join_edges(arrived, reach, power, entry)
        if step == 1:
            around.hand_on()
        lax.fori_loop(*share(units, count + 2, step), forward_unit, 0)
        if hosts and step == 2:
            for item in twin[0].values():
                item.wait_recv()
            full = pltpu.make_async_copy(wholes[0], weight, weight_sem.at[0])
            full.start()
            own.wait()
            around.wait()
            load_block(0).start()
            full.wait()
        if hosts and step >= 2:
            lax.fori_loop(*share(blocks * tiles, count, step - 2), value_unit, 0)
    if hosts:
        for index in (blocks * tiles - 2, blocks * tiles - 1):
            for item in store_tiles(index):
                item.wait()
    for w in range(count):
        for item in twin[w].values():
            item.wait_send()
            if w or not hosts:
                item.wait_recv()
        for item in line[w] + wide[w] + tall[w]:
            item.wait_send()
        for both in cross[w].values():
            both[0].wait_send()
            both[1].wait_send()
    if not hosts:
        own.wait()
        around.wait()


def vmem(count):
    return [pl.BlockSpec(memory_space=pltpu.VMEM)] * count


def anywhere(count):
    return [pl.BlockSpec(memory_space=pl.ANY)] * count


def gather_weights(shards, feed, keep, decay, gain, reach, power, halo):
    sizes = shape_of()
    depth, cores, down, across = sizes
    seqs = down * across
    count = len(shards)
    pieces = [piece_shape(*shard.shape) for shard in shards]
    slots = (depth - 1) + (across - 1) + (down - 1) + 2 * (across - 1) * (down - 1) + across * down
    rows, length, chans = feed.shape
    state = (rows, 16, chans)
    width = min(FORWARD_WIDTH, chans)
    hosts = pieces[0] == shards[0].shape
    made, extra = [], []
    if hosts:
        wide = shards[0].shape[1]
        made = [jax.ShapeDtypeStruct((rows, halo + 1, length, wide), jnp.bfloat16)] * 2
        extra = [
            pltpu.VMEM(sizes + pieces[0], jnp.bfloat16),
            pltpu.VMEM((2, length, chans), jnp.bfloat16),
            pltpu.VMEM((2, length, HOST_TILE), jnp.bfloat16),
            pltpu.VMEM((2, length, HOST_TILE), jnp.bfloat16),
            pltpu.SemaphoreType.DMA((1,)),
            pltpu.SemaphoreType.DMA((2,)),
            pltpu.SemaphoreType.DMA((2, 2)),
        ]
    results = pl.pallas_call(
        functools.partial(gather_kernel, sizes, count, halo, hosts),
        out_shape=[jax.ShapeDtypeStruct(sizes + piece, jnp.bfloat16) for piece in pieces]
        + [
            jax.ShapeDtypeStruct((rows, halo + 1, length, chans), jnp.bfloat16),
            jax.ShapeDtypeStruct(state, jnp.float32),
            jax.ShapeDtypeStruct(feed.shape, jnp.bfloat16),
        ]
        + made,
        in_specs=anywhere(count) + vmem(6),
        out_specs=anywhere(count + 1) + vmem(2) + anywhere(len(made)),
        scratch_shapes=[
            pltpu.SemaphoreType.DMA((count, slots)),
            pltpu.SemaphoreType.DMA((count, slots)),
            pltpu.SemaphoreType.DMA((count + 1,)),
            pltpu.VMEM(state, jnp.float32),
            pltpu.VMEM((seqs - 1,) + state, jnp.float32),
            pltpu.SemaphoreType.DMA((seqs - 1,)),
            pltpu.SemaphoreType.DMA((seqs - 1,)),
            pltpu.VMEM(feed.shape, jnp.bfloat16),
            pltpu.SemaphoreType.DMA((halo,)),
            pltpu.SemaphoreType.DMA((halo,)),
            pltpu.SemaphoreType.DMA((halo,)),
            pltpu.SemaphoreType.DMA((1,)),
            pltpu.VMEM((width // LANES, length, LANES), jnp.float32),
            pltpu.VMEM((width // LANES * EMA_STEP * 8, LANES), jnp.float32),
            *extra,
        ],
        compiler_params=pltpu.CompilerParams(collective_id=0, has_side_effects=True, vmem_limit_bytes=48 * 2**20),
        name="gather_weights",
    )(*[shard.reshape(piece) for shard, piece in zip(shards, pieces)], feed, keep, decay, gain, reach, power)
    total = depth * cores * down * across
    wholes = [whole.reshape(total * shard.shape[0], shard.shape[1]) for whole, shard in zip(results, shards)]
    return wholes, *results[count:]


def add_rows(target, total, others):
    rows = total.shape[0]
    chunk = 16 if rows % 16 == 0 else rows

    def body(index, carry):
        at = pl.ds(pl.multiple_of(index * chunk, chunk), chunk)
        result = total[at, :].astype(jnp.float32)
        for other in others:
            result = result + other[at, :].astype(jnp.float32)
        target[at, :] = result.astype(target.dtype)
        return carry

    lax.fori_loop(0, rows // chunk, body, 0)


def scatter_kernel(sizes, count, *refs):
    grads, small = refs[:count], refs[count]
    feed, grad, keep, decay, gain, start, reach, power = refs[count + 1 : count + 9]
    refs = refs[count + 9 :]
    outs, (small_out, back_out) = refs[:count], refs[count : count + 2]
    rest = refs[count + 2 :]
    rest, (
        edge, arrived, end, edge_send, edge_recv, wide, wide_grad, part, kept_states,
    ) = rest[:-9], rest[-9:]
    rows, length, chans = feed.shape
    width = wide.shape[0] * LANES
    seqs = sizes[2] * sizes[3]
    names = ("arrive", "own", "first_a", "first_b", "second_a", "second_b", "third")
    held = {name: rest[at * count : (at + 1) * count] for at, name in enumerate(names)}
    small_parts, send_sem, recv_sem, own_sem, small_send, small_recv = rest[len(names) * count :]
    depth, cores, down, across = sizes
    spot = place_of()
    z, c, a, b = spot
    half = depth // 2
    front, back = pl.ds(0, half), pl.ds(half, depth - half)
    greet(sizes, spot)
    slots = {}

    def copy(w, kind, source, target, axis, by):
        slot = slots.setdefault(kind, len(slots))
        return pltpu.make_async_remote_copy(
            src_ref=source,
            dst_ref=target,
            send_sem=send_sem.at[w, slot],
            recv_sem=recv_sem.at[w, slot],
            device_id=peer_of(sizes, spot, axis, by),
            device_id_type=MESH,
        )

    def at_a(by):
        return lax.rem(a + by, down)

    def at_b(by):
        return lax.rem(b + by, across)

    twin, first, second, third = [], [], [], []
    for w in range(count):
        arrive = held["arrive"][w]
        twin.append(copy(w, "c", grads[w].at[:, 1 - c], arrive, 1, 1))
        first.append(
            [
                copy(w, ("a1", k), arrive.at[front, :, at_b(k)], held["first_a"][w].at[k - 1], 3, k)
                for k in range(1, across)
            ]
            + [
                copy(w, ("b1", l), arrive.at[back, at_a(l)], held["first_b"][w].at[l - 1], 2, l)
                for l in range(1, down)
            ]
        )
        second.append(
            [
                copy(w, ("a2", l), arrive.at[front, at_a(l), b], held["second_a"][w].at[l - 1], 2, l)
                for l in range(1, down)
            ]
            + [
                copy(w, ("b2", k), arrive.at[back, a, at_b(k)], held["second_b"][w].at[k - 1], 3, k)
                for k in range(1, across)
            ]
        )
        third.append(
            [
                copy(w, ("z", k), arrive.at[lax.rem(z + k, depth), a, b], held["third"][w].at[k - 1], 0, k)
                for k in range(1, depth)
            ]
        )

    stages = [(axis, 1 << bit) for axis in (1, 2, 3, 0) for bit in range(sizes[axis].bit_length() - 1)]

    def small_copy(at):
        axis, bit = stages[at]
        mine = spot[axis]
        towards = jnp.where(lax.rem(mine // bit, 2) == 0, bit, sizes[axis] - bit)
        return pltpu.make_async_remote_copy(
            src_ref=small_out,
            dst_ref=small_parts.at[at],
            send_sem=small_send.at[at],
            recv_sem=small_recv.at[at],
            device_id=peer_of(sizes, spot, axis, towards),
            device_id_type=MESH,
        )

    def own_load(w, at):
        return pltpu.make_async_copy(grads[w].at[at, c], held["own"][w].at[lax.rem(at, 2)], own_sem.at[w, lax.rem(at, 2)])

    def add_own(w):
        own_load(w, 0).start()

        def body(at, carry):
            @pl.when(at + 1 < depth)
            def _():
                own_load(w, at + 1).start()

            own_load(w, at).wait()
            for down_at in range(down):
                for across_at in range(across):
                    spot_ref = held["arrive"][w].at[at, down_at, across_at]
                    add_rows(spot_ref, spot_ref, [held["own"][w].at[lax.rem(at, 2), down_at, across_at]])
            return carry

        lax.fori_loop(0, depth, body, 0)

    small_out[...] = small[...]
    edges = spread_edge(seqs, edge, arrived, edge_send, edge_recv, False)
    units = rows * (chans // width)

    def last_unit(index, carry):
        row, base = unit_of(index, width, chans)
        ema_last(True, row, base, grad, keep, decay, edge, wide)
        return carry

    def backward_unit(index, carry):
        row, base = unit_of(index, width, chans)
        ema_backward(
            row, base, feed, grad, keep, decay, gain, start, end, back_out, small_out, wide, wide_grad, part, kept_states
        )
        return carry

    for w in range(min(2, count)):
        twin[w].start()
    lax.fori_loop(0, units, last_unit, 0)
    for item in edges:
        item.start()
    busy = count - 1
    for step in range(max(count + 3, busy + len(stages))):
        if step < count:
            w = step
            twin[w].wait_recv()
            if w + 2 < count:
                twin[w + 2].start()
            add_own(w)
            for item in first[w]:
                item.start()
        if 1 <= step <= count:
            w = step - 1
            arrive = held["arrive"][w]
            for item in first[w]:
                item.wait_recv()
            for at in range(half):
                for l in range(down):
                    spot_ref = arrive.at[at, l, b]
                    add_rows(spot_ref, spot_ref, [held["first_a"][w].at[k, at, l] for k in range(across - 1)])
            for at in range(half, depth):
                for k in range(across):
                    spot_ref = arrive.at[at, a, k]
                    add_rows(spot_ref, spot_ref, [held["first_b"][w].at[l, at - half, k] for l in range(down - 1)])
            for item in second[w]:
                item.start()
        if 2 <= step <= count + 1:
            w = step - 2
            arrive = held["arrive"][w]
            for item in second[w]:
                item.wait_recv()
            for at in range(half):
                spot_ref = arrive.at[at, a, b]
                add_rows(spot_ref, spot_ref, [held["second_a"][w].at[l, at] for l in range(down - 1)])
            for at in range(half, depth):
                spot_ref = arrive.at[at, a, b]
                add_rows(spot_ref, spot_ref, [held["second_b"][w].at[k, at - half] for k in range(across - 1)])
            for item in third[w]:
                item.start()
        if 3 <= step <= count + 2:
            w = step - 3
            for item in third[w]:
                item.wait_recv()
            add_rows(outs[w], held["arrive"][w].at[z, a, b], [held["third"][w].at[k] for k in range(depth - 1)])
        if step == 0:
            for item in edges:
                item.wait()
            join_edges(arrived, reach, power, end)
        if step < busy:
            lax.fori_loop(*share(units, busy, step), backward_unit, 0)
        stage = step - busy
        if stage == -1:
            small_copy(0).start()
        if 0 <= stage < len(stages):
            small_copy(stage).wait()
            small_out[...] = small_out[...] + small_parts[stage]
            if stage + 1 < len(stages):
                small_copy(stage + 1).start()
    for w in range(count):
        for item in [twin[w]] + first[w] + second[w] + third[w]:
            item.wait_send()


def scatter_grads(grads, small, feed, grad, keep, decay, gain, start, reach, power):
    sizes = shape_of()
    depth, cores, down, across = sizes
    total = depth * cores * down * across
    count = len(grads)
    half = depth // 2
    pieces = [piece_shape(g.shape[0] // total, g.shape[1]) for g in grads]
    leads = (
        (depth, down, across),
        (2, down, across),
        (across - 1, half, down),
        (down - 1, depth - half, across),
        (down - 1, half),
        (across - 1, depth - half),
        (depth - 1,),
    )
    slots = 1 + 2 * (across - 1 + down - 1) + depth - 1
    stages = sum(size.bit_length() - 1 for size in sizes)
    rows, length, chans = feed.shape
    state = (rows, 16, chans)
    width = min(BACKWARD_WIDTH, chans)
    seqs = down * across
    results = pl.pallas_call(
        functools.partial(scatter_kernel, sizes, count),
        out_shape=[jax.ShapeDtypeStruct(piece, jnp.float32) for piece in pieces]
        + [
            jax.ShapeDtypeStruct(small.shape, jnp.float32),
            jax.ShapeDtypeStruct(feed.shape, jnp.bfloat16),
        ],
        in_specs=anywhere(count) + vmem(9),
        out_specs=vmem(count + 2),
        scratch_shapes=[pltpu.VMEM(lead + piece, jnp.bfloat16) for lead in leads for piece in pieces]
        + [
            pltpu.VMEM((stages,) + small.shape, jnp.float32),
            pltpu.SemaphoreType.DMA((count, slots)),
            pltpu.SemaphoreType.DMA((count, slots)),
            pltpu.SemaphoreType.DMA((count, 2)),
            pltpu.SemaphoreType.DMA((stages,)),
            pltpu.SemaphoreType.DMA((stages,)),
            pltpu.VMEM(state, jnp.float32),
            pltpu.VMEM((seqs - 1,) + state, jnp.float32),
            pltpu.VMEM(state, jnp.float32),
            pltpu.SemaphoreType.DMA((seqs - 1,)),
            pltpu.SemaphoreType.DMA((seqs - 1,)),
            pltpu.VMEM((width // LANES, length, LANES), jnp.float32),
            pltpu.VMEM((width // LANES, length, LANES), jnp.float32),
            pltpu.VMEM((width // LANES * EMA_STEP * 8, LANES), jnp.float32),
            pltpu.VMEM((length * 16, width), jnp.float32),
        ],
        compiler_params=pltpu.CompilerParams(collective_id=1, has_side_effects=True, vmem_limit_bytes=62 * 2**20),
        name="scatter_grads",
    )(
        *[g.reshape(sizes + piece) for g, piece in zip(grads, pieces)],
        small, feed, grad, keep, decay, gain, start, reach, power,
    )
    sums = [result.reshape(g.shape[0] // total, g.shape[1]) for result, g in zip(results[:count], grads)]
    return sums, *results[count:]


def passed_on(alive, forward):
    count = lax.axis_size("seq")
    place = lax.axis_index("seq")
    through = jnp.ones((alive.shape[0], 1, 1), jnp.float32)
    factors = []
    for away in range(1, count):
        exists = place >= away if forward else place + away < count
        factors.append(jnp.broadcast_to(jnp.where(exists, through, 0.0), (alive.shape[0], 16, LANES)))
        at = jnp.clip(place - away if forward else place + away, 0, count - 1)
        through = through * lax.dynamic_slice_in_dim(alive, at, 1, 1)[:, :, None]
    return jnp.stack(factors)


QUERY_BLOCK = 256
KEY_BLOCK = 512
VALUE_BLOCK = 1024


def attend_kernel(halo_span, query, key, value, key_docs, query_docs, out, probs):
    size, span = probs.shape
    first = pl.program_id(1) * size
    keys = pl.ds(pl.multiple_of(first, LANES), span)
    scores = against(query[0], key[0, keys, :]) * Z ** (-0.5)
    query_at = lax.broadcasted_iota(jnp.int32, (size, span), 0) + halo_span
    key_at = lax.broadcasted_iota(jnp.int32, (size, span), 1)
    allowed = (key_at <= query_at) & (key_docs[0, :, keys] == query_docs[0])
    scores = jnp.where(allowed, scores, NEG_FILL)
    expo = jnp.exp(scores - jnp.max(scores, axis=1, keepdims=True))
    probs[...] = low(expo / jnp.sum(expo, axis=1, keepdims=True))

    def body(at, carry):
        columns = pl.ds(pl.multiple_of(at * VALUE_BLOCK, VALUE_BLOCK), VALUE_BLOCK)
        out[0, :, columns] = product(probs[...], value[0, keys, columns])
        return carry

    lax.fori_loop(0, out.shape[2] // VALUE_BLOCK, body, 0)


def attend(query, key, value, docs_row, docs_column, halo):
    rows, places, _ = query.shape
    window, wide = value.shape[1:]
    size = min(QUERY_BLOCK, places)
    span = halo * places + size
    return pl.pallas_call(
        functools.partial(attend_kernel, halo * places),
        out_shape=jax.ShapeDtypeStruct((rows, places, wide), jnp.float32),
        grid=(rows, places // size),
        in_specs=[
            pl.BlockSpec((1, size, Z), lambda r, i: (r, i, 0)),
            pl.BlockSpec((1, window, Z), lambda r, i: (r, 0, 0)),
            pl.BlockSpec((1, window, wide), lambda r, i: (r, 0, 0)),
            pl.BlockSpec((1, 1, window), lambda r, i: (r, 0, 0)),
            pl.BlockSpec((1, size, 1), lambda r, i: (r, i, 0)),
        ],
        out_specs=pl.BlockSpec((1, size, wide), lambda r, i: (r, i, 0)),
        scratch_shapes=[pltpu.VMEM((size, span), jnp.bfloat16)],
        compiler_params=pltpu.CompilerParams(vmem_limit_bytes=40 * 2**20),
        cost_estimate=pl.CostEstimate(
            flops=2 * rows * places * span * (wide + Z),
            bytes_accessed=rows * (window * wide * 2 + places * wide * 4),
            transcendentals=rows * places * span,
        ),
        name="attend",
    )(query, key, value, docs_row, docs_column[:, halo * places :])


def attend_back_kernel(
    halo_span, query, key, value, slope, pulled, key_docs, query_docs, d_query, d_key, d_value, chances, pulls, balance
):
    window, places = chances.shape
    step = d_value.shape[1]
    chunk = pl.program_id(1)

    @pl.when(chunk == 0)
    def _():
        peak = jnp.full((1, places), NEG_FILL, jnp.float32)

        def score(at, peak):
            keys = pl.ds(pl.multiple_of(at * step, step), step)
            scores = against(key[0, keys, :], query[0]) * Z ** (-0.5)
            key_at = lax.broadcasted_iota(jnp.int32, (step, places), 0) + at * step
            query_at = lax.broadcasted_iota(jnp.int32, (step, places), 1) + halo_span
            allowed = (key_at <= query_at) & (key_docs[0, keys, :] == query_docs[0])
            scores = jnp.where(allowed, scores, NEG_FILL)
            chances[keys, :] = scores
            return jnp.maximum(peak, jnp.max(scores, axis=0, keepdims=True))

        peak = lax.fori_loop(0, window // step, score, peak)

        def weigh(at, total):
            keys = pl.ds(pl.multiple_of(at * step, step), step)
            expo = jnp.exp(chances[keys, :] - peak)
            chances[keys, :] = expo
            return total + jnp.sum(expo, axis=0, keepdims=True)

        total = lax.fori_loop(0, window // step, weigh, jnp.zeros((1, places), jnp.float32))

        def pull(at, held):
            keys = pl.ds(pl.multiple_of(at * step, step), step)
            probs = chances[keys, :] / total
            chances[keys, :] = probs
            local = against(value[0, keys, :], pulled[0])
            pulls[keys, :] = local
            return held + jnp.sum(probs * local, axis=0, keepdims=True)

        balance[...] = lax.fori_loop(0, window // step, pull, jnp.zeros((1, places), jnp.float32))
        d_query[...] = jnp.zeros_like(d_query)

    keys = pl.ds(pl.multiple_of(chunk * step, step), step)
    probs = chances[keys, :]
    d_scores = low(probs * (pulls[keys, :] - balance[...]))
    d_key[0] = product(d_scores, query[0]) * Z ** (-0.5)
    d_query[0] = d_query[0] + transposed(d_scores, key[0, keys, :]) * Z ** (-0.5)
    probs_low = low(probs)

    def body(at, carry):
        columns = pl.ds(pl.multiple_of(at * VALUE_BLOCK, VALUE_BLOCK), VALUE_BLOCK)
        local = product(probs_low, pulled[0, :, columns])
        d_value[0, :, columns] = low(local * slope[0, :, columns].astype(jnp.float32))
        return carry

    lax.fori_loop(0, d_value.shape[2] // VALUE_BLOCK, body, 0)


def attend_back(query, key, value, slope, pulled, docs_row, docs_column, halo):
    rows, places, _ = query.shape
    window, wide = value.shape[1:]
    step = min(KEY_BLOCK, places)
    return pl.pallas_call(
        functools.partial(attend_back_kernel, halo * places),
        out_shape=[
            jax.ShapeDtypeStruct((rows, places, Z), jnp.float32),
            jax.ShapeDtypeStruct((rows, window, Z), jnp.float32),
            jax.ShapeDtypeStruct((rows, window, wide), jnp.bfloat16),
        ],
        grid=(rows, window // step),
        in_specs=[
            pl.BlockSpec((1, places, Z), lambda r, i: (r, 0, 0)),
            pl.BlockSpec((1, window, Z), lambda r, i: (r, 0, 0)),
            pl.BlockSpec((1, window, wide), lambda r, i: (r, 0, 0)),
            pl.BlockSpec((1, step, wide), lambda r, i: (r, i, 0)),
            pl.BlockSpec((1, places, wide), lambda r, i: (r, 0, 0)),
            pl.BlockSpec((1, window, 1), lambda r, i: (r, 0, 0)),
            pl.BlockSpec((1, 1, places), lambda r, i: (r, 0, 0)),
        ],
        out_specs=[
            pl.BlockSpec((1, places, Z), lambda r, i: (r, 0, 0)),
            pl.BlockSpec((1, step, Z), lambda r, i: (r, i, 0)),
            pl.BlockSpec((1, step, wide), lambda r, i: (r, i, 0)),
        ],
        scratch_shapes=[
            pltpu.VMEM((window, places), jnp.float32),
            pltpu.VMEM((window, places), jnp.float32),
            pltpu.VMEM((1, places), jnp.float32),
        ],
        compiler_params=pltpu.CompilerParams(vmem_limit_bytes=48 * 2**20),
        cost_estimate=pl.CostEstimate(
            flops=4 * rows * places * window * (wide + Z),
            bytes_accessed=rows * (window * wide * 6 + places * wide * 2),
            transcendentals=rows * places * window,
        ),
        name="attend_back",
    )(query, key, value, slope, pulled, docs_column, docs_row[:, :, halo * places :])


def on_device(
    layer_input,
    cotangent,
    doc_ids,
    resets,
    mix_weight,
    value_weight,
    head_weight,
    expand_weight,
    shrink_weight,
    chan_vectors,
    ema_logits,
    ema_beta_eta,
    z_affine,
):
    seq_count = lax.axis_size("seq")
    seq_place = lax.axis_index("seq")
    rows, places, width = layer_input.shape
    tokens = rows * places
    halo = min(-(-(REACH - 1) // places), seq_count - 1)
    window = (halo + 1) * places

    inputs32 = layer_input.astype(jnp.float32)
    center = inputs32 - jnp.mean(inputs32, axis=-1, keepdims=True)
    unit = lax.rsqrt(jnp.mean(center * center, axis=-1, keepdims=True) + 1e-05)
    plain = center * unit
    normed = plain * chan_vectors[0]
    normed_low = low(normed)

    rate = jax.nn.sigmoid(ema_logits[0])
    damping = jax.nn.sigmoid(ema_logits[1])
    decay = (1.0 - rate * damping).T
    weight_in = rate * ema_beta_eta[0]
    weight_out = ema_beta_eta[1]
    gain = (weight_in * weight_out).T
    decay_all = decay
    reach = 1
    while reach < places:
        decay_all = decay_all * decay_all
        reach *= 2
    powers = [jnp.ones_like(decay)]
    while len(powers) < seq_count - 1:
        powers.append(powers[-1] * decay_all)
    power = jnp.stack(powers)
    keep_row = 1.0 - resets.astype(jnp.float32)
    keep_own = lax.dynamic_slice_in_dim(keep_row, seq_place * places, places, 1)
    keep = jnp.broadcast_to(keep_own[:, None, :, None], (rows, 1, places, LANES)).reshape(rows, places, LANES)
    alive = jnp.min(keep_row.reshape(rows, seq_count, places), axis=2)

    (value_full, mix_full, head_full, expand_full), normed_window, start, ema_low, *made = gather_weights(
        (value_weight, mix_weight, head_weight, expand_weight),
        normed_low,
        keep,
        decay,
        gain,
        passed_on(alive, True),
        power,
        halo,
    )
    normed_window = normed_window.reshape(rows * window, width)
    value_full, mix_full, head_full, expand_full, shrink_late = lax.optimization_barrier(
        (value_full, mix_full, head_full, expand_full, shrink_weight)
    )
    shrink_full = lax.all_gather(shrink_late, BOTH, axis=0, tiled=True)

    premix = (ema_low.astype(jnp.float32) + chan_vectors[2] * normed).reshape(tokens, width)
    mixed_low = low(jax.nn.silu(premix))
    if made:
        values_low, value_slope = (item.reshape(rows, window, V) for item in made)
    else:
        value_pre = product(normed_window, value_full)
        values_low = low(jax.nn.silu(value_pre)).reshape(rows, window, V)
        value_slope = low(silu_slope(value_pre)).reshape(rows, window, V)
    shared_pre = product(mixed_low, mix_full[:, :Z])
    shared = jax.nn.silu(shared_pre)
    queries_low = low(shared * z_affine[0] + z_affine[1]).reshape(rows, places, Z)
    keys_low = low(shared * z_affine[2]).reshape(rows, places, Z)
    keys_low, mixed_low = lax.optimization_barrier((keys_low, mixed_low))
    key_window = jnp.concatenate([shift_seq(keys_low, by) for by in range(halo, 0, -1)] + [keys_low], axis=1)
    projected = product(mixed_low, mix_full)
    reset_pre = projected[:, Z : Z + V]
    head_base = projected[:, Z + V : Z + V + width]
    update_pre = projected[:, Z + V + width :]
    reset_gate = jax.nn.silu(reset_pre)
    update_gate = jax.nn.sigmoid(update_pre)

    padded_docs = jnp.pad(doc_ids, ((0, 0), (halo * places, 0)), constant_values=-1)
    key_docs = lax.dynamic_slice_in_dim(padded_docs, seq_place * places, window, 1)
    docs_row, docs_column = key_docs[:, None, :], key_docs[:, :, None]
    attended = attend(queries_low, key_window, values_low, docs_row, docs_column, halo).reshape(tokens, V)
    gated_low = low(reset_gate * attended)
    head_pre = head_base + product(gated_low, head_full)
    candidate = jax.nn.silu(head_pre)
    residual_in = inputs32.reshape(tokens, width)
    first = residual_in + update_gate * (candidate - residual_in)
    second, second_pull = jax.vjp(scaled_norm, first, chan_vectors[1])
    second_low = low(second)
    expand_pre = product(second_low, expand_full)
    expand_slope = silu_slope(expand_pre)
    hidden_low, expand_slope = lax.optimization_barrier((low(jax.nn.silu(expand_pre)), expand_slope))
    output = low(first + product(hidden_low, shrink_full)).reshape(rows, places, width)

    cot_low = cotangent.reshape(tokens, width)
    shrink_part = low(transposed(hidden_low, cot_low))
    d_expand = low(against(cot_low, shrink_full) * expand_slope)
    expand_part = low(transposed(second_low, d_expand))
    d_first_norm, d_gain_two = second_pull(against(d_expand, expand_full))
    d_first = cot_low.astype(jnp.float32) + d_first_norm
    d_update = d_first * (candidate - residual_in) * update_gate * (1.0 - update_gate)
    d_direct = d_first * (1.0 - update_gate)
    d_head = d_first * update_gate * silu_slope(head_pre)
    d_head_low = low(d_head)
    head_part = low(transposed(gated_low, d_head_low))
    d_gated = against(d_head_low, head_full)
    d_reset = d_gated * attended * silu_slope(reset_pre)
    d_attended = low(d_gated * reset_gate).reshape(rows, places, V)
    d_queries, key_term, d_value_pre = attend_back(
        queries_low, key_window, values_low, value_slope, d_attended, docs_row, docs_column, halo
    )
    d_value_pre = d_value_pre.reshape(rows * window, V)
    d_keys = key_term[:, halo * places :]
    for by in range(1, halo + 1):
        begin = (halo - by) * places
        d_keys = d_keys + shift_seq(low(key_term[:, begin : begin + places]), -by).astype(jnp.float32)
    d_keys32 = low(d_keys).astype(jnp.float32).reshape(tokens, Z)
    value_part = low(transposed(normed_window, d_value_pre))
    value_term = against(d_value_pre, value_full).reshape(rows, halo + 1, places, width)
    terms = low(value_term[:, :halo])
    d_normed_value = value_term[:, halo]
    for by in range(1, halo + 1):
        d_normed_value = d_normed_value + shift_seq(terms[:, halo - by], -by).astype(jnp.float32)
    d_query_flat = d_queries.reshape(tokens, Z)
    d_shared = d_query_flat * z_affine[0] + d_keys32 * z_affine[2]
    affine_part = jnp.stack(
        [
            jnp.sum(d_query_flat * shared, axis=0),
            jnp.sum(d_query_flat, axis=0),
            jnp.sum(d_keys32 * shared, axis=0),
        ]
    )
    d_projected = low(
        jnp.concatenate([d_shared * silu_slope(shared_pre), d_reset, d_head, d_update], axis=1)
    )
    mix_part = low(transposed(mixed_low, d_projected))
    d_premix = against(d_projected, mix_full) * silu_slope(premix)
    omega_part = jnp.sum(d_premix * normed.reshape(tokens, width), axis=0)
    d_premix = d_premix.reshape(rows, places, width)
    d_ema = low(d_premix)
    known = d_premix * chan_vectors[2] + d_normed_value
    d_gain_one = jnp.sum(known * plain, axis=(0, 1))
    small_part = jnp.concatenate(
        [
            jnp.zeros((32, width), jnp.float32),
            jnp.stack([d_gain_one, d_gain_two, omega_part]),
            jnp.pad(affine_part.reshape(1, 3 * Z), ((0, 4), (0, width - 3 * Z))),
        ],
        axis=0,
    )
    (shrink_grad, expand_grad, head_grad, value_grad, mix_grad), small_sum, d_feed = scatter_grads(
        (shrink_part, expand_part, head_part, value_part, mix_part),
        small_part,
        normed_low,
        d_ema,
        keep,
        decay,
        gain,
        start,
        passed_on(alive, False),
        power,
    )
    d_normed = known + d_feed.astype(jnp.float32)
    pulled = d_normed * chan_vectors[0]
    pulled = pulled - jnp.mean(pulled, axis=-1, keepdims=True) - plain * jnp.mean(pulled * plain, axis=-1, keepdims=True)
    x_grad = d_direct.reshape(rows, places, width) + pulled * unit
    gain_sum = small_sum[:16]
    decay_sum = small_sum[16:32]
    chan_grad = small_sum[32:35].at[0].add(jnp.sum(gain * gain_sum, axis=0) / chan_vectors[0])
    affine_grad = small_sum[35, : 3 * Z].reshape(3, Z)
    d_gain = gain_sum.T
    d_decay = (decay_sum * gain).T
    d_weight_in = d_gain * weight_out
    coef_grad = jnp.stack([d_weight_in * rate, d_gain * weight_in])
    d_rate = d_weight_in * ema_beta_eta[0] - d_decay * damping
    d_damping = -d_decay * rate
    logits_grad = jnp.stack([d_rate * rate * (1.0 - rate), d_damping * damping * (1.0 - damping)])
    return (
        output,
        x_grad,
        mix_grad,
        value_grad,
        head_grad,
        expand_grad,
        shrink_grad,
        chan_grad,
        logits_grad,
        coef_grad,
        affine_grad,
    )


def solution(mesh):
    placed = (
        P("dp", "seq", None),
        P("dp", "seq", None),
        P("dp", None),
        P("dp", None),
        P(BOTH, None),
        P(BOTH, None),
        P(BOTH, None),
        P(BOTH, None),
        P(BOTH, None),
        P(),
        P(),
        P(),
        P(),
    )
    return jax.shard_map(
        on_device,
        mesh=mesh,
        in_specs=placed,
        out_specs=(
            P("dp", "seq", None),
            P("dp", "seq", None),
            P(BOTH, None),
            P(BOTH, None),
            P(BOTH, None),
            P(BOTH, None),
            P(BOTH, None),
            P(),
            P(),
            P(),
            P(),
        ),
        check_vma=False,
    )
```

```python
import functools
import jax
import jax.numpy as jnp
from jax import lax
from jax.experimental import pallas as pl
from jax.experimental.pallas import tpu as pltpu
from jax.sharding import PartitionSpec as P

Z = 128
V = 2048
REACH = 1024
NEG_FILL = -1000000000.0
BOTH = ("dp", "seq")
MESH = pl.DeviceIdType.MESH
LANES = 128
EMA_STEP = 16
FORWARD_WIDTH = 512
BACKWARD_WIDTH = 256
HOST_TILE = 512


def lanes_at(base, group):
    return pl.ds(pl.multiple_of(base + group * LANES, LANES), LANES)


def row_of(ref, step, group):
    return ref[group, pl.ds(step, 8, stride=0), :]


def widen(source, row, base, wide):
    for group in range(wide.shape[0]):
        wide[group] = source[row, :, lanes_at(base, group)].astype(jnp.float32)


def halves_of(ref, base, groups, row=None):
    spots = [(slice(h * 8, h * 8 + 8), lanes_at(base, g)) for g in range(groups) for h in range(2)]
    return [ref[spot] if row is None else ref[(row,) + spot] for spot in spots]


def put_halves(ref, base, values, row):
    for at, value in enumerate(values):
        g, h = divmod(at, 2)
        ref[row, h * 8 : h * 8 + 8, lanes_at(base, g)] = value


def add_halves(ref, first, base, values):
    for at, value in enumerate(values):
        g, h = divmod(at, 2)
        spot = (slice(first + h * 8, first + h * 8 + 8), lanes_at(base, g))
        ref[spot] = ref[spot] + value


def fold_rows(part, group):
    halves = []
    for half in range(EMA_STEP // 8):
        base = group * EMA_STEP * 8 + half * 64
        total = part[pl.ds(base, 8, stride=8), :]
        for sub in range(1, 8):
            total = total + part[pl.ds(base + sub, 8, stride=8), :]
        halves.append(total)
    return jnp.concatenate(halves, axis=0).astype(jnp.bfloat16)


def unit_of(index, width, chans):
    across = chans // width
    return lax.div(index, across), pl.multiple_of(lax.rem(index, across) * width, width)


def ema_last(reverse, row, base, feed, keep, decay, last, wide):
    length, groups = feed.shape[1], wide.shape[0]
    widen(feed, row, base, wide)
    decays = halves_of(decay, base, groups)

    def body(index, states):
        states = list(states)
        block = (length // EMA_STEP - 1 - index) if reverse else index
        first = pl.multiple_of(block * EMA_STEP, EMA_STEP)
        for offset in range(EMA_STEP):
            step = first + (EMA_STEP - 1 - offset if reverse else offset)
            kept = row_of(keep, step, row)
            for at in range(2 * groups):
                fed = row_of(wide, step, at // 2)
                if reverse:
                    states[at] = (kept * decays[at]) * (states[at] + fed)
                else:
                    states[at] = (kept * decays[at]) * states[at] + fed
        return tuple(states)

    zero = jnp.zeros((8, LANES), jnp.float32)
    put_halves(last, base, lax.fori_loop(0, length // EMA_STEP, body, (zero,) * (2 * groups)), row)


def ema_forward(row, base, feed, keep, decay, gain, start, out, wide, part):
    length, groups = feed.shape[1], wide.shape[0]
    widen(feed, row, base, wide)
    decays, gains = halves_of(decay, base, groups), halves_of(gain, base, groups)

    def body(index, states):
        states = list(states)
        first = pl.multiple_of(index * EMA_STEP, EMA_STEP)
        for offset in range(EMA_STEP):
            kept = row_of(keep, first + offset, row)
            for g in range(groups):
                fed = row_of(wide, first + offset, g)
                both = []
                for at in (2 * g, 2 * g + 1):
                    states[at] = (kept * decays[at]) * states[at] + fed
                    both.append(gains[at] * states[at])
                spot = g * EMA_STEP * 8 + offset * 8
                part[spot : spot + 8, :] = both[0] + both[1]
        for g in range(groups):
            out[row, pl.ds(first, EMA_STEP), lanes_at(base, g)] = fold_rows(part, g)
        return tuple(states)

    lax.fori_loop(0, length // EMA_STEP, body, tuple(halves_of(start, base, groups, row)))


def ema_backward(row, base, feed, grad, keep, decay, gain, start, end, back, sums, wide, wide_grad, part, held):
    length, groups = feed.shape[1], wide.shape[0]
    widen(feed, row, base, wide)
    widen(grad, row, base, wide_grad)
    decays, gains = halves_of(decay, base, groups), halves_of(gain, base, groups)
    blocks = length // EMA_STEP

    def forward(index, states):
        states = list(states)
        first = pl.multiple_of(index * EMA_STEP, EMA_STEP)
        for offset in range(EMA_STEP):
            kept = row_of(keep, first + offset, row)
            for at in range(2 * groups):
                g, h = divmod(at, 2)
                held[pl.ds((first + offset) * 16 + h * 8, 8), g * LANES : (g + 1) * LANES] = kept * states[at]
                states[at] = (kept * decays[at]) * states[at] + row_of(wide, first + offset, g)
        return tuple(states)

    lax.fori_loop(0, blocks, forward, tuple(halves_of(start, base, groups, row)))

    def backward(index, carried):
        pulls, gain_sums, decay_sums = (list(c) for c in carried)
        first = pl.multiple_of((blocks - 1 - index) * EMA_STEP, EMA_STEP)
        for offset in reversed(range(EMA_STEP)):
            step = first + offset
            kept = row_of(keep, step, row)
            for g in range(groups):
                pulled, fed = row_of(wide_grad, step, g), row_of(wide, step, g)
                both = []
                for h in range(2):
                    at = 2 * g + h
                    local = pulls[at] + pulled
                    both.append(gains[at] * local)
                    gain_sums[at] = gain_sums[at] + local * fed
                    before = held[pl.ds(step * 16 + h * 8, 8), g * LANES : (g + 1) * LANES]
                    decay_sums[at] = decay_sums[at] + local * before
                    pulls[at] = (kept * decays[at]) * local
                spot = g * EMA_STEP * 8 + offset * 8
                part[spot : spot + 8, :] = both[0] + both[1]
        for g in range(groups):
            back[row, pl.ds(first, EMA_STEP), lanes_at(base, g)] = fold_rows(part, g)
        return (tuple(pulls), tuple(gain_sums), tuple(decay_sums))

    zeros = (jnp.zeros((8, LANES), jnp.float32),) * (2 * groups)
    _, gain_sums, decay_sums = lax.fori_loop(
        0, blocks, backward, (tuple(halves_of(end, base, groups, row)), zeros, zeros)
    )
    add_halves(sums, 0, base, gain_sums)
    add_halves(sums, 16, base, decay_sums)


def layer_norm(values):
    center = values - jnp.mean(values, axis=-1, keepdims=True)
    spread = jnp.mean(center * center, axis=-1, keepdims=True)
    return center * lax.rsqrt(spread + 1e-05)


def scaled_norm(values, gain):
    return layer_norm(values) * gain


def silu_slope(values):
    squash = jax.nn.sigmoid(values)
    return squash * (1.0 + values * (1.0 - squash))


def product(left, right):
    return jnp.dot(left, right, preferred_element_type=jnp.float32)


def against(left, right):
    return lax.dot_general(left, right, (((1,), (1,)), ((), ())), preferred_element_type=jnp.float32)


def transposed(left, right):
    return lax.dot_general(left, right, (((0,), (0,)), ((), ())), preferred_element_type=jnp.float32)


def low(values):
    return values.astype(jnp.bfloat16)


def shift_seq(values, by):
    count = lax.axis_size("seq")
    pairs = [(i, i + by) for i in range(count) if 0 <= i + by < count]
    return lax.ppermute(values, "seq", pairs)


def side_of(count):
    side = 1
    while side * side < count:
        side *= 2
    return side


def shape_of():
    depth = lax.axis_size("dp") // 2
    seqs = lax.axis_size("seq")
    down = side_of(seqs)
    return depth, 2, down, seqs // down


def place_of():
    depth, cores, down, across = shape_of()
    dp, seq = lax.axis_index("dp"), lax.axis_index("seq")
    return lax.div(dp, cores), lax.rem(dp, cores), lax.div(seq, across), lax.rem(seq, across)


def peer_of(sizes, spot, axis, by):
    spot = list(spot)
    spot[axis] = lax.rem(spot[axis] + by, sizes[axis])
    return {"dp": spot[0] * sizes[1] + spot[1], "seq": spot[2] * sizes[3] + spot[3]}


def along(count, by):
    return {"dp": lax.axis_index("dp"), "seq": lax.rem(lax.axis_index("seq") + by, count)}


def greet(sizes, spot):
    barrier = pltpu.get_barrier_semaphore()
    seqs = sizes[2] * sizes[3]
    peers = [peer_of(sizes, spot, axis, by) for axis in (0, 1) for by in range(1, sizes[axis])]
    peers += [along(seqs, by) for by in range(1, seqs)]
    for peer in peers:
        pl.semaphore_signal(barrier, inc=1, device_id=peer, device_id_type=MESH)
    pl.semaphore_wait(barrier, len(peers))


def piece_shape(rows, columns):
    return (rows, columns) if rows % 16 == 0 else (rows * columns // LANES, LANES)


def chunks_of(pieces):
    chunks = []
    for at, (rows, columns) in enumerate(pieces):
        if rows * columns >= 2**17:
            half = columns // (2 * LANES) * LANES
            chunks += [(at, pl.ds(0, half)), (at, pl.ds(half, columns - half))]
        else:
            chunks.append((at, pl.ds(0, columns)))
    return chunks


def share(total, parts, at):
    return total * at // parts, total * (at + 1) // parts


def spread_edge(seqs, edge, arrived, send, recv, forward):
    return [
        pltpu.make_async_remote_copy(
            src_ref=edge,
            dst_ref=arrived.at[by - 1],
            send_sem=send.at[by - 1],
            recv_sem=recv.at[by - 1],
            device_id=along(seqs, by if forward else seqs - by),
            device_id_type=MESH,
        )
        for by in range(1, seqs)
    ]


def join_edges(arrived, reach, power, entry):
    rows, _, chans = entry.shape

    def body(row, carry):
        for group in range(chans // LANES):
            spot = slice(group * LANES, (group + 1) * LANES)
            total = None
            for at in range(arrived.shape[0]):
                term = reach[at, row] * power[at, :, spot] * arrived[at, row, :, spot]
                total = term if total is None else total + term
            entry[row, :, spot] = total
        return carry

    lax.fori_loop(0, rows, body, 0)


class Halo:
    def __init__(self, count, seqs, feed, window, zero, send, recv, local, hand_send):
        place = lax.axis_index("seq")
        relay = seqs == 4 and count == 2
        self.items = []

        def copy(source, by, towards, sent):
            return pltpu.make_async_remote_copy(
                src_ref=source,
                dst_ref=window.at[:, count - by],
                send_sem=sent,
                recv_sem=recv.at[by - 1],
                device_id=along(seqs, towards),
                device_id_type=MESH,
            )

        for by in range(1, count + 1):
            gives = place + by < seqs
            if relay and by == 1:
                gives = jnp.logical_and(gives, place != 1)
            blank = pltpu.make_async_copy(zero, window.at[:, count - by], local.at[by - 1])
            self.items.append((gives, place >= by, copy(feed, by, by, send.at[by - 1]), blank))
        self.hands = (place == 3, copy(window.at[:, 0], 1, 3, hand_send.at[0])) if relay else None

    def start(self):
        for gives, takes, remote, blank in self.items:
            pl.when(gives)(remote.start)
            pl.when(jnp.logical_not(takes))(blank.start)

    def hand_on(self):
        if self.hands:
            at_hand, hand = self.hands

            @pl.when(at_hand)
            def _():
                self.items[1][2].wait_recv()
                hand.start()

    def wait(self):
        for at, (gives, takes, remote, blank) in enumerate(self.items):
            waits = takes
            if self.hands and at == 1:
                waits = jnp.logical_and(takes, jnp.logical_not(self.hands[0]))
            pl.when(waits)(remote.wait_recv)
            pl.when(jnp.logical_not(takes))(blank.wait)
            pl.when(gives)(remote.wait_send)
        if self.hands:
            pl.when(self.hands[0])(self.hands[1].wait_send)


def gather_kernel(sizes, count, halo, hosts, chunks, *refs):
    shards, (feed, keep, decay, gain, reach, power) = refs[:count], refs[count : count + 6]
    wholes, (window, entry, out) = refs[count + 6 : 2 * count + 6], refs[2 * count + 6 : 2 * count + 9]
    if hosts:
        values, slopes = refs[2 * count + 9 : 2 * count + 11]
        weight, block_in, value_tile, slope_tile, weight_sem, in_sem, out_sem = refs[-7:]
        refs = refs[: 2 * count + 9] + refs[2 * count + 11 : -7]
    (
        send_sem, recv_sem, local_sem, edge, arrived, edge_send, edge_recv,
        zero, halo_send, halo_recv, halo_local, hand_send, wide_feed, part,
    ) = refs[2 * count + 9 :]
    rows, length, chans = feed.shape
    width = wide_feed.shape[0] * LANES
    seqs = sizes[2] * sizes[3]
    depth, cores, down, across = sizes
    spot = place_of()
    z, c, a, b = spot
    half = depth // 2
    greet(sizes, spot)
    slots = {}

    def copy(w, kind, source, target, axis, by):
        slot = slots.setdefault(kind, len(slots))
        return pltpu.make_async_remote_copy(
            src_ref=source,
            dst_ref=target,
            send_sem=send_sem.at[w, slot],
            recv_sem=recv_sem.at[w, slot],
            device_id=peer_of(sizes, spot, axis, by),
            device_id_type=MESH,
        )

    def block(w, a_by=0, b_by=0, part=None):
        at = pl.ds(0, depth) if part is None else part
        whole, columns = chunks[w]
        beside = lax.rem(a - a_by + down, down), lax.rem(b - b_by + across, across)
        return wholes[whole].at[at, c, *beside, :, columns]

    front, back = pl.ds(0, half), pl.ds(half, depth - half)
    local, line, wide, tall, cross, twin = [], [], [], [], [], []
    flat, count = len(chunks) - 1, len(chunks) - 1
    for w, (whole, columns) in enumerate(chunks[:count]):
        own = wholes[whole].at[z, c, a, b, :, columns]
        shard = shards[whole].at[:, columns]
        local.append(pltpu.make_async_copy(shard, own, local_sem.at[w]))
        line.append([copy(w, ("z", k), shard, own, 0, k) for k in range(1, depth)])
        wide.append([copy(w, ("x", k), block(w), block(w), 3, k) for k in range(1, across)])
        tall.append([copy(w, ("y", l), block(w), block(w), 2, l) for l in range(1, down)])
        pairs = [(k, l) for k in range(1, across) for l in range(1, down)]
        cross.append(
            {
                (k, l): (
                    copy(w, ("f", k, l), block(w, 0, k, front), block(w, 0, k, front), 2, l),
                    copy(w, ("g", k, l), block(w, l, 0, back), block(w, l, 0, back), 3, k),
                )
                for k, l in pairs
            }
        )
        twin.append(
            {
                (l, k): copy(w, ("c", l, k), block(w, l, k), block(w, l, k), 1, 1)
                for l in range(down)
                for k in range(across)
            }
        )
    whole, columns = chunks[flat]

    def plane(back_by=0):
        return wholes[whole].at[lax.rem(z - back_by + depth, depth), c, :, :, :, columns]

    def flat_copy(slot, source, target, device):
        return pltpu.make_async_remote_copy(
            src_ref=source,
            dst_ref=target,
            send_sem=send_sem.at[flat, slot],
            recv_sem=recv_sem.at[flat, slot],
            device_id=device,
            device_id_type=MESH,
        )

    flat_shard, flat_own = shards[whole].at[:, columns], wholes[whole].at[z, c, a, b, :, columns]
    flat_local = pltpu.make_async_copy(flat_shard, flat_own, local_sem.at[flat])
    flat_row = [flat_copy(by - 1, flat_shard, flat_own, along(seqs, by)) for by in range(1, seqs)]
    flat_line = [
        flat_copy(seqs - 2 + k, plane(), plane(), peer_of(sizes, spot, 0, k)) for k in range(1, depth)
    ]
    flat_twin = [
        flat_copy(seqs + depth - 2 + k, plane(k), plane(k), peer_of(sizes, spot, 1, 1)) for k in range(depth)
    ]
    zero[...] = jnp.zeros_like(zero)
    around = Halo(halo, seqs, feed, window, zero, halo_send, halo_recv, halo_local, hand_send)
    own = pltpu.make_async_copy(feed, window.at[:, halo], local_sem.at[count + 1])
    edges = spread_edge(seqs, edge, arrived, edge_send, edge_recv, True)
    for w in range(count):
        local[w].start()
    for item in line[0]:
        item.start()
    own.start()
    around.start()
    flat_local.start()
    for item in flat_row:
        item.start()
    for w in range(1, min(2, count)):
        for item in line[w]:
            item.start()
    units = rows * (chans // width)

    def last_unit(index, carry):
        row, base = unit_of(index, width, chans)
        ema_last(False, row, base, feed, keep, decay, edge, wide_feed)
        return carry

    def forward_unit(index, carry):
        row, base = unit_of(index, width, chans)
        ema_forward(row, base, feed, keep, decay, gain, entry, out, wide_feed, part)
        return carry

    def block_place(index):
        return lax.rem(index, rows), halo - lax.div(index, rows)

    def load_block(index):
        slot = lax.rem(index, 2)
        return pltpu.make_async_copy(window.at[block_place(index)], block_in.at[slot], in_sem.at[slot])

    def store_tiles(index):
        slot = lax.rem(index, 2)
        row, back_by = block_place(lax.div(index, tiles))
        columns = pl.ds(pl.multiple_of(lax.rem(index, tiles) * HOST_TILE, HOST_TILE), HOST_TILE)
        return [
            pltpu.make_async_copy(tile.at[slot], whole.at[row, back_by, :, columns], out_sem.at[at, slot])
            for at, (tile, whole) in enumerate(((value_tile, values), (slope_tile, slopes)))
        ]

    blocks = rows * (halo + 1)
    tiles = wholes[0].shape[-1] // HOST_TILE

    def value_unit(index, carry):
        block, slot = lax.div(index, tiles), lax.rem(index, 2)

        @pl.when(lax.rem(index, tiles) == 0)
        def _():
            load_block(block).wait()

            @pl.when(block + 1 < blocks)
            def _():
                load_block(block + 1).start()

        columns = pl.ds(pl.multiple_of(lax.rem(index, tiles) * HOST_TILE, HOST_TILE), HOST_TILE)
        part_weight = weight[:, :, :, :, :, columns].reshape(chans, HOST_TILE)
        before = product(block_in[lax.rem(block, 2)], part_weight)
        squash = jax.nn.sigmoid(before)

        @pl.when(index >= 2)
        def _():
            for item in store_tiles(index - 2):
                item.wait()

        value_tile[slot] = low(before * squash)
        slope_tile[slot] = low(squash * (1.0 + before * (1.0 - squash)))
        for item in store_tiles(index):
            item.start()
        return carry

    lax.fori_loop(0, units, last_unit, 0)
    for item in edges:
        item.start()
    for step in range(count + 2):
        if step < count:
            w = step
            local[w].wait()
            for item in line[w]:
                item.wait_recv()
            for item in wide[w] + tall[w]:
                item.start()
            twin[w][0, 0].start()
            if w + 2 < count:
                for item in line[w + 2]:
                    item.start()
        if 1 <= step <= count:
            w = step - 1
            for k in range(1, across):
                wide[w][k - 1].wait_recv()
                for l in range(1, down):
                    cross[w][k, l][0].start()
                twin[w][0, k].start()
            for l in range(1, down):
                tall[w][l - 1].wait_recv()
                for k in range(1, across):
                    cross[w][k, l][1].start()
                twin[w][l, 0].start()
        if step >= 2:
            w = step - 2
            for (k, l), both in cross[w].items():
                both[0].wait_recv()
                both[1].wait_recv()
                twin[w][l, k].start()
        if step == 0:
            for item in edges:
                item.wait()
            join_edges(arrived, reach, power, entry)
        if step == 1:
            around.hand_on()
            flat_local.wait()
            for item in flat_row:
                item.wait_recv()
            for item in flat_line + flat_twin[:1]:
                item.start()
        if step == count:
            for item, on in zip(flat_line, flat_twin[1:]):
                item.wait_recv()
                on.start()
        lax.fori_loop(*share(units, count + 2, step), forward_unit, 0)
        if hosts and step == 2:
            for item in twin[0].values():
                item.wait_recv()
            full = pltpu.make_async_copy(wholes[0], weight, weight_sem.at[0])
            full.start()
            own.wait()
            around.wait()
            load_block(0).start()
            full.wait()
        if hosts and step >= 2:
            lax.fori_loop(*share(blocks * tiles, count, step - 2), value_unit, 0)
    if hosts:
        for index in (blocks * tiles - 2, blocks * tiles - 1):
            for item in store_tiles(index):
                item.wait()
    for item in flat_twin:
        item.wait()
    for item in flat_row + flat_line:
        item.wait_send()
    for w in range(count):
        for item in twin[w].values():
            item.wait_send()
            if w or not hosts:
                item.wait_recv()
        for item in line[w] + wide[w] + tall[w]:
            item.wait_send()
        for both in cross[w].values():
            both[0].wait_send()
            both[1].wait_send()
    if not hosts:
        own.wait()
        around.wait()


def vmem(count):
    return [pl.BlockSpec(memory_space=pltpu.VMEM)] * count


def anywhere(count):
    return [pl.BlockSpec(memory_space=pl.ANY)] * count


def gather_weights(shards, feed, keep, decay, gain, reach, power, halo):
    sizes = shape_of()
    depth, cores, down, across = sizes
    seqs = down * across
    count = len(shards)
    pieces = [piece_shape(*shard.shape) for shard in shards]
    slots = (depth - 1) + (across - 1) + (down - 1) + 2 * (across - 1) * (down - 1) + across * down
    rows, length, chans = feed.shape
    state = (rows, 16, chans)
    width = min(FORWARD_WIDTH, chans)
    hosts = pieces[0] == shards[0].shape
    chunks = chunks_of(pieces)
    made, extra = [], []
    if hosts:
        wide = shards[0].shape[1]
        made = [jax.ShapeDtypeStruct((rows, halo + 1, length, wide), jnp.bfloat16)] * 2
        extra = [
            pltpu.VMEM(sizes + pieces[0], jnp.bfloat16),
            pltpu.VMEM((2, length, chans), jnp.bfloat16),
            pltpu.VMEM((2, length, HOST_TILE), jnp.bfloat16),
            pltpu.VMEM((2, length, HOST_TILE), jnp.bfloat16),
            pltpu.SemaphoreType.DMA((1,)),
            pltpu.SemaphoreType.DMA((2,)),
            pltpu.SemaphoreType.DMA((2, 2)),
        ]
    results = pl.pallas_call(
        functools.partial(gather_kernel, sizes, count, halo, hosts, chunks),
        out_shape=[jax.ShapeDtypeStruct(sizes + piece, jnp.bfloat16) for piece in pieces]
        + [
            jax.ShapeDtypeStruct((rows, halo + 1, length, chans), jnp.bfloat16),
            jax.ShapeDtypeStruct(state, jnp.float32),
            jax.ShapeDtypeStruct(feed.shape, jnp.bfloat16),
        ]
        + made,
        in_specs=anywhere(count) + vmem(6),
        out_specs=anywhere(count + 1) + vmem(2) + anywhere(len(made)),
        scratch_shapes=[
            pltpu.SemaphoreType.DMA((len(chunks), slots)),
            pltpu.SemaphoreType.DMA((len(chunks), slots)),
            pltpu.SemaphoreType.DMA((len(chunks) + 1,)),
            pltpu.VMEM(state, jnp.float32),
            pltpu.VMEM((seqs - 1,) + state, jnp.float32),
            pltpu.SemaphoreType.DMA((seqs - 1,)),
            pltpu.SemaphoreType.DMA((seqs - 1,)),
            pltpu.VMEM(feed.shape, jnp.bfloat16),
            pltpu.SemaphoreType.DMA((halo,)),
            pltpu.SemaphoreType.DMA((halo,)),
            pltpu.SemaphoreType.DMA((halo,)),
            pltpu.SemaphoreType.DMA((1,)),
            pltpu.VMEM((width // LANES, length, LANES), jnp.float32),
            pltpu.VMEM((width // LANES * EMA_STEP * 8, LANES), jnp.float32),
            *extra,
        ],
        compiler_params=pltpu.CompilerParams(collective_id=0, has_side_effects=True, vmem_limit_bytes=48 * 2**20),
        name="gather_weights",
    )(*[shard.reshape(piece) for shard, piece in zip(shards, pieces)], feed, keep, decay, gain, reach, power)
    total = depth * cores * down * across
    wholes = [whole.reshape(total * shard.shape[0], shard.shape[1]) for whole, shard in zip(results, shards)]
    return wholes, *results[count:]


def add_rows(target, total, others):
    rows = total.shape[0]
    chunk = 16 if rows % 16 == 0 else rows

    def body(index, carry):
        at = pl.ds(pl.multiple_of(index * chunk, chunk), chunk)
        result = total[at, :].astype(jnp.float32)
        for other in others:
            result = result + other[at, :].astype(jnp.float32)
        target[at, :] = result.astype(target.dtype)
        return carry

    lax.fori_loop(0, rows // chunk, body, 0)


def scatter_kernel(sizes, count, chunks, *refs):
    grads, small = refs[:count], refs[count]
    feed, grad, keep, decay, gain, start, reach, power = refs[count + 1 : count + 9]
    refs = refs[count + 9 :]
    outs, (small_out, back_out) = refs[:count], refs[count : count + 2]
    rest = refs[count + 2 :]
    rest, (
        edge, arrived, end, edge_send, edge_recv, wide, wide_grad, part, kept_states,
    ) = rest[:-9], rest[-9:]
    rows, length, chans = feed.shape
    width = wide.shape[0] * LANES
    seqs = sizes[2] * sizes[3]
    count = len(chunks)
    names = ("arrive", "own", "first_a", "first_b", "second_a", "second_b", "third")
    held = {name: rest[at * count : (at + 1) * count] for at, name in enumerate(names)}
    flat_planes, flat_pieces, small_parts, send_sem, recv_sem, own_sem, small_send, small_recv = rest[len(names) * count :]
    depth, cores, down, across = sizes
    spot = place_of()
    z, c, a, b = spot
    half = depth // 2
    front, back = pl.ds(0, half), pl.ds(half, depth - half)
    greet(sizes, spot)
    slots = {}

    def copy(w, kind, source, target, axis, by):
        slot = slots.setdefault(kind, len(slots))
        return pltpu.make_async_remote_copy(
            src_ref=source,
            dst_ref=target,
            send_sem=send_sem.at[w, slot],
            recv_sem=recv_sem.at[w, slot],
            device_id=peer_of(sizes, spot, axis, by),
            device_id_type=MESH,
        )

    def at_a(by):
        return lax.rem(a + by, down)

    def at_b(by):
        return lax.rem(b + by, across)

    twin, first, second, third = [], [], [], []
    for w in range(count):
        arrive = held["arrive"][w]
        twin.append(copy(w, "c", grads[chunks[w][0]].at[:, 1 - c, :, :, :, chunks[w][1]], arrive, 1, 1))
        first.append(
            [
                copy(w, ("a1", k), arrive.at[front, :, at_b(k)], held["first_a"][w].at[k - 1], 3, k)
                for k in range(1, across)
            ]
            + [
                copy(w, ("b1", l), arrive.at[back, at_a(l)], held["first_b"][w].at[l - 1], 2, l)
                for l in range(1, down)
            ]
        )
        second.append(
            [
                copy(w, ("a2", l), arrive.at[front, at_a(l), b], held["second_a"][w].at[l - 1], 2, l)
                for l in range(1, down)
            ]
            + [
                copy(w, ("b2", k), arrive.at[back, a, at_b(k)], held["second_b"][w].at[k - 1], 3, k)
                for k in range(1, across)
            ]
        )
        third.append(
            [
                copy(w, ("z", k), arrive.at[lax.rem(z + k, depth), a, b], held["third"][w].at[k - 1], 0, k)
                for k in range(1, depth)
            ]
        )

    stages = [(axis, 1 << bit) for axis in (1, 2, 3, 0) for bit in range(sizes[axis].bit_length() - 1)]

    def small_copy(at):
        axis, bit = stages[at]
        mine = spot[axis]
        towards = jnp.where(lax.rem(mine // bit, 2) == 0, bit, sizes[axis] - bit)
        return pltpu.make_async_remote_copy(
            src_ref=small_out,
            dst_ref=small_parts.at[at],
            send_sem=small_send.at[at],
            recv_sem=small_recv.at[at],
            device_id=peer_of(sizes, spot, axis, towards),
            device_id_type=MESH,
        )

    def own_load(w, at):
        return pltpu.make_async_copy(grads[chunks[w][0]].at[at, c, :, :, :, chunks[w][1]], held["own"][w].at[lax.rem(at, 2)], own_sem.at[w, lax.rem(at, 2)])

    def add_own(w):
        own_load(w, 0).start()

        def body(at, carry):
            @pl.when(at + 1 < depth)
            def _():
                own_load(w, at + 1).start()

            own_load(w, at).wait()
            for down_at in range(down):
                for across_at in range(across):
                    spot_ref = held["arrive"][w].at[at, down_at, across_at]
                    add_rows(spot_ref, spot_ref, [held["own"][w].at[lax.rem(at, 2), down_at, across_at]])
            return carry

        lax.fori_loop(0, depth, body, 0)

    flat = count - 1
    count = flat
    flat_arrive = held["arrive"][flat]

    def flat_copy(slot, source, target, device):
        return pltpu.make_async_remote_copy(
            src_ref=source,
            dst_ref=target,
            send_sem=send_sem.at[flat, slot],
            recv_sem=recv_sem.at[flat, slot],
            device_id=device,
            device_id_type=MESH,
        )

    flat_line = [
        flat_copy(k, flat_arrive.at[lax.rem(z + k, depth)], flat_planes.at[k - 1], peer_of(sizes, spot, 0, k))
        for k in range(1, depth)
    ]
    flat_row = []
    for by in range(1, seqs):
        to = lax.rem(a * across + b + by, seqs)
        source = flat_arrive.at[z, lax.div(to, across), lax.rem(to, across)]
        flat_row.append(flat_copy(depth - 1 + by, source, flat_pieces.at[by - 1], along(seqs, by)))

    def flat_pair():
        twin[flat].wait_recv()
        add_own(flat)
        for item in flat_line:
            item.start()

    def flat_sum():
        for item in flat_line:
            item.wait_recv()
        for down_at in range(down):
            for across_at in range(across):
                spot_ref = flat_arrive.at[z, down_at, across_at]
                add_rows(spot_ref, spot_ref, [flat_planes.at[k, down_at, across_at] for k in range(depth - 1)])
        for item in flat_row:
            item.start()

    def flat_finish():
        for item in flat_row:
            item.wait_recv()
        out = outs[chunks[flat][0]].at[:, chunks[flat][1]]
        add_rows(out, flat_arrive.at[z, a, b], [flat_pieces.at[at] for at in range(seqs - 1)])

    small_out[...] = small[...]
    edges = spread_edge(seqs, edge, arrived, edge_send, edge_recv, False)
    units = rows * (chans // width)

    def last_unit(index, carry):
        row, base = unit_of(index, width, chans)
        ema_last(True, row, base, grad, keep, decay, edge, wide)
        return carry

    def backward_unit(index, carry):
        row, base = unit_of(index, width, chans)
        ema_backward(
            row, base, feed, grad, keep, decay, gain, start, end, back_out, small_out, wide, wide_grad, part, kept_states
        )
        return carry

    for w in range(min(2, count)):
        twin[w].start()
    twin[flat].start()
    lax.fori_loop(0, units, last_unit, 0)
    for item in edges:
        item.start()
    busy = count - 1
    for step in range(max(count + 3, busy + len(stages))):
        if step < count:
            w = step
            twin[w].wait_recv()
            if w + 2 < count:
                twin[w + 2].start()
            add_own(w)
            for item in first[w]:
                item.start()
        if step == 0:
            flat_pair()
        if step == 2:
            flat_sum()
        if step == 4:
            flat_finish()
        if 1 <= step <= count:
            w = step - 1
            arrive = held["arrive"][w]
            for item in first[w]:
                item.wait_recv()
            for at in range(half):
                for l in range(down):
                    spot_ref = arrive.at[at, l, b]
                    add_rows(spot_ref, spot_ref, [held["first_a"][w].at[k, at, l] for k in range(across - 1)])
            for at in range(half, depth):
                for k in range(across):
                    spot_ref = arrive.at[at, a, k]
                    add_rows(spot_ref, spot_ref, [held["first_b"][w].at[l, at - half, k] for l in range(down - 1)])
            for item in second[w]:
                item.start()
        if 2 <= step <= count + 1:
            w = step - 2
            arrive = held["arrive"][w]
            for item in second[w]:
                item.wait_recv()
            for at in range(half):
                spot_ref = arrive.at[at, a, b]
                add_rows(spot_ref, spot_ref, [held["second_a"][w].at[l, at] for l in range(down - 1)])
            for at in range(half, depth):
                spot_ref = arrive.at[at, a, b]
                add_rows(spot_ref, spot_ref, [held["second_b"][w].at[k, at - half] for k in range(across - 1)])
            for item in third[w]:
                item.start()
        if 3 <= step <= count + 2:
            w = step - 3
            for item in third[w]:
                item.wait_recv()
            add_rows(outs[chunks[w][0]].at[:, chunks[w][1]], held["arrive"][w].at[z, a, b], [held["third"][w].at[k] for k in range(depth - 1)])
        if step == 0:
            for item in edges:
                item.wait()
            join_edges(arrived, reach, power, end)
        if step < busy:
            lax.fori_loop(*share(units, busy, step), backward_unit, 0)
        stage = step - busy
        if stage == -1:
            small_copy(0).start()
        if 0 <= stage < len(stages):
            small_copy(stage).wait()
            small_out[...] = small_out[...] + small_parts[stage]
            if stage + 1 < len(stages):
                small_copy(stage + 1).start()
    for item in [twin[flat]] + flat_line + flat_row:
        item.wait_send()
    for w in range(count):
        for item in [twin[w]] + first[w] + second[w] + third[w]:
            item.wait_send()


def scatter_grads(grads, small, feed, grad, keep, decay, gain, start, reach, power):
    sizes = shape_of()
    depth, cores, down, across = sizes
    total = depth * cores * down * across
    count = len(grads)
    half = depth // 2
    pieces = [piece_shape(g.shape[0] // total, g.shape[1]) for g in grads]
    leads = (
        (depth, down, across),
        (2, down, across),
        (across - 1, half, down),
        (down - 1, depth - half, across),
        (down - 1, half),
        (across - 1, depth - half),
        (depth - 1,),
    )
    slots = max(2 * (across - 1 + down - 1), down * across - 1) + depth
    stages = sum(size.bit_length() - 1 for size in sizes)
    chunks = chunks_of(pieces)
    parts = [(pieces[at][0], columns.size) for at, columns in chunks]
    rows, length, chans = feed.shape
    state = (rows, 16, chans)
    width = min(BACKWARD_WIDTH, chans)
    seqs = down * across
    results = pl.pallas_call(
        functools.partial(scatter_kernel, sizes, count, chunks),
        out_shape=[jax.ShapeDtypeStruct(piece, jnp.float32) for piece in pieces]
        + [
            jax.ShapeDtypeStruct(small.shape, jnp.float32),
            jax.ShapeDtypeStruct(feed.shape, jnp.bfloat16),
        ],
        in_specs=anywhere(count) + vmem(9),
        out_specs=vmem(count + 2),
        scratch_shapes=[pltpu.VMEM(lead + part, jnp.bfloat16) for lead in leads for part in parts]
        + [pltpu.VMEM((depth - 1, down, across) + parts[-1], jnp.bfloat16), pltpu.VMEM((down * across - 1,) + parts[-1], jnp.bfloat16)]
        + [
            pltpu.VMEM((stages,) + small.shape, jnp.float32),
            pltpu.SemaphoreType.DMA((len(chunks), slots)),
            pltpu.SemaphoreType.DMA((len(chunks), slots)),
            pltpu.SemaphoreType.DMA((len(chunks), 2)),
            pltpu.SemaphoreType.DMA((stages,)),
            pltpu.SemaphoreType.DMA((stages,)),
            pltpu.VMEM(state, jnp.float32),
            pltpu.VMEM((seqs - 1,) + state, jnp.float32),
            pltpu.VMEM(state, jnp.float32),
            pltpu.SemaphoreType.DMA((seqs - 1,)),
            pltpu.SemaphoreType.DMA((seqs - 1,)),
            pltpu.VMEM((width // LANES, length, LANES), jnp.float32),
            pltpu.VMEM((width // LANES, length, LANES), jnp.float32),
            pltpu.VMEM((width // LANES * EMA_STEP * 8, LANES), jnp.float32),
            pltpu.VMEM((length * 16, width), jnp.float32),
        ],
        compiler_params=pltpu.CompilerParams(collective_id=1, has_side_effects=True, vmem_limit_bytes=62 * 2**20),
        name="scatter_grads",
    )(
        *[g.reshape(sizes + piece) for g, piece in zip(grads, pieces)],
        small, feed, grad, keep, decay, gain, start, reach, power,
    )
    sums = [result.reshape(g.shape[0] // total, g.shape[1]) for result, g in zip(results[:count], grads)]
    return sums, *results[count:]


def passed_on(alive, forward):
    count = lax.axis_size("seq")
    place = lax.axis_index("seq")
    through = jnp.ones((alive.shape[0], 1, 1), jnp.float32)
    factors = []
    for away in range(1, count):
        exists = place >= away if forward else place + away < count
        factors.append(jnp.broadcast_to(jnp.where(exists, through, 0.0), (alive.shape[0], 16, LANES)))
        at = jnp.clip(place - away if forward else place + away, 0, count - 1)
        through = through * lax.dynamic_slice_in_dim(alive, at, 1, 1)[:, :, None]
    return jnp.stack(factors)


QUERY_BLOCK = 256
KEY_BLOCK = 512
VALUE_BLOCK = 1024


def attend_kernel(halo_span, query, key, value, key_docs, query_docs, out, probs):
    size, span = probs.shape
    first = pl.program_id(1) * size
    keys = pl.ds(pl.multiple_of(first, LANES), span)
    scores = against(query[0], key[0, keys, :]) * Z ** (-0.5)
    query_at = lax.broadcasted_iota(jnp.int32, (size, span), 0) + halo_span
    key_at = lax.broadcasted_iota(jnp.int32, (size, span), 1)
    allowed = (key_at <= query_at) & (key_docs[0, :, keys] == query_docs[0])
    scores = jnp.where(allowed, scores, NEG_FILL)
    expo = jnp.exp(scores - jnp.max(scores, axis=1, keepdims=True))
    probs[...] = low(expo / jnp.sum(expo, axis=1, keepdims=True))

    def body(at, carry):
        columns = pl.ds(pl.multiple_of(at * VALUE_BLOCK, VALUE_BLOCK), VALUE_BLOCK)
        out[0, :, columns] = product(probs[...], value[0, keys, columns])
        return carry

    lax.fori_loop(0, out.shape[2] // VALUE_BLOCK, body, 0)


def attend(query, key, value, docs_row, docs_column, halo):
    rows, places, _ = query.shape
    window, wide = value.shape[1:]
    size = min(QUERY_BLOCK, places)
    span = halo * places + size
    return pl.pallas_call(
        functools.partial(attend_kernel, halo * places),
        out_shape=jax.ShapeDtypeStruct((rows, places, wide), jnp.float32),
        grid=(rows, places // size),
        in_specs=[
            pl.BlockSpec((1, size, Z), lambda r, i: (r, i, 0)),
            pl.BlockSpec((1, window, Z), lambda r, i: (r, 0, 0)),
            pl.BlockSpec((1, window, wide), lambda r, i: (r, 0, 0)),
            pl.BlockSpec((1, 1, window), lambda r, i: (r, 0, 0)),
            pl.BlockSpec((1, size, 1), lambda r, i: (r, i, 0)),
        ],
        out_specs=pl.BlockSpec((1, size, wide), lambda r, i: (r, i, 0)),
        scratch_shapes=[pltpu.VMEM((size, span), jnp.bfloat16)],
        compiler_params=pltpu.CompilerParams(vmem_limit_bytes=40 * 2**20),
        cost_estimate=pl.CostEstimate(
            flops=2 * rows * places * span * (wide + Z),
            bytes_accessed=rows * (window * wide * 2 + places * wide * 4),
            transcendentals=rows * places * span,
        ),
        name="attend",
    )(query, key, value, docs_row, docs_column[:, halo * places :])


def attend_back_kernel(
    halo_span, query, key, value, slope, pulled, key_docs, query_docs, d_query, d_key, d_value, chances, pulls, balance
):
    window, places = chances.shape
    step = d_value.shape[1]
    chunk = pl.program_id(1)

    @pl.when(chunk == 0)
    def _():
        peak = jnp.full((1, places), NEG_FILL, jnp.float32)

        def score(at, peak):
            keys = pl.ds(pl.multiple_of(at * step, step), step)
            scores = against(key[0, keys, :], query[0]) * Z ** (-0.5)
            key_at = lax.broadcasted_iota(jnp.int32, (step, places), 0) + at * step
            query_at = lax.broadcasted_iota(jnp.int32, (step, places), 1) + halo_span
            allowed = (key_at <= query_at) & (key_docs[0, keys, :] == query_docs[0])
            scores = jnp.where(allowed, scores, NEG_FILL)
            chances[keys, :] = scores
            return jnp.maximum(peak, jnp.max(scores, axis=0, keepdims=True))

        peak = lax.fori_loop(0, window // step, score, peak)

        def weigh(at, total):
            keys = pl.ds(pl.multiple_of(at * step, step), step)
            expo = jnp.exp(chances[keys, :] - peak)
            chances[keys, :] = expo
            return total + jnp.sum(expo, axis=0, keepdims=True)

        total = lax.fori_loop(0, window // step, weigh, jnp.zeros((1, places), jnp.float32))

        def pull(at, held):
            keys = pl.ds(pl.multiple_of(at * step, step), step)
            probs = chances[keys, :] / total
            chances[keys, :] = probs
            local = against(value[0, keys, :], pulled[0])
            pulls[keys, :] = local
            return held + jnp.sum(probs * local, axis=0, keepdims=True)

        balance[...] = lax.fori_loop(0, window // step, pull, jnp.zeros((1, places), jnp.float32))
        d_query[...] = jnp.zeros_like(d_query)

    keys = pl.ds(pl.multiple_of(chunk * step, step), step)
    probs = chances[keys, :]
    d_scores = low(probs * (pulls[keys, :] - balance[...]))
    d_key[0] = product(d_scores, query[0]) * Z ** (-0.5)
    d_query[0] = d_query[0] + transposed(d_scores, key[0, keys, :]) * Z ** (-0.5)
    probs_low = low(probs)

    def body(at, carry):
        columns = pl.ds(pl.multiple_of(at * VALUE_BLOCK, VALUE_BLOCK), VALUE_BLOCK)
        local = product(probs_low, pulled[0, :, columns])
        d_value[0, :, columns] = low(local * slope[0, :, columns].astype(jnp.float32))
        return carry

    lax.fori_loop(0, d_value.shape[2] // VALUE_BLOCK, body, 0)


def attend_back(query, key, value, slope, pulled, docs_row, docs_column, halo):
    rows, places, _ = query.shape
    window, wide = value.shape[1:]
    step = min(KEY_BLOCK, places)
    return pl.pallas_call(
        functools.partial(attend_back_kernel, halo * places),
        out_shape=[
            jax.ShapeDtypeStruct((rows, places, Z), jnp.float32),
            jax.ShapeDtypeStruct((rows, window, Z), jnp.float32),
            jax.ShapeDtypeStruct((rows, window, wide), jnp.bfloat16),
        ],
        grid=(rows, window // step),
        in_specs=[
            pl.BlockSpec((1, places, Z), lambda r, i: (r, 0, 0)),
            pl.BlockSpec((1, window, Z), lambda r, i: (r, 0, 0)),
            pl.BlockSpec((1, window, wide), lambda r, i: (r, 0, 0)),
            pl.BlockSpec((1, step, wide), lambda r, i: (r, i, 0)),
            pl.BlockSpec((1, places, wide), lambda r, i: (r, 0, 0)),
            pl.BlockSpec((1, window, 1), lambda r, i: (r, 0, 0)),
            pl.BlockSpec((1, 1, places), lambda r, i: (r, 0, 0)),
        ],
        out_specs=[
            pl.BlockSpec((1, places, Z), lambda r, i: (r, 0, 0)),
            pl.BlockSpec((1, step, Z), lambda r, i: (r, i, 0)),
            pl.BlockSpec((1, step, wide), lambda r, i: (r, i, 0)),
        ],
        scratch_shapes=[
            pltpu.VMEM((window, places), jnp.float32),
            pltpu.VMEM((window, places), jnp.float32),
            pltpu.VMEM((1, places), jnp.float32),
        ],
        compiler_params=pltpu.CompilerParams(vmem_limit_bytes=48 * 2**20),
        cost_estimate=pl.CostEstimate(
            flops=4 * rows * places * window * (wide + Z),
            bytes_accessed=rows * (window * wide * 6 + places * wide * 2),
            transcendentals=rows * places * window,
        ),
        name="attend_back",
    )(query, key, value, slope, pulled, docs_column, docs_row[:, :, halo * places :])


def on_device(
    layer_input,
    cotangent,
    doc_ids,
    resets,
    mix_weight,
    value_weight,
    head_weight,
    expand_weight,
    shrink_weight,
    chan_vectors,
    ema_logits,
    ema_beta_eta,
    z_affine,
):
    seq_count = lax.axis_size("seq")
    seq_place = lax.axis_index("seq")
    rows, places, width = layer_input.shape
    tokens = rows * places
    halo = min(-(-(REACH - 1) // places), seq_count - 1)
    window = (halo + 1) * places

    inputs32 = layer_input.astype(jnp.float32)
    center = inputs32 - jnp.mean(inputs32, axis=-1, keepdims=True)
    unit = lax.rsqrt(jnp.mean(center * center, axis=-1, keepdims=True) + 1e-05)
    plain = center * unit
    normed = plain * chan_vectors[0]
    normed_low = low(normed)

    rate = jax.nn.sigmoid(ema_logits[0])
    damping = jax.nn.sigmoid(ema_logits[1])
    decay = (1.0 - rate * damping).T
    weight_in = rate * ema_beta_eta[0]
    weight_out = ema_beta_eta[1]
    gain = (weight_in * weight_out).T
    decay_all = decay
    reach = 1
    while reach < places:
        decay_all = decay_all * decay_all
        reach *= 2
    powers = [jnp.ones_like(decay)]
    while len(powers) < seq_count - 1:
        powers.append(powers[-1] * decay_all)
    power = jnp.stack(powers)
    keep_row = 1.0 - resets.astype(jnp.float32)
    keep_own = lax.dynamic_slice_in_dim(keep_row, seq_place * places, places, 1)
    keep = jnp.broadcast_to(keep_own[:, None, :, None], (rows, 1, places, LANES)).reshape(rows, places, LANES)
    alive = jnp.min(keep_row.reshape(rows, seq_count, places), axis=2)

    (value_full, mix_full, expand_full, head_full), normed_window, start, ema_low, *made = gather_weights(
        (value_weight, mix_weight, expand_weight, head_weight),
        normed_low,
        keep,
        decay,
        gain,
        passed_on(alive, True),
        power,
        halo,
    )
    normed_window = normed_window.reshape(rows * window, width)
    value_full, mix_full, head_full, expand_full, shrink_late = lax.optimization_barrier(
        (value_full, mix_full, head_full, expand_full, shrink_weight)
    )
    shrink_full = lax.all_gather(shrink_late, BOTH, axis=0, tiled=True)

    premix = (ema_low.astype(jnp.float32) + chan_vectors[2] * normed).reshape(tokens, width)
    mixed_low = low(jax.nn.silu(premix))
    if made:
        values_low, value_slope = (item.reshape(rows, window, V) for item in made)
    else:
        value_pre = product(normed_window, value_full)
        values_low = low(jax.nn.silu(value_pre)).reshape(rows, window, V)
        value_slope = low(silu_slope(value_pre)).reshape(rows, window, V)
    shared_pre = product(mixed_low, mix_full[:, :Z])
    shared = jax.nn.silu(shared_pre)
    queries_low = low(shared * z_affine[0] + z_affine[1]).reshape(rows, places, Z)
    keys_low = low(shared * z_affine[2]).reshape(rows, places, Z)
    keys_low, mixed_low = lax.optimization_barrier((keys_low, mixed_low))
    key_window = jnp.concatenate([shift_seq(keys_low, by) for by in range(halo, 0, -1)] + [keys_low], axis=1)
    projected = product(mixed_low, mix_full)
    reset_pre = projected[:, Z : Z + V]
    head_base = projected[:, Z + V : Z + V + width]
    update_pre = projected[:, Z + V + width :]
    reset_gate = jax.nn.silu(reset_pre)
    update_gate = jax.nn.sigmoid(update_pre)

    padded_docs = jnp.pad(doc_ids, ((0, 0), (halo * places, 0)), constant_values=-1)
    key_docs = lax.dynamic_slice_in_dim(padded_docs, seq_place * places, window, 1)
    docs_row, docs_column = key_docs[:, None, :], key_docs[:, :, None]
    attended = attend(queries_low, key_window, values_low, docs_row, docs_column, halo).reshape(tokens, V)
    gated_low = low(reset_gate * attended)
    head_pre = head_base + product(gated_low, head_full)
    candidate = jax.nn.silu(head_pre)
    residual_in = inputs32.reshape(tokens, width)
    first = residual_in + update_gate * (candidate - residual_in)
    second, second_pull = jax.vjp(scaled_norm, first, chan_vectors[1])
    second_low = low(second)
    expand_pre = product(second_low, expand_full)
    expand_slope = silu_slope(expand_pre)
    hidden_low, expand_slope = lax.optimization_barrier((low(jax.nn.silu(expand_pre)), expand_slope))
    output = low(first + product(hidden_low, shrink_full)).reshape(rows, places, width)

    cot_low = cotangent.reshape(tokens, width)
    shrink_part = low(transposed(hidden_low, cot_low))
    d_expand = low(against(cot_low, shrink_full) * expand_slope)
    d_first_norm, d_gain_two = second_pull(against(d_expand, expand_full))
    d_first = cot_low.astype(jnp.float32) + d_first_norm
    d_update = d_first * (candidate - residual_in) * update_gate * (1.0 - update_gate)
    d_direct = d_first * (1.0 - update_gate)
    d_head = d_first * update_gate * silu_slope(head_pre)
    d_head_low = low(d_head)
    d_gated = against(d_head_low, head_full)
    d_reset = d_gated * attended * silu_slope(reset_pre)
    d_attended = low(d_gated * reset_gate).reshape(rows, places, V)
    d_queries, key_term, d_value_pre = attend_back(
        queries_low, key_window, values_low, value_slope, d_attended, docs_row, docs_column, halo
    )
    d_value_pre, second_late, gated_late = lax.optimization_barrier((d_value_pre, second_low, gated_low))
    expand_part = low(transposed(second_late, d_expand))
    head_part = low(transposed(gated_late, d_head_low))
    d_value_pre = d_value_pre.reshape(rows * window, V)
    d_keys = key_term[:, halo * places :]
    for by in range(1, halo + 1):
        begin = (halo - by) * places
        d_keys = d_keys + shift_seq(low(key_term[:, begin : begin + places]), -by).astype(jnp.float32)
    d_keys32 = low(d_keys).astype(jnp.float32).reshape(tokens, Z)
    value_part = low(transposed(normed_window, d_value_pre))
    value_term = against(d_value_pre, value_full).reshape(rows, halo + 1, places, width)
    terms = low(value_term[:, :halo])
    d_normed_value = value_term[:, halo]
    for by in range(1, halo + 1):
        d_normed_value = d_normed_value + shift_seq(terms[:, halo - by], -by).astype(jnp.float32)
    d_query_flat = d_queries.reshape(tokens, Z)
    d_shared = d_query_flat * z_affine[0] + d_keys32 * z_affine[2]
    affine_part = jnp.stack(
        [
            jnp.sum(d_query_flat * shared, axis=0),
            jnp.sum(d_query_flat, axis=0),
            jnp.sum(d_keys32 * shared, axis=0),
        ]
    )
    d_projected = low(
        jnp.concatenate([d_shared * silu_slope(shared_pre), d_reset, d_head, d_update], axis=1)
    )
    mix_part = low(transposed(mixed_low, d_projected))
    d_premix = against(d_projected, mix_full) * silu_slope(premix)
    omega_part = jnp.sum(d_premix * normed.reshape(tokens, width), axis=0)
    d_premix = d_premix.reshape(rows, places, width)
    d_ema = low(d_premix)
    known = d_premix * chan_vectors[2] + d_normed_value
    d_gain_one = jnp.sum(known * plain, axis=(0, 1))
    small_part = jnp.concatenate(
        [
            jnp.zeros((32, width), jnp.float32),
            jnp.stack([d_gain_one, d_gain_two, omega_part]),
            jnp.pad(affine_part.reshape(1, 3 * Z), ((0, 4), (0, width - 3 * Z))),
        ],
        axis=0,
    )
    (shrink_grad, expand_grad, value_grad, mix_grad, head_grad), small_sum, d_feed = scatter_grads(
        (shrink_part, expand_part, value_part, mix_part, head_part),
        small_part,
        normed_low,
        d_ema,
        keep,
        decay,
        gain,
        start,
        passed_on(alive, False),
        power,
    )
    d_normed = known + d_feed.astype(jnp.float32)
    pulled = d_normed * chan_vectors[0]
    pulled = pulled - jnp.mean(pulled, axis=-1, keepdims=True) - plain * jnp.mean(pulled * plain, axis=-1, keepdims=True)
    x_grad = d_direct.reshape(rows, places, width) + pulled * unit
    gain_sum = small_sum[:16]
    decay_sum = small_sum[16:32]
    chan_grad = small_sum[32:35].at[0].add(jnp.sum(gain * gain_sum, axis=0) / chan_vectors[0])
    affine_grad = small_sum[35, : 3 * Z].reshape(3, Z)
    d_gain = gain_sum.T
    d_decay = (decay_sum * gain).T
    d_weight_in = d_gain * weight_out
    coef_grad = jnp.stack([d_weight_in * rate, d_gain * weight_in])
    d_rate = d_weight_in * ema_beta_eta[0] - d_decay * damping
    d_damping = -d_decay * rate
    logits_grad = jnp.stack([d_rate * rate * (1.0 - rate), d_damping * damping * (1.0 - damping)])
    return (
        output,
        x_grad,
        mix_grad,
        value_grad,
        head_grad,
        expand_grad,
        shrink_grad,
        chan_grad,
        logits_grad,
        coef_grad,
        affine_grad,
    )


def solution(mesh):
    placed = (
        P("dp", "seq", None),
        P("dp", "seq", None),
        P("dp", None),
        P("dp", None),
        P(BOTH, None),
        P(BOTH, None),
        P(BOTH, None),
        P(BOTH, None),
        P(BOTH, None),
        P(),
        P(),
        P(),
        P(),
    )
    return jax.shard_map(
        on_device,
        mesh=mesh,
        in_specs=placed,
        out_specs=(
            P("dp", "seq", None),
            P("dp", "seq", None),
            P(BOTH, None),
            P(BOTH, None),
            P(BOTH, None),
            P(BOTH, None),
            P(BOTH, None),
            P(),
            P(),
            P(),
            P(),
        ),
        check_vma=False,
    )
```

```python
import functools
import jax
import jax.numpy as jnp
from jax import lax
from jax.experimental import pallas as pl
from jax.experimental.pallas import tpu as pltpu
from jax.sharding import PartitionSpec as P

Z = 128
V = 2048
REACH = 1024
NEG_FILL = -1000000000.0
BOTH = ("dp", "seq")
MESH = pl.DeviceIdType.MESH
LANES = 128
EMA_STEP = 16
FORWARD_WIDTH = 512
BACKWARD_WIDTH = 256
HOST_TILE = 512
PROJECT_TILE = 384


def lanes_at(base, group):
    return pl.ds(pl.multiple_of(base + group * LANES, LANES), LANES)


def row_of(ref, step, group):
    return ref[group, pl.ds(step, 8, stride=0), :]


def widen(source, row, base, wide):
    for group in range(wide.shape[0]):
        wide[group] = source[row, :, lanes_at(base, group)].astype(jnp.float32)


def halves_of(ref, base, groups, row=None):
    spots = [(slice(h * 8, h * 8 + 8), lanes_at(base, g)) for g in range(groups) for h in range(2)]
    return [ref[spot] if row is None else ref[(row,) + spot] for spot in spots]


def put_halves(ref, base, values, row):
    for at, value in enumerate(values):
        g, h = divmod(at, 2)
        ref[row, h * 8 : h * 8 + 8, lanes_at(base, g)] = value


def add_halves(ref, first, base, values):
    for at, value in enumerate(values):
        g, h = divmod(at, 2)
        spot = (slice(first + h * 8, first + h * 8 + 8), lanes_at(base, g))
        ref[spot] = ref[spot] + value


def fold_rows(part, group):
    halves = []
    for half in range(EMA_STEP // 8):
        base = group * EMA_STEP * 8 + half * 64
        total = part[pl.ds(base, 8, stride=8), :]
        for sub in range(1, 8):
            total = total + part[pl.ds(base + sub, 8, stride=8), :]
        halves.append(total)
    return jnp.concatenate(halves, axis=0).astype(jnp.bfloat16)


def unit_of(index, width, chans):
    across = chans // width
    return lax.div(index, across), pl.multiple_of(lax.rem(index, across) * width, width)


def ema_last(reverse, row, base, feed, keep, decay, last, wide):
    length, groups = feed.shape[1], wide.shape[0]
    widen(feed, row, base, wide)
    decays = halves_of(decay, base, groups)

    def body(index, states):
        states = list(states)
        block = (length // EMA_STEP - 1 - index) if reverse else index
        first = pl.multiple_of(block * EMA_STEP, EMA_STEP)
        for offset in range(EMA_STEP):
            step = first + (EMA_STEP - 1 - offset if reverse else offset)
            kept = row_of(keep, step, row)
            for at in range(2 * groups):
                fed = row_of(wide, step, at // 2)
                if reverse:
                    states[at] = (kept * decays[at]) * (states[at] + fed)
                else:
                    states[at] = (kept * decays[at]) * states[at] + fed
        return tuple(states)

    zero = jnp.zeros((8, LANES), jnp.float32)
    put_halves(last, base, lax.fori_loop(0, length // EMA_STEP, body, (zero,) * (2 * groups)), row)


def ema_forward(row, base, feed, keep, decay, gain, start, out, wide, part):
    length, groups = feed.shape[1], wide.shape[0]
    widen(feed, row, base, wide)
    decays, gains = halves_of(decay, base, groups), halves_of(gain, base, groups)

    def body(index, states):
        states = list(states)
        first = pl.multiple_of(index * EMA_STEP, EMA_STEP)
        for offset in range(EMA_STEP):
            kept = row_of(keep, first + offset, row)
            for g in range(groups):
                fed = row_of(wide, first + offset, g)
                both = []
                for at in (2 * g, 2 * g + 1):
                    states[at] = (kept * decays[at]) * states[at] + fed
                    both.append(gains[at] * states[at])
                spot = g * EMA_STEP * 8 + offset * 8
                part[spot : spot + 8, :] = both[0] + both[1]
        for g in range(groups):
            out[row, pl.ds(first, EMA_STEP), lanes_at(base, g)] = fold_rows(part, g)
        return tuple(states)

    lax.fori_loop(0, length // EMA_STEP, body, tuple(halves_of(start, base, groups, row)))


def ema_backward(row, base, feed, grad, keep, decay, gain, start, end, back, sums, wide, wide_grad, part, held):
    length, groups = feed.shape[1], wide.shape[0]
    widen(feed, row, base, wide)
    widen(grad, row, base, wide_grad)
    decays, gains = halves_of(decay, base, groups), halves_of(gain, base, groups)
    blocks = length // EMA_STEP

    def forward(index, states):
        states = list(states)
        first = pl.multiple_of(index * EMA_STEP, EMA_STEP)
        for offset in range(EMA_STEP):
            kept = row_of(keep, first + offset, row)
            for at in range(2 * groups):
                g, h = divmod(at, 2)
                held[pl.ds((first + offset) * 16 + h * 8, 8), g * LANES : (g + 1) * LANES] = kept * states[at]
                states[at] = (kept * decays[at]) * states[at] + row_of(wide, first + offset, g)
        return tuple(states)

    lax.fori_loop(0, blocks, forward, tuple(halves_of(start, base, groups, row)))

    def backward(index, carried):
        pulls, gain_sums, decay_sums = (list(c) for c in carried)
        first = pl.multiple_of((blocks - 1 - index) * EMA_STEP, EMA_STEP)
        for offset in reversed(range(EMA_STEP)):
            step = first + offset
            kept = row_of(keep, step, row)
            for g in range(groups):
                pulled, fed = row_of(wide_grad, step, g), row_of(wide, step, g)
                both = []
                for h in range(2):
                    at = 2 * g + h
                    local = pulls[at] + pulled
                    both.append(gains[at] * local)
                    gain_sums[at] = gain_sums[at] + local * fed
                    before = held[pl.ds(step * 16 + h * 8, 8), g * LANES : (g + 1) * LANES]
                    decay_sums[at] = decay_sums[at] + local * before
                    pulls[at] = (kept * decays[at]) * local
                spot = g * EMA_STEP * 8 + offset * 8
                part[spot : spot + 8, :] = both[0] + both[1]
        for g in range(groups):
            back[row, pl.ds(first, EMA_STEP), lanes_at(base, g)] = fold_rows(part, g)
        return (tuple(pulls), tuple(gain_sums), tuple(decay_sums))

    zeros = (jnp.zeros((8, LANES), jnp.float32),) * (2 * groups)
    _, gain_sums, decay_sums = lax.fori_loop(
        0, blocks, backward, (tuple(halves_of(end, base, groups, row)), zeros, zeros)
    )
    add_halves(sums, 0, base, gain_sums)
    add_halves(sums, 16, base, decay_sums)


def layer_norm(values):
    center = values - jnp.mean(values, axis=-1, keepdims=True)
    spread = jnp.mean(center * center, axis=-1, keepdims=True)
    return center * lax.rsqrt(spread + 1e-05)


def scaled_norm(values, gain):
    return layer_norm(values) * gain


def silu_slope(values):
    squash = jax.nn.sigmoid(values)
    return squash * (1.0 + values * (1.0 - squash))


def product(left, right):
    return jnp.dot(left, right, preferred_element_type=jnp.float32)


def against(left, right):
    return lax.dot_general(left, right, (((1,), (1,)), ((), ())), preferred_element_type=jnp.float32)


def transposed(left, right):
    return lax.dot_general(left, right, (((0,), (0,)), ((), ())), preferred_element_type=jnp.float32)


def low(values):
    return values.astype(jnp.bfloat16)


def shift_seq(values, by):
    count = lax.axis_size("seq")
    pairs = [(i, i + by) for i in range(count) if 0 <= i + by < count]
    return lax.ppermute(values, "seq", pairs)


def side_of(count):
    side = 1
    while side * side < count:
        side *= 2
    return side


def shape_of():
    depth = lax.axis_size("dp") // 2
    seqs = lax.axis_size("seq")
    down = side_of(seqs)
    return depth, 2, down, seqs // down


def place_of():
    depth, cores, down, across = shape_of()
    dp, seq = lax.axis_index("dp"), lax.axis_index("seq")
    return lax.div(dp, cores), lax.rem(dp, cores), lax.div(seq, across), lax.rem(seq, across)


def peer_of(sizes, spot, axis, by):
    spot = list(spot)
    spot[axis] = lax.rem(spot[axis] + by, sizes[axis])
    return {"dp": spot[0] * sizes[1] + spot[1], "seq": spot[2] * sizes[3] + spot[3]}


def along(count, by):
    return {"dp": lax.axis_index("dp"), "seq": lax.rem(lax.axis_index("seq") + by, count)}


def greet(sizes, spot):
    barrier = pltpu.get_barrier_semaphore()
    seqs = sizes[2] * sizes[3]
    peers = [peer_of(sizes, spot, axis, by) for axis in (0, 1) for by in range(1, sizes[axis])]
    peers += [along(seqs, by) for by in range(1, seqs)]
    for peer in peers:
        pl.semaphore_signal(barrier, inc=1, device_id=peer, device_id_type=MESH)
    pl.semaphore_wait(barrier, len(peers))


def piece_shape(rows, columns):
    return (rows, columns) if rows % 16 == 0 else (rows * columns // LANES, LANES)


def chunks_of(pieces):
    chunks = []
    for at, (rows, columns) in enumerate(pieces):
        if rows * columns >= 2**17:
            half = columns // (2 * LANES) * LANES
            chunks += [(at, pl.ds(0, half)), (at, pl.ds(half, columns - half))]
        else:
            chunks.append((at, pl.ds(0, columns)))
    return chunks


def share(total, parts, at):
    return total * at // parts, total * (at + 1) // parts


def spread_edge(seqs, edge, arrived, send, recv, forward):
    return [
        pltpu.make_async_remote_copy(
            src_ref=edge,
            dst_ref=arrived.at[by - 1],
            send_sem=send.at[by - 1],
            recv_sem=recv.at[by - 1],
            device_id=along(seqs, by if forward else seqs - by),
            device_id_type=MESH,
        )
        for by in range(1, seqs)
    ]


def join_edges(arrived, reach, power, entry):
    rows, _, chans = entry.shape

    def body(row, carry):
        for group in range(chans // LANES):
            spot = slice(group * LANES, (group + 1) * LANES)
            total = None
            for at in range(arrived.shape[0]):
                term = reach[at, row] * power[at, :, spot] * arrived[at, row, :, spot]
                total = term if total is None else total + term
            entry[row, :, spot] = total
        return carry

    lax.fori_loop(0, rows, body, 0)


class Halo:
    def __init__(self, count, seqs, feed, window, zero, send, recv, local, hand_send):
        place = lax.axis_index("seq")
        relay = seqs == 4 and count == 2
        self.items = []

        def copy(source, by, towards, sent):
            return pltpu.make_async_remote_copy(
                src_ref=source,
                dst_ref=window.at[:, count - by],
                send_sem=sent,
                recv_sem=recv.at[by - 1],
                device_id=along(seqs, towards),
                device_id_type=MESH,
            )

        for by in range(1, count + 1):
            gives = place + by < seqs
            if relay and by == 1:
                gives = jnp.logical_and(gives, place != 1)
            blank = pltpu.make_async_copy(zero, window.at[:, count - by], local.at[by - 1])
            self.items.append((gives, place >= by, copy(feed, by, by, send.at[by - 1]), blank))
        self.hands = (place == 3, copy(window.at[:, 0], 1, 3, hand_send.at[0])) if relay else None

    def start(self):
        for gives, takes, remote, blank in self.items:
            pl.when(gives)(remote.start)
            pl.when(jnp.logical_not(takes))(blank.start)

    def hand_on(self):
        if self.hands:
            at_hand, hand = self.hands

            @pl.when(at_hand)
            def _():
                self.items[1][2].wait_recv()
                hand.start()

    def wait(self):
        for at, (gives, takes, remote, blank) in enumerate(self.items):
            waits = takes
            if self.hands and at == 1:
                waits = jnp.logical_and(takes, jnp.logical_not(self.hands[0]))
            pl.when(waits)(remote.wait_recv)
            pl.when(jnp.logical_not(takes))(blank.wait)
            pl.when(gives)(remote.wait_send)
        if self.hands:
            pl.when(self.hands[0])(self.hands[1].wait_send)


def gather_kernel(sizes, count, halo, hosts, chunks, *refs):
    hosts_in = refs[count + 6 : count + 8] if hosts else ()
    refs = refs[: count + 6] + refs[count + 6 + len(hosts_in) :]
    shards, (feed, keep, decay, gain, reach, power) = refs[:count], refs[count : count + 6]
    wholes, (window, entry, out) = refs[count + 6 : 2 * count + 6], refs[2 * count + 6 : 2 * count + 9]
    if hosts:
        skip, key_gain = hosts_in
        values, slopes, mixed_out, projected, key_window = refs[2 * count + 9 : 2 * count + 14]
        weight, block_in, value_tile, slope_tile, weight_sem, in_sem, out_sem = refs[-7:]
        (
            mix_full, mix_sem, skip_in, skip_sem, mixed, project_tile, project_sem, keys, keys_sem, mixed_sem,
            key_send, key_recv, key_local, key_hand,
        ) = refs[-21:-7]
        refs = refs[: 2 * count + 9] + refs[2 * count + 14 : -21]
    (
        send_sem, recv_sem, local_sem, edge, arrived, edge_send, edge_recv,
        zero, halo_send, halo_recv, halo_local, hand_send, wide_feed, part,
    ) = refs[2 * count + 9 :]
    rows, length, chans = feed.shape
    width = wide_feed.shape[0] * LANES
    seqs = sizes[2] * sizes[3]
    depth, cores, down, across = sizes
    spot = place_of()
    z, c, a, b = spot
    half = depth // 2
    greet(sizes, spot)
    slots = {}

    def copy(w, kind, source, target, axis, by):
        slot = slots.setdefault(kind, len(slots))
        return pltpu.make_async_remote_copy(
            src_ref=source,
            dst_ref=target,
            send_sem=send_sem.at[w, slot],
            recv_sem=recv_sem.at[w, slot],
            device_id=peer_of(sizes, spot, axis, by),
            device_id_type=MESH,
        )

    def block(w, a_by=0, b_by=0, part=None):
        at = pl.ds(0, depth) if part is None else part
        whole, columns = chunks[w]
        beside = lax.rem(a - a_by + down, down), lax.rem(b - b_by + across, across)
        return wholes[whole].at[at, c, *beside, :, columns]

    front, back = pl.ds(0, half), pl.ds(half, depth - half)
    local, line, wide, tall, cross, twin = [], [], [], [], [], []
    flat, count = len(chunks) - 1, len(chunks) - 1
    for w, (whole, columns) in enumerate(chunks[:count]):
        own = wholes[whole].at[z, c, a, b, :, columns]
        shard = shards[whole].at[:, columns]
        local.append(pltpu.make_async_copy(shard, own, local_sem.at[w]))
        line.append([copy(w, ("z", k), shard, own, 0, k) for k in range(1, depth)])
        wide.append([copy(w, ("x", k), block(w), block(w), 3, k) for k in range(1, across)])
        tall.append([copy(w, ("y", l), block(w), block(w), 2, l) for l in range(1, down)])
        pairs = [(k, l) for k in range(1, across) for l in range(1, down)]
        cross.append(
            {
                (k, l): (
                    copy(w, ("f", k, l), block(w, 0, k, front), block(w, 0, k, front), 2, l),
                    copy(w, ("g", k, l), block(w, l, 0, back), block(w, l, 0, back), 3, k),
                )
                for k, l in pairs
            }
        )
        twin.append(
            {
                (l, k): copy(w, ("c", l, k), block(w, l, k), block(w, l, k), 1, 1)
                for l in range(down)
                for k in range(across)
            }
        )
    whole, columns = chunks[flat]

    def plane(back_by=0):
        return wholes[whole].at[lax.rem(z - back_by + depth, depth), c, :, :, :, columns]

    def flat_copy(slot, source, target, device):
        return pltpu.make_async_remote_copy(
            src_ref=source,
            dst_ref=target,
            send_sem=send_sem.at[flat, slot],
            recv_sem=recv_sem.at[flat, slot],
            device_id=device,
            device_id_type=MESH,
        )

    flat_shard, flat_own = shards[whole].at[:, columns], wholes[whole].at[z, c, a, b, :, columns]
    flat_local = pltpu.make_async_copy(flat_shard, flat_own, local_sem.at[flat])
    flat_row = [flat_copy(by - 1, flat_shard, flat_own, along(seqs, by)) for by in range(1, seqs)]
    flat_line = [
        flat_copy(seqs - 2 + k, plane(), plane(), peer_of(sizes, spot, 0, k)) for k in range(1, depth)
    ]
    flat_twin = [
        flat_copy(seqs + depth - 2 + k, plane(k), plane(k), peer_of(sizes, spot, 1, 1)) for k in range(depth)
    ]
    zero[...] = jnp.zeros_like(zero)
    around = Halo(halo, seqs, feed, window, zero, halo_send, halo_recv, halo_local, hand_send)
    own = pltpu.make_async_copy(feed, window.at[:, halo], local_sem.at[count + 1])
    edges = spread_edge(seqs, edge, arrived, edge_send, edge_recv, True)
    for w in range(count):
        local[w].start()
    for item in line[0]:
        item.start()
    own.start()
    around.start()
    flat_local.start()
    for item in flat_row:
        item.start()
    for w in range(1, min(2, count)):
        for item in line[w]:
            item.start()
    units = rows * (chans // width)

    def last_unit(index, carry):
        row, base = unit_of(index, width, chans)
        ema_last(False, row, base, feed, keep, decay, edge, wide_feed)
        return carry

    def forward_unit(index, carry):
        row, base = unit_of(index, width, chans)
        ema_forward(row, base, feed, keep, decay, gain, entry, out, wide_feed, part)
        return carry

    def block_place(index):
        return lax.rem(index, rows), halo - lax.div(index, rows)

    def load_block(index):
        slot = lax.rem(index, 2)
        return pltpu.make_async_copy(window.at[block_place(index)], block_in.at[slot], in_sem.at[slot])

    def store_tiles(index):
        slot = lax.rem(index, 2)
        row, back_by = block_place(lax.div(index, tiles))
        columns = pl.ds(pl.multiple_of(lax.rem(index, tiles) * HOST_TILE, HOST_TILE), HOST_TILE)
        return [
            pltpu.make_async_copy(tile.at[slot], whole.at[row, back_by, :, columns], out_sem.at[at, slot])
            for at, (tile, whole) in enumerate(((value_tile, values), (slope_tile, slopes)))
        ]

    blocks = rows * (halo + 1)
    tiles = wholes[0].shape[-1] // HOST_TILE

    def value_unit(index, carry):
        block, slot = lax.div(index, tiles), lax.rem(index, 2)

        @pl.when(lax.rem(index, tiles) == 0)
        def _():
            load_block(block).wait()

            @pl.when(block + 1 < blocks)
            def _():
                load_block(block + 1).start()

        columns = pl.ds(pl.multiple_of(lax.rem(index, tiles) * HOST_TILE, HOST_TILE), HOST_TILE)
        part_weight = weight[:, :, :, :, :, columns].reshape(chans, HOST_TILE)
        before = product(block_in[lax.rem(block, 2)], part_weight)
        squash = jax.nn.sigmoid(before)

        @pl.when(index >= 2)
        def _():
            for item in store_tiles(index - 2):
                item.wait()

        value_tile[slot] = low(before * squash)
        slope_tile[slot] = low(squash * (1.0 + before * (1.0 - squash)))
        for item in store_tiles(index):
            item.start()
        return carry

    if hosts:
        near = Halo(
            halo, seqs, keys, key_window, zero.at[:, :, pl.ds(0, Z)], key_send, key_recv, key_local, key_hand
        )
        key_own = pltpu.make_async_copy(keys, key_window.at[:, halo], keys_sem.at[0])
        project_units = rows * (wholes[1].shape[-1] // PROJECT_TILE)
        mixed_copy = pltpu.make_async_copy(mixed, mixed_out, mixed_sem.at[0])

    def mix_row(row, carry):
        load = pltpu.make_async_copy(skip.at[row], skip_in, skip_sem.at[0])
        load.start()
        load.wait()
        before = out[row].astype(jnp.float32) + skip_in[...]
        mixed[row] = low(jax.nn.silu(before))
        return carry

    def store_project(index):
        slot = lax.rem(index, 2)
        columns = pl.ds(pl.multiple_of(lax.div(index, rows) * PROJECT_TILE, LANES), PROJECT_TILE)
        return pltpu.make_async_copy(
            project_tile.at[slot], projected.at[lax.rem(index, rows), :, columns], project_sem.at[slot]
        )

    def project_unit(index, carry):
        row, slot = lax.rem(index, rows), lax.rem(index, 2)
        columns = pl.ds(pl.multiple_of(lax.div(index, rows) * PROJECT_TILE, LANES), PROJECT_TILE)
        part_weight = mix_full[:, :, :, :, :, columns].reshape(chans, PROJECT_TILE)
        result = product(mixed[row], part_weight)

        @pl.when(index < rows)
        def _():
            keys[row] = low(jax.nn.silu(result[:, :Z]) * key_gain[...])

        @pl.when(index >= 2)
        def _():
            store_project(index - 2).wait()

        project_tile[slot] = result
        store_project(index).start()
        return carry

    lax.fori_loop(0, units, last_unit, 0)
    for item in edges:
        item.start()
    for step in range(count + 2):
        if step < count:
            w = step
            local[w].wait()
            for item in line[w]:
                item.wait_recv()
            for item in wide[w] + tall[w]:
                item.start()
            twin[w][0, 0].start()
            if w + 2 < count:
                for item in line[w + 2]:
                    item.start()
        if 1 <= step <= count:
            w = step - 1
            for k in range(1, across):
                wide[w][k - 1].wait_recv()
                for l in range(1, down):
                    cross[w][k, l][0].start()
                twin[w][0, k].start()
            for l in range(1, down):
                tall[w][l - 1].wait_recv()
                for k in range(1, across):
                    cross[w][k, l][1].start()
                twin[w][l, 0].start()
        if step >= 2:
            w = step - 2
            for (k, l), both in cross[w].items():
                both[0].wait_recv()
                both[1].wait_recv()
                twin[w][l, k].start()
        if step == 0:
            for item in edges:
                item.wait()
            join_edges(arrived, reach, power, entry)
        if step == 1:
            around.hand_on()
            flat_local.wait()
            for item in flat_row:
                item.wait_recv()
            for item in flat_line + flat_twin[:1]:
                item.start()
        if step == count:
            for item, on in zip(flat_line, flat_twin[1:]):
                item.wait_recv()
                on.start()
        if step < count - 1:
            lax.fori_loop(*share(units, count - 1, step), forward_unit, 0)
        if hosts and step == 2:
            for item in twin[0].values():
                item.wait_recv()
            full = pltpu.make_async_copy(wholes[0], weight, weight_sem.at[0])
            full.start()
            own.wait()
            around.wait()
            load_block(0).start()
            full.wait()
        if hosts and 2 <= step < count:
            lax.fori_loop(*share(blocks * tiles, count - 2, step - 2), value_unit, 0)
        if hosts and step == count - 1:
            lax.fori_loop(0, rows, mix_row, 0)
            mixed_copy.start()
            for w in (1, 2):
                for item in twin[w].values():
                    item.wait_recv()
            full_mix = pltpu.make_async_copy(wholes[1], mix_full, mix_sem.at[0])
            full_mix.start()
        if hosts and step == count:
            full_mix.wait()
            lax.fori_loop(0, rows, project_unit, 0)
            near.start()
            key_own.start()
            lax.fori_loop(rows, project_units // 2, project_unit, 0)
            near.hand_on()
        if hosts and step == count + 1:
            lax.fori_loop(project_units // 2, project_units, project_unit, 0)
    if hosts:
        for index in (blocks * tiles - 2, blocks * tiles - 1):
            for item in store_tiles(index):
                item.wait()
        for index in (project_units - 2, project_units - 1):
            store_project(index).wait()
        near.wait()
        key_own.wait()
        mixed_copy.wait()
    for item in flat_twin:
        item.wait()
    for item in flat_row + flat_line:
        item.wait_send()
    for w in range(count):
        for item in twin[w].values():
            item.wait_send()
            if w > 2 or not hosts:
                item.wait_recv()
        for item in line[w] + wide[w] + tall[w]:
            item.wait_send()
        for both in cross[w].values():
            both[0].wait_send()
            both[1].wait_send()
    if not hosts:
        own.wait()
        around.wait()


def vmem(count):
    return [pl.BlockSpec(memory_space=pltpu.VMEM)] * count


def anywhere(count):
    return [pl.BlockSpec(memory_space=pl.ANY)] * count


def gather_weights(shards, feed, keep, decay, gain, reach, power, halo, skip, key_gain):
    sizes = shape_of()
    depth, cores, down, across = sizes
    seqs = down * across
    count = len(shards)
    pieces = [piece_shape(*shard.shape) for shard in shards]
    slots = (depth - 1) + (across - 1) + (down - 1) + 2 * (across - 1) * (down - 1) + across * down
    rows, length, chans = feed.shape
    state = (rows, 16, chans)
    width = min(FORWARD_WIDTH, chans)
    hosts = pieces[0] == shards[0].shape and shards[1].shape[1] % PROJECT_TILE == 0
    chunks = chunks_of(pieces)
    made, extra = [], []
    if hosts:
        wide = shards[0].shape[1]
        made = [jax.ShapeDtypeStruct((rows, halo + 1, length, wide), jnp.bfloat16)] * 2
        made += [
            jax.ShapeDtypeStruct(feed.shape, jnp.bfloat16),
            jax.ShapeDtypeStruct((rows, length, shards[1].shape[1]), jnp.float32),
            jax.ShapeDtypeStruct((rows, halo + 1, length, Z), jnp.bfloat16),
        ]
        extra = [
            pltpu.VMEM(sizes + pieces[1], jnp.bfloat16),
            pltpu.SemaphoreType.DMA((1,)),
            pltpu.VMEM((length, chans), jnp.float32),
            pltpu.SemaphoreType.DMA((1,)),
            pltpu.VMEM(feed.shape, jnp.bfloat16),
            pltpu.VMEM((2, length, PROJECT_TILE), jnp.float32),
            pltpu.SemaphoreType.DMA((2,)),
            pltpu.VMEM((rows, length, Z), jnp.bfloat16),
            pltpu.SemaphoreType.DMA((1,)),
            pltpu.SemaphoreType.DMA((1,)),
            pltpu.SemaphoreType.DMA((halo,)),
            pltpu.SemaphoreType.DMA((halo,)),
            pltpu.SemaphoreType.DMA((halo,)),
            pltpu.SemaphoreType.DMA((1,)),
            pltpu.VMEM(sizes + pieces[0], jnp.bfloat16),
            pltpu.VMEM((2, length, chans), jnp.bfloat16),
            pltpu.VMEM((2, length, HOST_TILE), jnp.bfloat16),
            pltpu.VMEM((2, length, HOST_TILE), jnp.bfloat16),
            pltpu.SemaphoreType.DMA((1,)),
            pltpu.SemaphoreType.DMA((2,)),
            pltpu.SemaphoreType.DMA((2, 2)),
        ]
    results = pl.pallas_call(
        functools.partial(gather_kernel, sizes, count, halo, hosts, chunks),
        out_shape=[jax.ShapeDtypeStruct(sizes + piece, jnp.bfloat16) for piece in pieces]
        + [
            jax.ShapeDtypeStruct((rows, halo + 1, length, chans), jnp.bfloat16),
            jax.ShapeDtypeStruct(state, jnp.float32),
            jax.ShapeDtypeStruct(feed.shape, jnp.bfloat16),
        ]
        + made,
        in_specs=anywhere(count) + vmem(6) + (anywhere(1) + vmem(1) if hosts else []),
        out_specs=anywhere(count + 1) + vmem(2) + anywhere(len(made)),
        scratch_shapes=[
            pltpu.SemaphoreType.DMA((len(chunks), slots)),
            pltpu.SemaphoreType.DMA((len(chunks), slots)),
            pltpu.SemaphoreType.DMA((len(chunks) + 1,)),
            pltpu.VMEM(state, jnp.float32),
            pltpu.VMEM((seqs - 1,) + state, jnp.float32),
            pltpu.SemaphoreType.DMA((seqs - 1,)),
            pltpu.SemaphoreType.DMA((seqs - 1,)),
            pltpu.VMEM(feed.shape, jnp.bfloat16),
            pltpu.SemaphoreType.DMA((halo,)),
            pltpu.SemaphoreType.DMA((halo,)),
            pltpu.SemaphoreType.DMA((halo,)),
            pltpu.SemaphoreType.DMA((1,)),
            pltpu.VMEM((width // LANES, length, LANES), jnp.float32),
            pltpu.VMEM((width // LANES * EMA_STEP * 8, LANES), jnp.float32),
            *extra,
        ],
        compiler_params=pltpu.CompilerParams(collective_id=0, has_side_effects=True, vmem_limit_bytes=48 * 2**20),
        name="gather_weights",
    )(*[shard.reshape(piece) for shard, piece in zip(shards, pieces)], feed, keep, decay, gain, reach, power, *([skip, key_gain] if hosts else []))
    total = depth * cores * down * across
    wholes = [whole.reshape(total * shard.shape[0], shard.shape[1]) for whole, shard in zip(results, shards)]
    return wholes, *results[count:]


def add_rows(target, total, others):
    rows = total.shape[0]
    chunk = 16 if rows % 16 == 0 else rows

    def body(index, carry):
        at = pl.ds(pl.multiple_of(index * chunk, chunk), chunk)
        result = total[at, :].astype(jnp.float32)
        for other in others:
            result = result + other[at, :].astype(jnp.float32)
        target[at, :] = result.astype(target.dtype)
        return carry

    lax.fori_loop(0, rows // chunk, body, 0)


def scatter_kernel(sizes, count, chunks, *refs):
    grads, small = refs[:count], refs[count]
    feed, grad, keep, decay, gain, start, reach, power = refs[count + 1 : count + 9]
    refs = refs[count + 9 :]
    outs, (small_out, back_out) = refs[:count], refs[count : count + 2]
    rest = refs[count + 2 :]
    rest, (
        edge, arrived, end, edge_send, edge_recv, wide, wide_grad, part, kept_states,
    ) = rest[:-9], rest[-9:]
    rows, length, chans = feed.shape
    width = wide.shape[0] * LANES
    seqs = sizes[2] * sizes[3]
    count = len(chunks)
    names = ("arrive", "own", "first_a", "first_b", "second_a", "second_b", "third")
    held = {name: rest[at * count : (at + 1) * count] for at, name in enumerate(names)}
    flat_planes, flat_pieces, small_parts, send_sem, recv_sem, own_sem, small_send, small_recv = rest[len(names) * count :]
    depth, cores, down, across = sizes
    spot = place_of()
    z, c, a, b = spot
    half = depth // 2
    front, back = pl.ds(0, half), pl.ds(half, depth - half)
    greet(sizes, spot)
    slots = {}

    def copy(w, kind, source, target, axis, by):
        slot = slots.setdefault(kind, len(slots))
        return pltpu.make_async_remote_copy(
            src_ref=source,
            dst_ref=target,
            send_sem=send_sem.at[w, slot],
            recv_sem=recv_sem.at[w, slot],
            device_id=peer_of(sizes, spot, axis, by),
            device_id_type=MESH,
        )

    def at_a(by):
        return lax.rem(a + by, down)

    def at_b(by):
        return lax.rem(b + by, across)

    twin, first, second, third = [], [], [], []
    for w in range(count):
        arrive = held["arrive"][w]
        twin.append(copy(w, "c", grads[chunks[w][0]].at[:, 1 - c, :, :, :, chunks[w][1]], arrive, 1, 1))
        first.append(
            [
                copy(w, ("a1", k), arrive.at[front, :, at_b(k)], held["first_a"][w].at[k - 1], 3, k)
                for k in range(1, across)
            ]
            + [
                copy(w, ("b1", l), arrive.at[back, at_a(l)], held["first_b"][w].at[l - 1], 2, l)
                for l in range(1, down)
            ]
        )
        second.append(
            [
                copy(w, ("a2", l), arrive.at[front, at_a(l), b], held["second_a"][w].at[l - 1], 2, l)
                for l in range(1, down)
            ]
            + [
                copy(w, ("b2", k), arrive.at[back, a, at_b(k)], held["second_b"][w].at[k - 1], 3, k)
                for k in range(1, across)
            ]
        )
        third.append(
            [
                copy(w, ("z", k), arrive.at[lax.rem(z + k, depth), a, b], held["third"][w].at[k - 1], 0, k)
                for k in range(1, depth)
            ]
        )

    stages = [(axis, 1 << bit) for axis in (1, 2, 3, 0) for bit in range(sizes[axis].bit_length() - 1)]

    def small_copy(at):
        axis, bit = stages[at]
        mine = spot[axis]
        towards = jnp.where(lax.rem(mine // bit, 2) == 0, bit, sizes[axis] - bit)
        return pltpu.make_async_remote_copy(
            src_ref=small_out,
            dst_ref=small_parts.at[at],
            send_sem=small_send.at[at],
            recv_sem=small_recv.at[at],
            device_id=peer_of(sizes, spot, axis, towards),
            device_id_type=MESH,
        )

    def own_load(w, at):
        return pltpu.make_async_copy(grads[chunks[w][0]].at[at, c, :, :, :, chunks[w][1]], held["own"][w].at[lax.rem(at, 2)], own_sem.at[w, lax.rem(at, 2)])

    def add_own(w):
        own_load(w, 0).start()

        def body(at, carry):
            @pl.when(at + 1 < depth)
            def _():
                own_load(w, at + 1).start()

            own_load(w, at).wait()
            for down_at in range(down):
                for across_at in range(across):
                    spot_ref = held["arrive"][w].at[at, down_at, across_at]
                    add_rows(spot_ref, spot_ref, [held["own"][w].at[lax.rem(at, 2), down_at, across_at]])
            return carry

        lax.fori_loop(0, depth, body, 0)

    flat = count - 1
    count = flat
    flat_arrive = held["arrive"][flat]

    def flat_copy(slot, source, target, device):
        return pltpu.make_async_remote_copy(
            src_ref=source,
            dst_ref=target,
            send_sem=send_sem.at[flat, slot],
            recv_sem=recv_sem.at[flat, slot],
            device_id=device,
            device_id_type=MESH,
        )

    flat_line = [
        flat_copy(k, flat_arrive.at[lax.rem(z + k, depth)], flat_planes.at[k - 1], peer_of(sizes, spot, 0, k))
        for k in range(1, depth)
    ]
    flat_row = []
    for by in range(1, seqs):
        to = lax.rem(a * across + b + by, seqs)
        source = flat_arrive.at[z, lax.div(to, across), lax.rem(to, across)]
        flat_row.append(flat_copy(depth - 1 + by, source, flat_pieces.at[by - 1], along(seqs, by)))

    def flat_pair():
        twin[flat].wait_recv()
        add_own(flat)
        for item in flat_line:
            item.start()

    def flat_sum():
        for item in flat_line:
            item.wait_recv()
        for down_at in range(down):
            for across_at in range(across):
                spot_ref = flat_arrive.at[z, down_at, across_at]
                add_rows(spot_ref, spot_ref, [flat_planes.at[k, down_at, across_at] for k in range(depth - 1)])
        for item in flat_row:
            item.start()

    def flat_finish():
        for item in flat_row:
            item.wait_recv()
        out = outs[chunks[flat][0]].at[:, chunks[flat][1]]
        add_rows(out, flat_arrive.at[z, a, b], [flat_pieces.at[at] for at in range(seqs - 1)])

    small_out[...] = small[...]
    edges = spread_edge(seqs, edge, arrived, edge_send, edge_recv, False)
    units = rows * (chans // width)

    def last_unit(index, carry):
        row, base = unit_of(index, width, chans)
        ema_last(True, row, base, grad, keep, decay, edge, wide)
        return carry

    def backward_unit(index, carry):
        row, base = unit_of(index, width, chans)
        ema_backward(
            row, base, feed, grad, keep, decay, gain, start, end, back_out, small_out, wide, wide_grad, part, kept_states
        )
        return carry

    for w in range(min(2, count)):
        twin[w].start()
    twin[flat].start()
    lax.fori_loop(0, units, last_unit, 0)
    for item in edges:
        item.start()
    busy = count - 1
    for step in range(max(count + 3, busy + len(stages))):
        if step < count:
            w = step
            twin[w].wait_recv()
            if w + 2 < count:
                twin[w + 2].start()
            add_own(w)
            for item in first[w]:
                item.start()
        if step == 0:
            flat_pair()
        if step == 2:
            flat_sum()
        if step == 4:
            flat_finish()
        if 1 <= step <= count:
            w = step - 1
            arrive = held["arrive"][w]
            for item in first[w]:
                item.wait_recv()
            for at in range(half):
                for l in range(down):
                    spot_ref = arrive.at[at, l, b]
                    add_rows(spot_ref, spot_ref, [held["first_a"][w].at[k, at, l] for k in range(across - 1)])
            for at in range(half, depth):
                for k in range(across):
                    spot_ref = arrive.at[at, a, k]
                    add_rows(spot_ref, spot_ref, [held["first_b"][w].at[l, at - half, k] for l in range(down - 1)])
            for item in second[w]:
                item.start()
        if 2 <= step <= count + 1:
            w = step - 2
            arrive = held["arrive"][w]
            for item in second[w]:
                item.wait_recv()
            for at in range(half):
                spot_ref = arrive.at[at, a, b]
                add_rows(spot_ref, spot_ref, [held["second_a"][w].at[l, at] for l in range(down - 1)])
            for at in range(half, depth):
                spot_ref = arrive.at[at, a, b]
                add_rows(spot_ref, spot_ref, [held["second_b"][w].at[k, at - half] for k in range(across - 1)])
            for item in third[w]:
                item.start()
        if 3 <= step <= count + 2:
            w = step - 3
            for item in third[w]:
                item.wait_recv()
            add_rows(outs[chunks[w][0]].at[:, chunks[w][1]], held["arrive"][w].at[z, a, b], [held["third"][w].at[k] for k in range(depth - 1)])
        if step == 0:
            for item in edges:
                item.wait()
            join_edges(arrived, reach, power, end)
        if step < busy:
            lax.fori_loop(*share(units, busy, step), backward_unit, 0)
        stage = step - busy
        if stage == -1:
            small_copy(0).start()
        if 0 <= stage < len(stages):
            small_copy(stage).wait()
            small_out[...] = small_out[...] + small_parts[stage]
            if stage + 1 < len(stages):
                small_copy(stage + 1).start()
    for item in [twin[flat]] + flat_line + flat_row:
        item.wait_send()
    for w in range(count):
        for item in [twin[w]] + first[w] + second[w] + third[w]:
            item.wait_send()


def scatter_grads(grads, small, feed, grad, keep, decay, gain, start, reach, power):
    sizes = shape_of()
    depth, cores, down, across = sizes
    total = depth * cores * down * across
    count = len(grads)
    half = depth // 2
    pieces = [piece_shape(g.shape[0] // total, g.shape[1]) for g in grads]
    leads = (
        (depth, down, across),
        (2, down, across),
        (across - 1, half, down),
        (down - 1, depth - half, across),
        (down - 1, half),
        (across - 1, depth - half),
        (depth - 1,),
    )
    slots = max(2 * (across - 1 + down - 1), down * across - 1) + depth
    stages = sum(size.bit_length() - 1 for size in sizes)
    chunks = chunks_of(pieces)
    parts = [(pieces[at][0], columns.size) for at, columns in chunks]
    rows, length, chans = feed.shape
    state = (rows, 16, chans)
    width = min(BACKWARD_WIDTH, chans)
    seqs = down * across
    results = pl.pallas_call(
        functools.partial(scatter_kernel, sizes, count, chunks),
        out_shape=[jax.ShapeDtypeStruct(piece, jnp.float32) for piece in pieces]
        + [
            jax.ShapeDtypeStruct(small.shape, jnp.float32),
            jax.ShapeDtypeStruct(feed.shape, jnp.bfloat16),
        ],
        in_specs=anywhere(count) + vmem(9),
        out_specs=vmem(count + 2),
        scratch_shapes=[pltpu.VMEM(lead + part, jnp.bfloat16) for lead in leads for part in parts]
        + [pltpu.VMEM((depth - 1, down, across) + parts[-1], jnp.bfloat16), pltpu.VMEM((down * across - 1,) + parts[-1], jnp.bfloat16)]
        + [
            pltpu.VMEM((stages,) + small.shape, jnp.float32),
            pltpu.SemaphoreType.DMA((len(chunks), slots)),
            pltpu.SemaphoreType.DMA((len(chunks), slots)),
            pltpu.SemaphoreType.DMA((len(chunks), 2)),
            pltpu.SemaphoreType.DMA((stages,)),
            pltpu.SemaphoreType.DMA((stages,)),
            pltpu.VMEM(state, jnp.float32),
            pltpu.VMEM((seqs - 1,) + state, jnp.float32),
            pltpu.VMEM(state, jnp.float32),
            pltpu.SemaphoreType.DMA((seqs - 1,)),
            pltpu.SemaphoreType.DMA((seqs - 1,)),
            pltpu.VMEM((width // LANES, length, LANES), jnp.float32),
            pltpu.VMEM((width // LANES, length, LANES), jnp.float32),
            pltpu.VMEM((width // LANES * EMA_STEP * 8, LANES), jnp.float32),
            pltpu.VMEM((length * 16, width), jnp.float32),
        ],
        compiler_params=pltpu.CompilerParams(collective_id=1, has_side_effects=True, vmem_limit_bytes=62 * 2**20),
        name="scatter_grads",
    )(
        *[g.reshape(sizes + piece) for g, piece in zip(grads, pieces)],
        small, feed, grad, keep, decay, gain, start, reach, power,
    )
    sums = [result.reshape(g.shape[0] // total, g.shape[1]) for result, g in zip(results[:count], grads)]
    return sums, *results[count:]


def passed_on(alive, forward):
    count = lax.axis_size("seq")
    place = lax.axis_index("seq")
    through = jnp.ones((alive.shape[0], 1, 1), jnp.float32)
    factors = []
    for away in range(1, count):
        exists = place >= away if forward else place + away < count
        factors.append(jnp.broadcast_to(jnp.where(exists, through, 0.0), (alive.shape[0], 16, LANES)))
        at = jnp.clip(place - away if forward else place + away, 0, count - 1)
        through = through * lax.dynamic_slice_in_dim(alive, at, 1, 1)[:, :, None]
    return jnp.stack(factors)


QUERY_BLOCK = 256
KEY_BLOCK = 512
VALUE_BLOCK = 1024


def attend_kernel(halo_span, query, key, value, key_docs, query_docs, out, probs):
    size, span = probs.shape
    first = pl.program_id(1) * size
    keys = pl.ds(pl.multiple_of(first, LANES), span)
    scores = against(query[0], key[0, keys, :]) * Z ** (-0.5)
    query_at = lax.broadcasted_iota(jnp.int32, (size, span), 0) + halo_span
    key_at = lax.broadcasted_iota(jnp.int32, (size, span), 1)
    allowed = (key_at <= query_at) & (key_docs[0, :, keys] == query_docs[0])
    scores = jnp.where(allowed, scores, NEG_FILL)
    expo = jnp.exp(scores - jnp.max(scores, axis=1, keepdims=True))
    probs[...] = low(expo / jnp.sum(expo, axis=1, keepdims=True))

    def body(at, carry):
        columns = pl.ds(pl.multiple_of(at * VALUE_BLOCK, VALUE_BLOCK), VALUE_BLOCK)
        out[0, :, columns] = product(probs[...], value[0, keys, columns])
        return carry

    lax.fori_loop(0, out.shape[2] // VALUE_BLOCK, body, 0)


def attend(query, key, value, docs_row, docs_column, halo):
    rows, places, _ = query.shape
    window, wide = value.shape[1:]
    size = min(QUERY_BLOCK, places)
    span = halo * places + size
    return pl.pallas_call(
        functools.partial(attend_kernel, halo * places),
        out_shape=jax.ShapeDtypeStruct((rows, places, wide), jnp.float32),
        grid=(rows, places // size),
        in_specs=[
            pl.BlockSpec((1, size, Z), lambda r, i: (r, i, 0)),
            pl.BlockSpec((1, window, Z), lambda r, i: (r, 0, 0)),
            pl.BlockSpec((1, window, wide), lambda r, i: (r, 0, 0)),
            pl.BlockSpec((1, 1, window), lambda r, i: (r, 0, 0)),
            pl.BlockSpec((1, size, 1), lambda r, i: (r, i, 0)),
        ],
        out_specs=pl.BlockSpec((1, size, wide), lambda r, i: (r, i, 0)),
        scratch_shapes=[pltpu.VMEM((size, span), jnp.bfloat16)],
        compiler_params=pltpu.CompilerParams(vmem_limit_bytes=40 * 2**20),
        cost_estimate=pl.CostEstimate(
            flops=2 * rows * places * span * (wide + Z),
            bytes_accessed=rows * (window * wide * 2 + places * wide * 4),
            transcendentals=rows * places * span,
        ),
        name="attend",
    )(query, key, value, docs_row, docs_column[:, halo * places :])


def attend_back_kernel(
    halo_span, query, key, value, slope, pulled, key_docs, query_docs, d_query, d_key, d_value, chances, pulls, balance
):
    window, places = chances.shape
    step = d_value.shape[1]
    chunk = pl.program_id(1)

    @pl.when(chunk == 0)
    def _():
        peak = jnp.full((1, places), NEG_FILL, jnp.float32)

        def score(at, peak):
            keys = pl.ds(pl.multiple_of(at * step, step), step)
            scores = against(key[0, keys, :], query[0]) * Z ** (-0.5)
            key_at = lax.broadcasted_iota(jnp.int32, (step, places), 0) + at * step
            query_at = lax.broadcasted_iota(jnp.int32, (step, places), 1) + halo_span
            allowed = (key_at <= query_at) & (key_docs[0, keys, :] == query_docs[0])
            scores = jnp.where(allowed, scores, NEG_FILL)
            chances[keys, :] = scores
            return jnp.maximum(peak, jnp.max(scores, axis=0, keepdims=True))

        peak = lax.fori_loop(0, window // step, score, peak)

        def weigh(at, total):
            keys = pl.ds(pl.multiple_of(at * step, step), step)
            expo = jnp.exp(chances[keys, :] - peak)
            chances[keys, :] = expo
            return total + jnp.sum(expo, axis=0, keepdims=True)

        total = lax.fori_loop(0, window // step, weigh, jnp.zeros((1, places), jnp.float32))

        def pull(at, held):
            keys = pl.ds(pl.multiple_of(at * step, step), step)
            probs = chances[keys, :] / total
            chances[keys, :] = probs
            local = against(value[0, keys, :], pulled[0])
            pulls[keys, :] = local
            return held + jnp.sum(probs * local, axis=0, keepdims=True)

        balance[...] = lax.fori_loop(0, window // step, pull, jnp.zeros((1, places), jnp.float32))
        d_query[...] = jnp.zeros_like(d_query)

    keys = pl.ds(pl.multiple_of(chunk * step, step), step)
    probs = chances[keys, :]
    d_scores = low(probs * (pulls[keys, :] - balance[...]))
    d_key[0] = product(d_scores, query[0]) * Z ** (-0.5)
    d_query[0] = d_query[0] + transposed(d_scores, key[0, keys, :]) * Z ** (-0.5)
    probs_low = low(probs)

    def body(at, carry):
        columns = pl.ds(pl.multiple_of(at * VALUE_BLOCK, VALUE_BLOCK), VALUE_BLOCK)
        local = product(probs_low, pulled[0, :, columns])
        d_value[0, :, columns] = low(local * slope[0, :, columns].astype(jnp.float32))
        return carry

    lax.fori_loop(0, d_value.shape[2] // VALUE_BLOCK, body, 0)


def attend_back(query, key, value, slope, pulled, docs_row, docs_column, halo):
    rows, places, _ = query.shape
    window, wide = value.shape[1:]
    step = min(KEY_BLOCK, places)
    return pl.pallas_call(
        functools.partial(attend_back_kernel, halo * places),
        out_shape=[
            jax.ShapeDtypeStruct((rows, places, Z), jnp.float32),
            jax.ShapeDtypeStruct((rows, window, Z), jnp.float32),
            jax.ShapeDtypeStruct((rows, window, wide), jnp.bfloat16),
        ],
        grid=(rows, window // step),
        in_specs=[
            pl.BlockSpec((1, places, Z), lambda r, i: (r, 0, 0)),
            pl.BlockSpec((1, window, Z), lambda r, i: (r, 0, 0)),
            pl.BlockSpec((1, window, wide), lambda r, i: (r, 0, 0)),
            pl.BlockSpec((1, step, wide), lambda r, i: (r, i, 0)),
            pl.BlockSpec((1, places, wide), lambda r, i: (r, 0, 0)),
            pl.BlockSpec((1, window, 1), lambda r, i: (r, 0, 0)),
            pl.BlockSpec((1, 1, places), lambda r, i: (r, 0, 0)),
        ],
        out_specs=[
            pl.BlockSpec((1, places, Z), lambda r, i: (r, 0, 0)),
            pl.BlockSpec((1, step, Z), lambda r, i: (r, i, 0)),
            pl.BlockSpec((1, step, wide), lambda r, i: (r, i, 0)),
        ],
        scratch_shapes=[
            pltpu.VMEM((window, places), jnp.float32),
            pltpu.VMEM((window, places), jnp.float32),
            pltpu.VMEM((1, places), jnp.float32),
        ],
        compiler_params=pltpu.CompilerParams(vmem_limit_bytes=48 * 2**20),
        cost_estimate=pl.CostEstimate(
            flops=4 * rows * places * window * (wide + Z),
            bytes_accessed=rows * (window * wide * 6 + places * wide * 2),
            transcendentals=rows * places * window,
        ),
        name="attend_back",
    )(query, key, value, slope, pulled, docs_column, docs_row[:, :, halo * places :])


def on_device(
    layer_input,
    cotangent,
    doc_ids,
    resets,
    mix_weight,
    value_weight,
    head_weight,
    expand_weight,
    shrink_weight,
    chan_vectors,
    ema_logits,
    ema_beta_eta,
    z_affine,
):
    seq_count = lax.axis_size("seq")
    seq_place = lax.axis_index("seq")
    rows, places, width = layer_input.shape
    tokens = rows * places
    halo = min(-(-(REACH - 1) // places), seq_count - 1)
    window = (halo + 1) * places

    inputs32 = layer_input.astype(jnp.float32)
    center = inputs32 - jnp.mean(inputs32, axis=-1, keepdims=True)
    unit = lax.rsqrt(jnp.mean(center * center, axis=-1, keepdims=True) + 1e-05)
    plain = center * unit
    normed = plain * chan_vectors[0]
    normed_low = low(normed)

    rate = jax.nn.sigmoid(ema_logits[0])
    damping = jax.nn.sigmoid(ema_logits[1])
    decay = (1.0 - rate * damping).T
    weight_in = rate * ema_beta_eta[0]
    weight_out = ema_beta_eta[1]
    gain = (weight_in * weight_out).T
    decay_all = decay
    reach = 1
    while reach < places:
        decay_all = decay_all * decay_all
        reach *= 2
    powers = [jnp.ones_like(decay)]
    while len(powers) < seq_count - 1:
        powers.append(powers[-1] * decay_all)
    power = jnp.stack(powers)
    keep_row = 1.0 - resets.astype(jnp.float32)
    keep_own = lax.dynamic_slice_in_dim(keep_row, seq_place * places, places, 1)
    keep = jnp.broadcast_to(keep_own[:, None, :, None], (rows, 1, places, LANES)).reshape(rows, places, LANES)
    alive = jnp.min(keep_row.reshape(rows, seq_count, places), axis=2)

    (value_full, mix_full, expand_full, head_full), normed_window, start, ema_low, *made = gather_weights(
        (value_weight, mix_weight, expand_weight, head_weight),
        normed_low,
        keep,
        decay,
        gain,
        passed_on(alive, True),
        power,
        halo,
        chan_vectors[2] * normed,
        z_affine[2:3],
    )
    normed_window = normed_window.reshape(rows * window, width)
    value_full, mix_full, head_full, expand_full, shrink_late = lax.optimization_barrier(
        (value_full, mix_full, head_full, expand_full, shrink_weight)
    )
    shrink_full = lax.all_gather(shrink_late, BOTH, axis=0, tiled=True)

    premix = (ema_low.astype(jnp.float32) + chan_vectors[2] * normed).reshape(tokens, width)
    if made:
        values_low, value_slope = (item.reshape(rows, window, V) for item in made[:2])
        mixed_low = made[2].reshape(tokens, width)
        projected = made[3].reshape(tokens, made[3].shape[2])
        key_window = made[4].reshape(rows, window, Z)
        shared_pre = projected[:, :Z]
        shared = jax.nn.silu(shared_pre)
        queries_low = low(shared * z_affine[0] + z_affine[1]).reshape(rows, places, Z)
    else:
        mixed_low = low(jax.nn.silu(premix))
        value_pre = product(normed_window, value_full)
        values_low = low(jax.nn.silu(value_pre)).reshape(rows, window, V)
        value_slope = low(silu_slope(value_pre)).reshape(rows, window, V)
        projected = product(mixed_low, mix_full)
        shared_pre = projected[:, :Z]
        shared = jax.nn.silu(shared_pre)
        queries_low = low(shared * z_affine[0] + z_affine[1]).reshape(rows, places, Z)
        keys_low = low(shared * z_affine[2]).reshape(rows, places, Z)
        keys_sent = [shift_seq(keys_low, by) for by in range(halo, 0, -1)]
        key_window = jnp.concatenate(keys_sent + [keys_low], axis=1)
    reset_pre = projected[:, Z : Z + V]
    head_base = projected[:, Z + V : Z + V + width]
    update_pre = projected[:, Z + V + width :]
    reset_gate = jax.nn.silu(reset_pre)
    update_gate = jax.nn.sigmoid(update_pre)

    padded_docs = jnp.pad(doc_ids, ((0, 0), (halo * places, 0)), constant_values=-1)
    key_docs = lax.dynamic_slice_in_dim(padded_docs, seq_place * places, window, 1)
    docs_row, docs_column = key_docs[:, None, :], key_docs[:, :, None]
    attended = attend(queries_low, key_window, values_low, docs_row, docs_column, halo).reshape(tokens, V)
    gated_low = low(reset_gate * attended)
    head_pre = head_base + product(gated_low, head_full)
    candidate = jax.nn.silu(head_pre)
    residual_in = inputs32.reshape(tokens, width)
    first = residual_in + update_gate * (candidate - residual_in)
    second, second_pull = jax.vjp(scaled_norm, first, chan_vectors[1])
    second_low = low(second)
    expand_pre = product(second_low, expand_full)
    expand_slope = silu_slope(expand_pre)
    hidden_low, expand_slope = lax.optimization_barrier((low(jax.nn.silu(expand_pre)), expand_slope))
    output = low(first + product(hidden_low, shrink_full)).reshape(rows, places, width)

    cot_low = cotangent.reshape(tokens, width)
    shrink_part = low(transposed(hidden_low, cot_low))
    d_expand = low(against(cot_low, shrink_full) * expand_slope)
    d_first_norm, d_gain_two = second_pull(against(d_expand, expand_full))
    d_first = cot_low.astype(jnp.float32) + d_first_norm
    d_update = d_first * (candidate - residual_in) * update_gate * (1.0 - update_gate)
    d_direct = d_first * (1.0 - update_gate)
    d_head = d_first * update_gate * silu_slope(head_pre)
    d_head_low = low(d_head)
    d_gated = against(d_head_low, head_full)
    d_reset = d_gated * attended * silu_slope(reset_pre)
    d_attended = low(d_gated * reset_gate).reshape(rows, places, V)
    d_queries, key_term, d_value_pre = attend_back(
        queries_low, key_window, values_low, value_slope, d_attended, docs_row, docs_column, halo
    )
    d_value_pre, second_late, gated_late = lax.optimization_barrier((d_value_pre, second_low, gated_low))
    expand_part = low(transposed(second_late, d_expand))
    head_part = low(transposed(gated_late, d_head_low))
    d_value_pre = d_value_pre.reshape(rows * window, V)
    d_keys = key_term[:, halo * places :]
    for by in range(1, halo + 1):
        begin = (halo - by) * places
        d_keys = d_keys + shift_seq(low(key_term[:, begin : begin + places]), -by).astype(jnp.float32)
    d_keys32 = low(d_keys).astype(jnp.float32).reshape(tokens, Z)
    value_part = low(transposed(normed_window, d_value_pre))
    value_term = against(d_value_pre, value_full).reshape(rows, halo + 1, places, width)
    terms = low(value_term[:, :halo])
    d_normed_value = value_term[:, halo]
    for by in range(1, halo + 1):
        d_normed_value = d_normed_value + shift_seq(terms[:, halo - by], -by).astype(jnp.float32)
    d_query_flat = d_queries.reshape(tokens, Z)
    d_shared = d_query_flat * z_affine[0] + d_keys32 * z_affine[2]
    affine_part = jnp.stack(
        [
            jnp.sum(d_query_flat * shared, axis=0),
            jnp.sum(d_query_flat, axis=0),
            jnp.sum(d_keys32 * shared, axis=0),
        ]
    )
    d_projected = low(
        jnp.concatenate([d_shared * silu_slope(shared_pre), d_reset, d_head, d_update], axis=1)
    )
    mix_part = low(transposed(mixed_low, d_projected))
    d_premix = against(d_projected, mix_full) * silu_slope(premix)
    omega_part = jnp.sum(d_premix * normed.reshape(tokens, width), axis=0)
    d_premix = d_premix.reshape(rows, places, width)
    d_ema = low(d_premix)
    known = d_premix * chan_vectors[2] + d_normed_value
    d_gain_one = jnp.sum(known * plain, axis=(0, 1))
    small_part = jnp.concatenate(
        [
            jnp.zeros((32, width), jnp.float32),
            jnp.stack([d_gain_one, d_gain_two, omega_part]),
            jnp.pad(affine_part.reshape(1, 3 * Z), ((0, 4), (0, width - 3 * Z))),
        ],
        axis=0,
    )
    (shrink_grad, expand_grad, value_grad, mix_grad, head_grad), small_sum, d_feed = scatter_grads(
        (shrink_part, expand_part, value_part, mix_part, head_part),
        small_part,
        normed_low,
        d_ema,
        keep,
        decay,
        gain,
        start,
        passed_on(alive, False),
        power,
    )
    d_normed = known + d_feed.astype(jnp.float32)
    pulled = d_normed * chan_vectors[0]
    pulled = pulled - jnp.mean(pulled, axis=-1, keepdims=True) - plain * jnp.mean(pulled * plain, axis=-1, keepdims=True)
    x_grad = d_direct.reshape(rows, places, width) + pulled * unit
    gain_sum = small_sum[:16]
    decay_sum = small_sum[16:32]
    chan_grad = small_sum[32:35].at[0].add(jnp.sum(gain * gain_sum, axis=0) / chan_vectors[0])
    affine_grad = small_sum[35, : 3 * Z].reshape(3, Z)
    d_gain = gain_sum.T
    d_decay = (decay_sum * gain).T
    d_weight_in = d_gain * weight_out
    coef_grad = jnp.stack([d_weight_in * rate, d_gain * weight_in])
    d_rate = d_weight_in * ema_beta_eta[0] - d_decay * damping
    d_damping = -d_decay * rate
    logits_grad = jnp.stack([d_rate * rate * (1.0 - rate), d_damping * damping * (1.0 - damping)])
    return (
        output,
        x_grad,
        mix_grad,
        value_grad,
        head_grad,
        expand_grad,
        shrink_grad,
        chan_grad,
        logits_grad,
        coef_grad,
        affine_grad,
    )


def solution(mesh):
    placed = (
        P("dp", "seq", None),
        P("dp", "seq", None),
        P("dp", None),
        P("dp", None),
        P(BOTH, None),
        P(BOTH, None),
        P(BOTH, None),
        P(BOTH, None),
        P(BOTH, None),
        P(),
        P(),
        P(),
        P(),
    )
    return jax.shard_map(
        on_device,
        mesh=mesh,
        in_specs=placed,
        out_specs=(
            P("dp", "seq", None),
            P("dp", "seq", None),
            P(BOTH, None),
            P(BOTH, None),
            P(BOTH, None),
            P(BOTH, None),
            P(BOTH, None),
            P(),
            P(),
            P(),
            P(),
        ),
        check_vma=False,
    )
```

```python
import functools
import jax
import jax.numpy as jnp
from jax import lax
from jax.experimental import pallas as pl
from jax.experimental.pallas import tpu as pltpu
from jax.sharding import PartitionSpec as P

Z = 128
V = 2048
REACH = 1024
NEG_FILL = -1000000000.0
BOTH = ("dp", "seq")
MESH = pl.DeviceIdType.MESH
LANES = 128
EMA_STEP = 16
FORWARD_WIDTH = 512
BACKWARD_WIDTH = 256
HOST_TILE = 512
PROJECT_TILE = 384


def lanes_at(base, group):
    return pl.ds(pl.multiple_of(base + group * LANES, LANES), LANES)


def row_of(ref, step, group):
    return ref[group, pl.ds(step, 8, stride=0), :]


def widen(source, row, base, wide):
    for group in range(wide.shape[0]):
        wide[group] = source[row, :, lanes_at(base, group)].astype(jnp.float32)


def halves_of(ref, base, groups, row=None):
    spots = [(slice(h * 8, h * 8 + 8), lanes_at(base, g)) for g in range(groups) for h in range(2)]
    return [ref[spot] if row is None else ref[(row,) + spot] for spot in spots]


def put_halves(ref, base, values, row):
    for at, value in enumerate(values):
        g, h = divmod(at, 2)
        ref[row, h * 8 : h * 8 + 8, lanes_at(base, g)] = value


def add_halves(ref, first, base, values):
    for at, value in enumerate(values):
        g, h = divmod(at, 2)
        spot = (slice(first + h * 8, first + h * 8 + 8), lanes_at(base, g))
        ref[spot] = ref[spot] + value


def fold_rows(part, group):
    halves = []
    for half in range(EMA_STEP // 8):
        base = group * EMA_STEP * 8 + half * 64
        total = part[pl.ds(base, 8, stride=8), :]
        for sub in range(1, 8):
            total = total + part[pl.ds(base + sub, 8, stride=8), :]
        halves.append(total)
    return jnp.concatenate(halves, axis=0).astype(jnp.bfloat16)


def unit_of(index, width, chans):
    across = chans // width
    return lax.div(index, across), pl.multiple_of(lax.rem(index, across) * width, width)


def ema_last(reverse, row, base, feed, keep, decay, last, wide):
    length, groups = feed.shape[1], wide.shape[0]
    widen(feed, row, base, wide)
    decays = halves_of(decay, base, groups)

    def body(index, states):
        states = list(states)
        block = (length // EMA_STEP - 1 - index) if reverse else index
        first = pl.multiple_of(block * EMA_STEP, EMA_STEP)
        for offset in range(EMA_STEP):
            step = first + (EMA_STEP - 1 - offset if reverse else offset)
            kept = row_of(keep, step, row)
            for at in range(2 * groups):
                fed = row_of(wide, step, at // 2)
                if reverse:
                    states[at] = (kept * decays[at]) * (states[at] + fed)
                else:
                    states[at] = (kept * decays[at]) * states[at] + fed
        return tuple(states)

    zero = jnp.zeros((8, LANES), jnp.float32)
    put_halves(last, base, lax.fori_loop(0, length // EMA_STEP, body, (zero,) * (2 * groups)), row)


def ema_forward(row, base, feed, keep, decay, gain, start, out, wide, part):
    length, groups = feed.shape[1], wide.shape[0]
    widen(feed, row, base, wide)
    decays, gains = halves_of(decay, base, groups), halves_of(gain, base, groups)

    def body(index, states):
        states = list(states)
        first = pl.multiple_of(index * EMA_STEP, EMA_STEP)
        for offset in range(EMA_STEP):
            kept = row_of(keep, first + offset, row)
            for g in range(groups):
                fed = row_of(wide, first + offset, g)
                both = []
                for at in (2 * g, 2 * g + 1):
                    states[at] = (kept * decays[at]) * states[at] + fed
                    both.append(gains[at] * states[at])
                spot = g * EMA_STEP * 8 + offset * 8
                part[spot : spot + 8, :] = both[0] + both[1]
        for g in range(groups):
            out[row, pl.ds(first, EMA_STEP), lanes_at(base, g)] = fold_rows(part, g)
        return tuple(states)

    lax.fori_loop(0, length // EMA_STEP, body, tuple(halves_of(start, base, groups, row)))


def ema_backward(row, base, feed, grad, keep, decay, gain, start, end, back, sums, wide, wide_grad, part, held):
    length, groups = feed.shape[1], wide.shape[0]
    widen(feed, row, base, wide)
    widen(grad, row, base, wide_grad)
    decays, gains = halves_of(decay, base, groups), halves_of(gain, base, groups)
    blocks = length // EMA_STEP

    def forward(index, states):
        states = list(states)
        first = pl.multiple_of(index * EMA_STEP, EMA_STEP)
        for offset in range(EMA_STEP):
            kept = row_of(keep, first + offset, row)
            for at in range(2 * groups):
                g, h = divmod(at, 2)
                held[pl.ds((first + offset) * 16 + h * 8, 8), g * LANES : (g + 1) * LANES] = kept * states[at]
                states[at] = (kept * decays[at]) * states[at] + row_of(wide, first + offset, g)
        return tuple(states)

    lax.fori_loop(0, blocks, forward, tuple(halves_of(start, base, groups, row)))

    def backward(index, carried):
        pulls, gain_sums, decay_sums = (list(c) for c in carried)
        first = pl.multiple_of((blocks - 1 - index) * EMA_STEP, EMA_STEP)
        for offset in reversed(range(EMA_STEP)):
            step = first + offset
            kept = row_of(keep, step, row)
            for g in range(groups):
                pulled, fed = row_of(wide_grad, step, g), row_of(wide, step, g)
                both = []
                for h in range(2):
                    at = 2 * g + h
                    local = pulls[at] + pulled
                    both.append(gains[at] * local)
                    gain_sums[at] = gain_sums[at] + local * fed
                    before = held[pl.ds(step * 16 + h * 8, 8), g * LANES : (g + 1) * LANES]
                    decay_sums[at] = decay_sums[at] + local * before
                    pulls[at] = (kept * decays[at]) * local
                spot = g * EMA_STEP * 8 + offset * 8
                part[spot : spot + 8, :] = both[0] + both[1]
        for g in range(groups):
            back[row, pl.ds(first, EMA_STEP), lanes_at(base, g)] = fold_rows(part, g)
        return (tuple(pulls), tuple(gain_sums), tuple(decay_sums))

    zeros = (jnp.zeros((8, LANES), jnp.float32),) * (2 * groups)
    _, gain_sums, decay_sums = lax.fori_loop(
        0, blocks, backward, (tuple(halves_of(end, base, groups, row)), zeros, zeros)
    )
    add_halves(sums, 0, base, gain_sums)
    add_halves(sums, 16, base, decay_sums)


def layer_norm(values):
    center = values - jnp.mean(values, axis=-1, keepdims=True)
    spread = jnp.mean(center * center, axis=-1, keepdims=True)
    return center * lax.rsqrt(spread + 1e-05)


def scaled_norm(values, gain):
    return layer_norm(values) * gain


def silu_slope(values):
    squash = jax.nn.sigmoid(values)
    return squash * (1.0 + values * (1.0 - squash))


def product(left, right):
    return jnp.dot(left, right, preferred_element_type=jnp.float32)


def against(left, right):
    return lax.dot_general(left, right, (((1,), (1,)), ((), ())), preferred_element_type=jnp.float32)


def transposed(left, right):
    return lax.dot_general(left, right, (((0,), (0,)), ((), ())), preferred_element_type=jnp.float32)


def low(values):
    return values.astype(jnp.bfloat16)


def shift_seq(values, by):
    count = lax.axis_size("seq")
    pairs = [(i, i + by) for i in range(count) if 0 <= i + by < count]
    return lax.ppermute(values, "seq", pairs)


def side_of(count):
    side = 1
    while side * side < count:
        side *= 2
    return side


def shape_of():
    depth = lax.axis_size("dp") // 2
    seqs = lax.axis_size("seq")
    down = side_of(seqs)
    return depth, 2, down, seqs // down


def place_of():
    depth, cores, down, across = shape_of()
    dp, seq = lax.axis_index("dp"), lax.axis_index("seq")
    return lax.div(dp, cores), lax.rem(dp, cores), lax.div(seq, across), lax.rem(seq, across)


def peer_of(sizes, spot, axis, by):
    spot = list(spot)
    spot[axis] = lax.rem(spot[axis] + by, sizes[axis])
    return {"dp": spot[0] * sizes[1] + spot[1], "seq": spot[2] * sizes[3] + spot[3]}


def along(count, by):
    return {"dp": lax.axis_index("dp"), "seq": lax.rem(lax.axis_index("seq") + by, count)}


def greet(sizes, spot):
    barrier = pltpu.get_barrier_semaphore()
    seqs = sizes[2] * sizes[3]
    peers = [peer_of(sizes, spot, axis, by) for axis in (0, 1) for by in range(1, sizes[axis])]
    peers += [along(seqs, by) for by in range(1, seqs)]
    for peer in peers:
        pl.semaphore_signal(barrier, inc=1, device_id=peer, device_id_type=MESH)
    pl.semaphore_wait(barrier, len(peers))


def piece_shape(rows, columns):
    return (rows, columns) if rows % 16 == 0 else (rows * columns // LANES, LANES)


def chunks_of(pieces):
    chunks = []
    for at, (rows, columns) in enumerate(pieces):
        if rows * columns >= 2**17:
            half = columns // (2 * LANES) * LANES
            chunks += [(at, pl.ds(0, half)), (at, pl.ds(half, columns - half))]
        else:
            chunks.append((at, pl.ds(0, columns)))
    return chunks


def share(total, parts, at):
    return total * at // parts, total * (at + 1) // parts


def spread_edge(seqs, edge, arrived, send, recv, forward):
    return [
        pltpu.make_async_remote_copy(
            src_ref=edge,
            dst_ref=arrived.at[by - 1],
            send_sem=send.at[by - 1],
            recv_sem=recv.at[by - 1],
            device_id=along(seqs, by if forward else seqs - by),
            device_id_type=MESH,
        )
        for by in range(1, seqs)
    ]


def join_edges(arrived, reach, power, entry):
    rows, _, chans = entry.shape

    def body(row, carry):
        for group in range(chans // LANES):
            spot = slice(group * LANES, (group + 1) * LANES)
            total = None
            for at in range(arrived.shape[0]):
                term = reach[at, row] * power[at, :, spot] * arrived[at, row, :, spot]
                total = term if total is None else total + term
            entry[row, :, spot] = total
        return carry

    lax.fori_loop(0, rows, body, 0)


class Halo:
    def __init__(self, count, seqs, feed, window, zero, send, recv, local, hand_send):
        place = lax.axis_index("seq")
        relay = seqs == 4 and count == 2
        self.items = []

        def copy(source, by, towards, sent):
            return pltpu.make_async_remote_copy(
                src_ref=source,
                dst_ref=window.at[:, count - by],
                send_sem=sent,
                recv_sem=recv.at[by - 1],
                device_id=along(seqs, towards),
                device_id_type=MESH,
            )

        for by in range(1, count + 1):
            gives = place + by < seqs
            if relay and by == 1:
                gives = jnp.logical_and(gives, place != 1)
            blank = pltpu.make_async_copy(zero, window.at[:, count - by], local.at[by - 1])
            self.items.append((gives, place >= by, copy(feed, by, by, send.at[by - 1]), blank))
        self.hands = (place == 3, copy(window.at[:, 0], 1, 3, hand_send.at[0])) if relay else None

    def start(self):
        for gives, takes, remote, blank in self.items:
            pl.when(gives)(remote.start)
            pl.when(jnp.logical_not(takes))(blank.start)

    def hand_on(self):
        if self.hands:
            at_hand, hand = self.hands

            @pl.when(at_hand)
            def _():
                self.items[1][2].wait_recv()
                hand.start()

    def wait(self):
        for at, (gives, takes, remote, blank) in enumerate(self.items):
            waits = takes
            if self.hands and at == 1:
                waits = jnp.logical_and(takes, jnp.logical_not(self.hands[0]))
            pl.when(waits)(remote.wait_recv)
            pl.when(jnp.logical_not(takes))(blank.wait)
            pl.when(gives)(remote.wait_send)
        if self.hands:
            pl.when(self.hands[0])(self.hands[1].wait_send)


def gather_kernel(sizes, count, halo, hosts, chunks, *refs):
    hosts_in = refs[count + 6 : count + 8] if hosts else ()
    refs = refs[: count + 6] + refs[count + 6 + len(hosts_in) :]
    shards, (feed, keep, decay, gain, reach, power) = refs[:count], refs[count : count + 6]
    wholes, (window, entry, out) = refs[count + 6 : 2 * count + 6], refs[2 * count + 6 : 2 * count + 9]
    if hosts:
        skip, key_gain = hosts_in
        values, slopes, mixed_out, projected, key_window = refs[2 * count + 9 : 2 * count + 14]
        weight, block_in, value_tile, slope_tile, weight_sem, in_sem, out_sem = refs[-7:]
        (
            mix_full, mix_sem, skip_in, skip_sem, mixed, project_tile, project_sem, keys, keys_sem, mixed_sem,
            key_send, key_recv, key_local, key_hand,
        ) = refs[-21:-7]
        refs = refs[: 2 * count + 9] + refs[2 * count + 14 : -21]
    (
        send_sem, recv_sem, local_sem, edge, arrived, edge_send, edge_recv,
        zero, halo_send, halo_recv, halo_local, hand_send, wide_feed, part,
    ) = refs[2 * count + 9 :]
    rows, length, chans = feed.shape
    width = wide_feed.shape[0] * LANES
    seqs = sizes[2] * sizes[3]
    depth, cores, down, across = sizes
    spot = place_of()
    z, c, a, b = spot
    half = depth // 2
    greet(sizes, spot)
    slots = {}

    def copy(w, kind, source, target, axis, by):
        slot = slots.setdefault(kind, len(slots))
        return pltpu.make_async_remote_copy(
            src_ref=source,
            dst_ref=target,
            send_sem=send_sem.at[w, slot],
            recv_sem=recv_sem.at[w, slot],
            device_id=peer_of(sizes, spot, axis, by),
            device_id_type=MESH,
        )

    def block(w, a_by=0, b_by=0, part=None):
        at = pl.ds(0, depth) if part is None else part
        whole, columns = chunks[w]
        beside = lax.rem(a - a_by + down, down), lax.rem(b - b_by + across, across)
        return wholes[whole].at[at, c, *beside, :, columns]

    front, back = pl.ds(0, half), pl.ds(half, depth - half)
    local, line, wide, tall, cross, twin = [], [], [], [], [], []
    flat, count = len(chunks) - 1, len(chunks) - 1
    for w, (whole, columns) in enumerate(chunks[:count]):
        own = wholes[whole].at[z, c, a, b, :, columns]
        shard = shards[whole].at[:, columns]
        local.append(pltpu.make_async_copy(shard, own, local_sem.at[w]))
        line.append([copy(w, ("z", k), shard, own, 0, k) for k in range(1, depth)])
        wide.append([copy(w, ("x", k), block(w), block(w), 3, k) for k in range(1, across)])
        tall.append([copy(w, ("y", l), block(w), block(w), 2, l) for l in range(1, down)])
        pairs = [(k, l) for k in range(1, across) for l in range(1, down)]
        cross.append(
            {
                (k, l): (
                    copy(w, ("f", k, l), block(w, 0, k, front), block(w, 0, k, front), 2, l),
                    copy(w, ("g", k, l), block(w, l, 0, back), block(w, l, 0, back), 3, k),
                )
                for k, l in pairs
            }
        )
        twin.append(
            {
                (l, k): copy(w, ("c", l, k), block(w, l, k), block(w, l, k), 1, 1)
                for l in range(down)
                for k in range(across)
            }
        )
    whole, columns = chunks[flat]

    def plane(back_by=0):
        return wholes[whole].at[lax.rem(z - back_by + depth, depth), c, :, :, :, columns]

    def flat_copy(slot, source, target, device):
        return pltpu.make_async_remote_copy(
            src_ref=source,
            dst_ref=target,
            send_sem=send_sem.at[flat, slot],
            recv_sem=recv_sem.at[flat, slot],
            device_id=device,
            device_id_type=MESH,
        )

    flat_shard, flat_own = shards[whole].at[:, columns], wholes[whole].at[z, c, a, b, :, columns]
    flat_local = pltpu.make_async_copy(flat_shard, flat_own, local_sem.at[flat])
    flat_row = [flat_copy(by - 1, flat_shard, flat_own, along(seqs, by)) for by in range(1, seqs)]
    flat_line = [
        flat_copy(seqs - 2 + k, plane(), plane(), peer_of(sizes, spot, 0, k)) for k in range(1, depth)
    ]
    flat_twin = [
        flat_copy(seqs + depth - 2 + k, plane(k), plane(k), peer_of(sizes, spot, 1, 1)) for k in range(depth)
    ]
    zero[...] = jnp.zeros_like(zero)
    around = Halo(halo, seqs, feed, window, zero, halo_send, halo_recv, halo_local, hand_send)
    own = pltpu.make_async_copy(feed, window.at[:, halo], local_sem.at[count + 1])
    edges = spread_edge(seqs, edge, arrived, edge_send, edge_recv, True)
    for w in range(count):
        local[w].start()
    for item in line[0]:
        item.start()
    own.start()
    around.start()
    flat_local.start()
    for item in flat_row:
        item.start()
    for w in range(1, min(2, count)):
        for item in line[w]:
            item.start()
    units = rows * (chans // width)

    def last_unit(index, carry):
        row, base = unit_of(index, width, chans)
        ema_last(False, row, base, feed, keep, decay, edge, wide_feed)
        return carry

    def forward_unit(index, carry):
        row, base = unit_of(index, width, chans)
        ema_forward(row, base, feed, keep, decay, gain, entry, out, wide_feed, part)
        return carry

    def block_place(index):
        return lax.rem(index, rows), halo - lax.div(index, rows)

    def load_block(index):
        slot = lax.rem(index, 2)
        return pltpu.make_async_copy(window.at[block_place(index)], block_in.at[slot], in_sem.at[slot])

    def store_tiles(index):
        slot = lax.rem(index, 2)
        row, back_by = block_place(lax.div(index, tiles))
        columns = pl.ds(pl.multiple_of(lax.rem(index, tiles) * HOST_TILE, HOST_TILE), HOST_TILE)
        return [
            pltpu.make_async_copy(tile.at[slot], whole.at[row, back_by, :, columns], out_sem.at[at, slot])
            for at, (tile, whole) in enumerate(((value_tile, values), (slope_tile, slopes)))
        ]

    blocks = rows * (halo + 1)
    tiles = wholes[0].shape[-1] // HOST_TILE

    def value_unit(index, carry):
        block, slot = lax.div(index, tiles), lax.rem(index, 2)

        @pl.when(lax.rem(index, tiles) == 0)
        def _():
            load_block(block).wait()

            @pl.when(block + 1 < blocks)
            def _():
                load_block(block + 1).start()

        columns = pl.ds(pl.multiple_of(lax.rem(index, tiles) * HOST_TILE, HOST_TILE), HOST_TILE)
        part_weight = weight[:, :, :, :, :, columns].reshape(chans, HOST_TILE)
        before = product(block_in[lax.rem(block, 2)], part_weight)
        squash = jax.nn.sigmoid(before)

        @pl.when(index >= 2)
        def _():
            for item in store_tiles(index - 2):
                item.wait()

        value_tile[slot] = low(before * squash)
        slope_tile[slot] = low(squash * (1.0 + before * (1.0 - squash)))
        for item in store_tiles(index):
            item.start()
        return carry

    if hosts:
        near = Halo(
            halo, seqs, keys, key_window, zero.at[:, :, pl.ds(0, Z)], key_send, key_recv, key_local, key_hand
        )
        key_own = pltpu.make_async_copy(keys, key_window.at[:, halo], keys_sem.at[0])
        project_units = rows * (wholes[1].shape[-1] // PROJECT_TILE)
        mixed_copy = pltpu.make_async_copy(mixed, mixed_out, mixed_sem.at[0])

    def mix_row(row, carry):
        load = pltpu.make_async_copy(skip.at[row], skip_in, skip_sem.at[0])
        load.start()
        load.wait()
        before = out[row].astype(jnp.float32) + skip_in[...]
        mixed[row] = low(jax.nn.silu(before))
        return carry

    def store_project(index):
        slot = lax.rem(index, 2)
        columns = pl.ds(pl.multiple_of(lax.div(index, rows) * PROJECT_TILE, LANES), PROJECT_TILE)
        return pltpu.make_async_copy(
            project_tile.at[slot], projected.at[lax.rem(index, rows), :, columns], project_sem.at[slot]
        )

    def project_unit(index, carry):
        row, slot = lax.rem(index, rows), lax.rem(index, 2)
        columns = pl.ds(pl.multiple_of(lax.div(index, rows) * PROJECT_TILE, LANES), PROJECT_TILE)
        part_weight = mix_full[:, :, :, :, :, columns].reshape(chans, PROJECT_TILE)
        result = product(mixed[row], part_weight)

        @pl.when(index < rows)
        def _():
            keys[row] = low(jax.nn.silu(result[:, :Z]) * key_gain[...])

        @pl.when(index >= 2)
        def _():
            store_project(index - 2).wait()

        project_tile[slot] = result
        store_project(index).start()
        return carry

    lax.fori_loop(0, units, last_unit, 0)
    for item in edges:
        item.start()
    for step in range(count + 2):
        if step < count:
            w = step
            local[w].wait()
            for item in line[w]:
                item.wait_recv()
            for item in wide[w] + tall[w]:
                item.start()
            twin[w][0, 0].start()
            if w + 2 < count:
                for item in line[w + 2]:
                    item.start()
        if 1 <= step <= count:
            w = step - 1
            for k in range(1, across):
                wide[w][k - 1].wait_recv()
                for l in range(1, down):
                    cross[w][k, l][0].start()
                twin[w][0, k].start()
            for l in range(1, down):
                tall[w][l - 1].wait_recv()
                for k in range(1, across):
                    cross[w][k, l][1].start()
                twin[w][l, 0].start()
        if step >= 2:
            w = step - 2
            for (k, l), both in cross[w].items():
                both[0].wait_recv()
                both[1].wait_recv()
                twin[w][l, k].start()
        if step == 0:
            for item in edges:
                item.wait()
            join_edges(arrived, reach, power, entry)
        if step == 1:
            around.hand_on()
            flat_local.wait()
            for item in flat_row:
                item.wait_recv()
            for item in flat_line + flat_twin[:1]:
                item.start()
        if step == count:
            for item, on in zip(flat_line, flat_twin[1:]):
                item.wait_recv()
                on.start()
        if step < count - 1:
            lax.fori_loop(*share(units, count - 1, step), forward_unit, 0)
        if hosts and step == 2:
            for item in twin[0].values():
                item.wait_recv()
            full = pltpu.make_async_copy(wholes[0], weight, weight_sem.at[0])
            full.start()
            own.wait()
            around.wait()
            load_block(0).start()
            full.wait()
        if hosts and 2 <= step < count:
            lax.fori_loop(*share(blocks * tiles, count - 2, step - 2), value_unit, 0)
        if hosts and step == count - 1:
            lax.fori_loop(0, rows, mix_row, 0)
            mixed_copy.start()
            for w in (1, 2):
                for item in twin[w].values():
                    item.wait_recv()
            full_mix = pltpu.make_async_copy(wholes[1], mix_full, mix_sem.at[0])
            full_mix.start()
        if hosts and step == count:
            full_mix.wait()
            lax.fori_loop(0, rows, project_unit, 0)
            near.start()
            key_own.start()
            lax.fori_loop(rows, project_units // 2, project_unit, 0)
            near.hand_on()
        if hosts and step == count + 1:
            lax.fori_loop(project_units // 2, project_units, project_unit, 0)
    if hosts:
        for index in (blocks * tiles - 2, blocks * tiles - 1):
            for item in store_tiles(index):
                item.wait()
        for index in (project_units - 2, project_units - 1):
            store_project(index).wait()
        near.wait()
        key_own.wait()
        mixed_copy.wait()
    for item in flat_twin:
        item.wait()
    for item in flat_row + flat_line:
        item.wait_send()
    for w in range(count):
        for item in twin[w].values():
            item.wait_send()
            if w > 2 or not hosts:
                item.wait_recv()
        for item in line[w] + wide[w] + tall[w]:
            item.wait_send()
        for both in cross[w].values():
            both[0].wait_send()
            both[1].wait_send()
    if not hosts:
        own.wait()
        around.wait()


def vmem(count):
    return [pl.BlockSpec(memory_space=pltpu.VMEM)] * count


def anywhere(count):
    return [pl.BlockSpec(memory_space=pl.ANY)] * count


def gather_weights(shards, feed, keep, decay, gain, reach, power, halo, skip, key_gain):
    sizes = shape_of()
    depth, cores, down, across = sizes
    seqs = down * across
    count = len(shards)
    pieces = [piece_shape(*shard.shape) for shard in shards]
    slots = (depth - 1) + (across - 1) + (down - 1) + 2 * (across - 1) * (down - 1) + across * down
    rows, length, chans = feed.shape
    state = (rows, 16, chans)
    width = min(FORWARD_WIDTH, chans)
    hosts = pieces[0] == shards[0].shape and shards[1].shape[1] % PROJECT_TILE == 0
    chunks = chunks_of(pieces)
    made, extra = [], []
    if hosts:
        wide = shards[0].shape[1]
        made = [jax.ShapeDtypeStruct((rows, halo + 1, length, wide), jnp.bfloat16)] * 2
        made += [
            jax.ShapeDtypeStruct(feed.shape, jnp.bfloat16),
            jax.ShapeDtypeStruct((rows, length, shards[1].shape[1]), jnp.float32),
            jax.ShapeDtypeStruct((rows, halo + 1, length, Z), jnp.bfloat16),
        ]
        extra = [
            pltpu.VMEM(sizes + pieces[1], jnp.bfloat16),
            pltpu.SemaphoreType.DMA((1,)),
            pltpu.VMEM((length, chans), jnp.float32),
            pltpu.SemaphoreType.DMA((1,)),
            pltpu.VMEM(feed.shape, jnp.bfloat16),
            pltpu.VMEM((2, length, PROJECT_TILE), jnp.float32),
            pltpu.SemaphoreType.DMA((2,)),
            pltpu.VMEM((rows, length, Z), jnp.bfloat16),
            pltpu.SemaphoreType.DMA((1,)),
            pltpu.SemaphoreType.DMA((1,)),
            pltpu.SemaphoreType.DMA((halo,)),
            pltpu.SemaphoreType.DMA((halo,)),
            pltpu.SemaphoreType.DMA((halo,)),
            pltpu.SemaphoreType.DMA((1,)),
            pltpu.VMEM(sizes + pieces[0], jnp.bfloat16),
            pltpu.VMEM((2, length, chans), jnp.bfloat16),
            pltpu.VMEM((2, length, HOST_TILE), jnp.bfloat16),
            pltpu.VMEM((2, length, HOST_TILE), jnp.bfloat16),
            pltpu.SemaphoreType.DMA((1,)),
            pltpu.SemaphoreType.DMA((2,)),
            pltpu.SemaphoreType.DMA((2, 2)),
        ]
    results = pl.pallas_call(
        functools.partial(gather_kernel, sizes, count, halo, hosts, chunks),
        out_shape=[jax.ShapeDtypeStruct(sizes + piece, jnp.bfloat16) for piece in pieces]
        + [
            jax.ShapeDtypeStruct((rows, halo + 1, length, chans), jnp.bfloat16),
            jax.ShapeDtypeStruct(state, jnp.float32),
            jax.ShapeDtypeStruct(feed.shape, jnp.bfloat16),
        ]
        + made,
        in_specs=anywhere(count) + vmem(6) + (anywhere(1) + vmem(1) if hosts else []),
        out_specs=anywhere(count + 1) + vmem(2) + anywhere(len(made)),
        scratch_shapes=[
            pltpu.SemaphoreType.DMA((len(chunks), slots)),
            pltpu.SemaphoreType.DMA((len(chunks), slots)),
            pltpu.SemaphoreType.DMA((len(chunks) + 1,)),
            pltpu.VMEM(state, jnp.float32),
            pltpu.VMEM((seqs - 1,) + state, jnp.float32),
            pltpu.SemaphoreType.DMA((seqs - 1,)),
            pltpu.SemaphoreType.DMA((seqs - 1,)),
            pltpu.VMEM(feed.shape, jnp.bfloat16),
            pltpu.SemaphoreType.DMA((halo,)),
            pltpu.SemaphoreType.DMA((halo,)),
            pltpu.SemaphoreType.DMA((halo,)),
            pltpu.SemaphoreType.DMA((1,)),
            pltpu.VMEM((width // LANES, length, LANES), jnp.float32),
            pltpu.VMEM((width // LANES * EMA_STEP * 8, LANES), jnp.float32),
            *extra,
        ],
        compiler_params=pltpu.CompilerParams(collective_id=0, has_side_effects=True, vmem_limit_bytes=48 * 2**20),
        name="gather_weights",
    )(*[shard.reshape(piece) for shard, piece in zip(shards, pieces)], feed, keep, decay, gain, reach, power, *([skip, key_gain] if hosts else []))
    total = depth * cores * down * across
    wholes = [whole.reshape(total * shard.shape[0], shard.shape[1]) for whole, shard in zip(results, shards)]
    return wholes, *results[count:]


def add_rows(target, total, others):
    rows = total.shape[0]
    chunk = 16 if rows % 16 == 0 else rows

    def body(index, carry):
        at = pl.ds(pl.multiple_of(index * chunk, chunk), chunk)
        result = total[at, :].astype(jnp.float32)
        for other in others:
            result = result + other[at, :].astype(jnp.float32)
        target[at, :] = result.astype(target.dtype)
        return carry

    lax.fori_loop(0, rows // chunk, body, 0)


def scatter_kernel(sizes, count, chunks, *refs):
    grads, small = refs[:count], refs[count]
    feed, grad, keep, decay, gain, start, reach, power = refs[count + 1 : count + 9]
    refs = refs[count + 9 :]
    outs, (small_out, back_out) = refs[:count], refs[count : count + 2]
    rest = refs[count + 2 :]
    rest, (
        edge, arrived, end, edge_send, edge_recv, wide, wide_grad, part, kept_states,
    ) = rest[:-9], rest[-9:]
    rows, length, chans = feed.shape
    width = wide.shape[0] * LANES
    seqs = sizes[2] * sizes[3]
    count = len(chunks)
    names = ("arrive", "own", "first_a", "first_b", "second_a", "second_b", "third")
    held = {name: rest[at * count : (at + 1) * count] for at, name in enumerate(names)}
    flat_planes, flat_pieces, small_parts, send_sem, recv_sem, own_sem, small_send, small_recv = rest[len(names) * count :]
    depth, cores, down, across = sizes
    spot = place_of()
    z, c, a, b = spot
    half = depth // 2
    front, back = pl.ds(0, half), pl.ds(half, depth - half)
    greet(sizes, spot)
    slots = {}

    def copy(w, kind, source, target, axis, by):
        slot = slots.setdefault(kind, len(slots))
        return pltpu.make_async_remote_copy(
            src_ref=source,
            dst_ref=target,
            send_sem=send_sem.at[w, slot],
            recv_sem=recv_sem.at[w, slot],
            device_id=peer_of(sizes, spot, axis, by),
            device_id_type=MESH,
        )

    def at_a(by):
        return lax.rem(a + by, down)

    def at_b(by):
        return lax.rem(b + by, across)

    twin, first, second, third = [], [], [], []
    for w in range(count):
        arrive = held["arrive"][w]
        twin.append(copy(w, "c", grads[chunks[w][0]].at[:, 1 - c, :, :, :, chunks[w][1]], arrive, 1, 1))
        first.append(
            [
                copy(w, ("a1", k), arrive.at[front, :, at_b(k)], held["first_a"][w].at[k - 1], 3, k)
                for k in range(1, across)
            ]
            + [
                copy(w, ("b1", l), arrive.at[back, at_a(l)], held["first_b"][w].at[l - 1], 2, l)
                for l in range(1, down)
            ]
        )
        second.append(
            [
                copy(w, ("a2", l), arrive.at[front, at_a(l), b], held["second_a"][w].at[l - 1], 2, l)
                for l in range(1, down)
            ]
            + [
                copy(w, ("b2", k), arrive.at[back, a, at_b(k)], held["second_b"][w].at[k - 1], 3, k)
                for k in range(1, across)
            ]
        )
        third.append(
            [
                copy(w, ("z", k), arrive.at[lax.rem(z + k, depth), a, b], held["third"][w].at[k - 1], 0, k)
                for k in range(1, depth)
            ]
        )

    stages = [(axis, 1 << bit) for axis in (1, 2, 3, 0) for bit in range(sizes[axis].bit_length() - 1)]

    def small_copy(at):
        axis, bit = stages[at]
        mine = spot[axis]
        towards = jnp.where(lax.rem(mine // bit, 2) == 0, bit, sizes[axis] - bit)
        return pltpu.make_async_remote_copy(
            src_ref=small_out,
            dst_ref=small_parts.at[at],
            send_sem=small_send.at[at],
            recv_sem=small_recv.at[at],
            device_id=peer_of(sizes, spot, axis, towards),
            device_id_type=MESH,
        )

    def own_load(w, at):
        return pltpu.make_async_copy(grads[chunks[w][0]].at[at, c, :, :, :, chunks[w][1]], held["own"][w].at[lax.rem(at, 2)], own_sem.at[w, lax.rem(at, 2)])

    def add_own(w):
        own_load(w, 0).start()

        def body(at, carry):
            @pl.when(at + 1 < depth)
            def _():
                own_load(w, at + 1).start()

            own_load(w, at).wait()
            for down_at in range(down):
                for across_at in range(across):
                    spot_ref = held["arrive"][w].at[at, down_at, across_at]
                    add_rows(spot_ref, spot_ref, [held["own"][w].at[lax.rem(at, 2), down_at, across_at]])
            return carry

        lax.fori_loop(0, depth, body, 0)

    flat = count - 1
    count = flat
    flat_arrive = held["arrive"][flat]

    def flat_copy(slot, source, target, device):
        return pltpu.make_async_remote_copy(
            src_ref=source,
            dst_ref=target,
            send_sem=send_sem.at[flat, slot],
            recv_sem=recv_sem.at[flat, slot],
            device_id=device,
            device_id_type=MESH,
        )

    flat_line = [
        flat_copy(k, flat_arrive.at[lax.rem(z + k, depth)], flat_planes.at[k - 1], peer_of(sizes, spot, 0, k))
        for k in range(1, depth)
    ]
    flat_row = []
    for by in range(1, seqs):
        to = lax.rem(a * across + b + by, seqs)
        source = flat_arrive.at[z, lax.div(to, across), lax.rem(to, across)]
        flat_row.append(flat_copy(depth - 1 + by, source, flat_pieces.at[by - 1], along(seqs, by)))

    def flat_pair():
        twin[flat].wait_recv()
        add_own(flat)
        for item in flat_line:
            item.start()

    def flat_sum():
        for item in flat_line:
            item.wait_recv()
        for down_at in range(down):
            for across_at in range(across):
                spot_ref = flat_arrive.at[z, down_at, across_at]
                add_rows(spot_ref, spot_ref, [flat_planes.at[k, down_at, across_at] for k in range(depth - 1)])
        for item in flat_row:
            item.start()

    def flat_finish():
        for item in flat_row:
            item.wait_recv()
        out = outs[chunks[flat][0]].at[:, chunks[flat][1]]
        add_rows(out, flat_arrive.at[z, a, b], [flat_pieces.at[at] for at in range(seqs - 1)])

    small_out[...] = small[...]
    edges = spread_edge(seqs, edge, arrived, edge_send, edge_recv, False)
    units = rows * (chans // width)

    def last_unit(index, carry):
        row, base = unit_of(index, width, chans)
        ema_last(True, row, base, grad, keep, decay, edge, wide)
        return carry

    def backward_unit(index, carry):
        row, base = unit_of(index, width, chans)
        ema_backward(
            row, base, feed, grad, keep, decay, gain, start, end, back_out, small_out, wide, wide_grad, part, kept_states
        )
        return carry

    for w in range(min(2, count)):
        twin[w].start()
    twin[flat].start()
    busy = count - 1
    for step in range(max(count + 3, busy + len(stages))):
        if step < count:
            w = step
            twin[w].wait_recv()
            if w + 2 < count:
                twin[w + 2].start()
            add_own(w)
            for item in first[w]:
                item.start()
        if step == 0:
            flat_pair()
        if step == 2:
            flat_sum()
        if step == 4:
            flat_finish()
        if 1 <= step <= count:
            w = step - 1
            arrive = held["arrive"][w]
            for item in first[w]:
                item.wait_recv()
            for at in range(half):
                for l in range(down):
                    spot_ref = arrive.at[at, l, b]
                    add_rows(spot_ref, spot_ref, [held["first_a"][w].at[k, at, l] for k in range(across - 1)])
            for at in range(half, depth):
                for k in range(across):
                    spot_ref = arrive.at[at, a, k]
                    add_rows(spot_ref, spot_ref, [held["first_b"][w].at[l, at - half, k] for l in range(down - 1)])
            for item in second[w]:
                item.start()
        if 2 <= step <= count + 1:
            w = step - 2
            arrive = held["arrive"][w]
            for item in second[w]:
                item.wait_recv()
            for at in range(half):
                spot_ref = arrive.at[at, a, b]
                add_rows(spot_ref, spot_ref, [held["second_a"][w].at[l, at] for l in range(down - 1)])
            for at in range(half, depth):
                spot_ref = arrive.at[at, a, b]
                add_rows(spot_ref, spot_ref, [held["second_b"][w].at[k, at - half] for k in range(across - 1)])
            for item in third[w]:
                item.start()
        if 3 <= step <= count + 2:
            w = step - 3
            for item in third[w]:
                item.wait_recv()
            add_rows(outs[chunks[w][0]].at[:, chunks[w][1]], held["arrive"][w].at[z, a, b], [held["third"][w].at[k] for k in range(depth - 1)])
        if step == 0:
            lax.fori_loop(0, units, last_unit, 0)
            for item in edges:
                item.start()
        if step == 1:
            for item in edges:
                item.wait()
            join_edges(arrived, reach, power, end)
        if 1 <= step < busy:
            lax.fori_loop(*share(units, busy - 1, step - 1), backward_unit, 0)
        stage = step - busy
        if stage == -1:
            small_copy(0).start()
        if 0 <= stage < len(stages):
            small_copy(stage).wait()
            small_out[...] = small_out[...] + small_parts[stage]
            if stage + 1 < len(stages):
                small_copy(stage + 1).start()
    for item in [twin[flat]] + flat_line + flat_row:
        item.wait_send()
    for w in range(count):
        for item in [twin[w]] + first[w] + second[w] + third[w]:
            item.wait_send()


def scatter_grads(grads, small, feed, grad, keep, decay, gain, start, reach, power):
    sizes = shape_of()
    depth, cores, down, across = sizes
    total = depth * cores * down * across
    count = len(grads)
    half = depth // 2
    pieces = [piece_shape(g.shape[0] // total, g.shape[1]) for g in grads]
    leads = (
        (depth, down, across),
        (2, down, across),
        (across - 1, half, down),
        (down - 1, depth - half, across),
        (down - 1, half),
        (across - 1, depth - half),
        (depth - 1,),
    )
    slots = max(2 * (across - 1 + down - 1), down * across - 1) + depth
    stages = sum(size.bit_length() - 1 for size in sizes)
    chunks = chunks_of(pieces)
    parts = [(pieces[at][0], columns.size) for at, columns in chunks]
    rows, length, chans = feed.shape
    state = (rows, 16, chans)
    width = min(BACKWARD_WIDTH, chans)
    seqs = down * across
    results = pl.pallas_call(
        functools.partial(scatter_kernel, sizes, count, chunks),
        out_shape=[jax.ShapeDtypeStruct(piece, jnp.float32) for piece in pieces]
        + [
            jax.ShapeDtypeStruct(small.shape, jnp.float32),
            jax.ShapeDtypeStruct(feed.shape, jnp.bfloat16),
        ],
        in_specs=anywhere(count) + vmem(9),
        out_specs=vmem(count + 2),
        scratch_shapes=[pltpu.VMEM(lead + part, jnp.bfloat16) for lead in leads for part in parts]
        + [pltpu.VMEM((depth - 1, down, across) + parts[-1], jnp.bfloat16), pltpu.VMEM((down * across - 1,) + parts[-1], jnp.bfloat16)]
        + [
            pltpu.VMEM((stages,) + small.shape, jnp.float32),
            pltpu.SemaphoreType.DMA((len(chunks), slots)),
            pltpu.SemaphoreType.DMA((len(chunks), slots)),
            pltpu.SemaphoreType.DMA((len(chunks), 2)),
            pltpu.SemaphoreType.DMA((stages,)),
            pltpu.SemaphoreType.DMA((stages,)),
            pltpu.VMEM(state, jnp.float32),
            pltpu.VMEM((seqs - 1,) + state, jnp.float32),
            pltpu.VMEM(state, jnp.float32),
            pltpu.SemaphoreType.DMA((seqs - 1,)),
            pltpu.SemaphoreType.DMA((seqs - 1,)),
            pltpu.VMEM((width // LANES, length, LANES), jnp.float32),
            pltpu.VMEM((width // LANES, length, LANES), jnp.float32),
            pltpu.VMEM((width // LANES * EMA_STEP * 8, LANES), jnp.float32),
            pltpu.VMEM((length * 16, width), jnp.float32),
        ],
        compiler_params=pltpu.CompilerParams(collective_id=1, has_side_effects=True, vmem_limit_bytes=62 * 2**20),
        name="scatter_grads",
    )(
        *[g.reshape(sizes + piece) for g, piece in zip(grads, pieces)],
        small, feed, grad, keep, decay, gain, start, reach, power,
    )
    sums = [result.reshape(g.shape[0] // total, g.shape[1]) for result, g in zip(results[:count], grads)]
    return sums, *results[count:]


def passed_on(alive, forward):
    count = lax.axis_size("seq")
    place = lax.axis_index("seq")
    through = jnp.ones((alive.shape[0], 1, 1), jnp.float32)
    factors = []
    for away in range(1, count):
        exists = place >= away if forward else place + away < count
        factors.append(jnp.broadcast_to(jnp.where(exists, through, 0.0), (alive.shape[0], 16, LANES)))
        at = jnp.clip(place - away if forward else place + away, 0, count - 1)
        through = through * lax.dynamic_slice_in_dim(alive, at, 1, 1)[:, :, None]
    return jnp.stack(factors)


QUERY_BLOCK = 256
KEY_BLOCK = 768
VALUE_BLOCK = 1024


def attend_kernel(halo_span, query, key, value, key_docs, query_docs, gates, out, gated, probs):
    size, span = probs.shape
    first = pl.program_id(1) * size
    keys = pl.ds(pl.multiple_of(first, LANES), span)
    scores = against(query[0], key[0, keys, :]) * Z ** (-0.5)
    query_at = lax.broadcasted_iota(jnp.int32, (size, span), 0) + halo_span
    key_at = lax.broadcasted_iota(jnp.int32, (size, span), 1)
    allowed = (key_at <= query_at) & (key_docs[0, :, keys] == query_docs[0])
    scores = jnp.where(allowed, scores, NEG_FILL)
    expo = jnp.exp(scores - jnp.max(scores, axis=1, keepdims=True))
    probs[...] = low(expo / jnp.sum(expo, axis=1, keepdims=True))

    def body(at, carry):
        columns = pl.ds(pl.multiple_of(at * VALUE_BLOCK, VALUE_BLOCK), VALUE_BLOCK)
        gate = jax.nn.silu(gates[0, :, pl.ds(pl.multiple_of(Z + at * VALUE_BLOCK, LANES), VALUE_BLOCK)])
        local = product(probs[...], value[0, keys, columns])
        out[0, :, columns] = local
        gated[0, :, columns] = low(gate * local)
        return carry

    lax.fori_loop(0, out.shape[2] // VALUE_BLOCK, body, 0)


def attend(query, key, value, docs_row, docs_column, gates, halo):
    rows, places, _ = query.shape
    window, wide = value.shape[1:]
    size = min(QUERY_BLOCK, places)
    span = halo * places + size
    return pl.pallas_call(
        functools.partial(attend_kernel, halo * places),
        out_shape=[
            jax.ShapeDtypeStruct((rows, places, wide), jnp.float32),
            jax.ShapeDtypeStruct((rows, places, wide), jnp.bfloat16),
        ],
        grid=(rows, places // size),
        in_specs=[
            pl.BlockSpec((1, size, Z), lambda r, i: (r, i, 0)),
            pl.BlockSpec((1, window, Z), lambda r, i: (r, 0, 0)),
            pl.BlockSpec((1, window, wide), lambda r, i: (r, 0, 0)),
            pl.BlockSpec((1, 1, window), lambda r, i: (r, 0, 0)),
            pl.BlockSpec((1, size, 1), lambda r, i: (r, i, 0)),
            pl.BlockSpec((1, size, gates.shape[2]), lambda r, i: (r, i, 0)),
        ],
        out_specs=[pl.BlockSpec((1, size, wide), lambda r, i: (r, i, 0))] * 2,
        scratch_shapes=[pltpu.VMEM((size, span), jnp.bfloat16)],
        compiler_params=pltpu.CompilerParams(vmem_limit_bytes=48 * 2**20),
        cost_estimate=pl.CostEstimate(
            flops=2 * rows * places * span * (wide + Z),
            bytes_accessed=rows * (window * wide * 2 + places * wide * 4),
            transcendentals=rows * places * span,
        ),
        name="attend",
    )(query, key, value, docs_row, docs_column[:, halo * places :], gates)


def attend_back_kernel(
    halo_span, query, key, value, slope, pulled, key_docs, query_docs, d_query, d_key, d_value, chances, pulls, balance
):
    window, places = chances.shape
    step = d_value.shape[1]
    chunk = pl.program_id(1)

    @pl.when(chunk == 0)
    def _():
        peak = jnp.full((1, places), NEG_FILL, jnp.float32)

        def score(at, peak):
            keys = pl.ds(pl.multiple_of(at * step, step), step)
            scores = against(key[0, keys, :], query[0]) * Z ** (-0.5)
            key_at = lax.broadcasted_iota(jnp.int32, (step, places), 0) + at * step
            query_at = lax.broadcasted_iota(jnp.int32, (step, places), 1) + halo_span
            allowed = (key_at <= query_at) & (key_docs[0, keys, :] == query_docs[0])
            scores = jnp.where(allowed, scores, NEG_FILL)
            chances[keys, :] = scores
            return jnp.maximum(peak, jnp.max(scores, axis=0, keepdims=True))

        peak = lax.fori_loop(0, window // step, score, peak)

        def weigh(at, total):
            keys = pl.ds(pl.multiple_of(at * step, step), step)
            expo = jnp.exp(chances[keys, :] - peak)
            chances[keys, :] = expo
            return total + jnp.sum(expo, axis=0, keepdims=True)

        portion = 1.0 / lax.fori_loop(0, window // step, weigh, jnp.zeros((1, places), jnp.float32))

        def pull(at, held):
            keys = pl.ds(pl.multiple_of(at * step, step), step)
            probs = chances[keys, :] * portion
            chances[keys, :] = probs
            local = against(value[0, keys, :], pulled[0])
            pulls[keys, :] = local
            return held + jnp.sum(probs * local, axis=0, keepdims=True)

        balance[...] = lax.fori_loop(0, window // step, pull, jnp.zeros((1, places), jnp.float32))
        d_query[...] = jnp.zeros_like(d_query)

    keys = pl.ds(pl.multiple_of(chunk * step, step), step)
    probs = chances[keys, :]
    d_scores = low(probs * (pulls[keys, :] - balance[...]))
    d_key[0] = product(d_scores, query[0]) * Z ** (-0.5)
    d_query[0] = d_query[0] + transposed(d_scores, key[0, keys, :]) * Z ** (-0.5)
    probs_low = low(probs)

    def body(at, carry):
        columns = pl.ds(pl.multiple_of(at * VALUE_BLOCK, VALUE_BLOCK), VALUE_BLOCK)
        local = product(probs_low, pulled[0, :, columns])
        d_value[0, :, columns] = low(local * slope[0, :, columns].astype(jnp.float32))
        return carry

    lax.fori_loop(0, d_value.shape[2] // VALUE_BLOCK, body, 0)


def attend_back(query, key, value, slope, pulled, docs_row, docs_column, halo):
    rows, places, _ = query.shape
    window, wide = value.shape[1:]
    step = KEY_BLOCK if window % KEY_BLOCK == 0 else places
    return pl.pallas_call(
        functools.partial(attend_back_kernel, halo * places),
        out_shape=[
            jax.ShapeDtypeStruct((rows, places, Z), jnp.float32),
            jax.ShapeDtypeStruct((rows, window, Z), jnp.float32),
            jax.ShapeDtypeStruct((rows, window, wide), jnp.bfloat16),
        ],
        grid=(rows, window // step),
        in_specs=[
            pl.BlockSpec((1, places, Z), lambda r, i: (r, 0, 0)),
            pl.BlockSpec((1, window, Z), lambda r, i: (r, 0, 0)),
            pl.BlockSpec((1, window, wide), lambda r, i: (r, 0, 0)),
            pl.BlockSpec((1, step, wide), lambda r, i: (r, i, 0)),
            pl.BlockSpec((1, places, wide), lambda r, i: (r, 0, 0)),
            pl.BlockSpec((1, window, 1), lambda r, i: (r, 0, 0)),
            pl.BlockSpec((1, 1, places), lambda r, i: (r, 0, 0)),
        ],
        out_specs=[
            pl.BlockSpec((1, places, Z), lambda r, i: (r, 0, 0)),
            pl.BlockSpec((1, step, Z), lambda r, i: (r, i, 0)),
            pl.BlockSpec((1, step, wide), lambda r, i: (r, i, 0)),
        ],
        scratch_shapes=[
            pltpu.VMEM((window, places), jnp.float32),
            pltpu.VMEM((window, places), jnp.float32),
            pltpu.VMEM((1, places), jnp.float32),
        ],
        compiler_params=pltpu.CompilerParams(vmem_limit_bytes=48 * 2**20),
        cost_estimate=pl.CostEstimate(
            flops=4 * rows * places * window * (wide + Z),
            bytes_accessed=rows * (window * wide * 6 + places * wide * 2),
            transcendentals=rows * places * window,
        ),
        name="attend_back",
    )(query, key, value, slope, pulled, docs_column, docs_row[:, :, halo * places :])


def on_device(
    layer_input,
    cotangent,
    doc_ids,
    resets,
    mix_weight,
    value_weight,
    head_weight,
    expand_weight,
    shrink_weight,
    chan_vectors,
    ema_logits,
    ema_beta_eta,
    z_affine,
):
    seq_count = lax.axis_size("seq")
    seq_place = lax.axis_index("seq")
    rows, places, width = layer_input.shape
    tokens = rows * places
    halo = min(-(-(REACH - 1) // places), seq_count - 1)
    window = (halo + 1) * places

    inputs32 = layer_input.astype(jnp.float32)
    center = inputs32 - jnp.mean(inputs32, axis=-1, keepdims=True)
    unit = lax.rsqrt(jnp.mean(center * center, axis=-1, keepdims=True) + 1e-05)
    plain = center * unit
    normed = plain * chan_vectors[0]
    normed_low = low(normed)

    rate = jax.nn.sigmoid(ema_logits[0])
    damping = jax.nn.sigmoid(ema_logits[1])
    decay = (1.0 - rate * damping).T
    weight_in = rate * ema_beta_eta[0]
    weight_out = ema_beta_eta[1]
    gain = (weight_in * weight_out).T
    decay_all = decay
    reach = 1
    while reach < places:
        decay_all = decay_all * decay_all
        reach *= 2
    powers = [jnp.ones_like(decay)]
    while len(powers) < seq_count - 1:
        powers.append(powers[-1] * decay_all)
    power = jnp.stack(powers)
    keep_row = 1.0 - resets.astype(jnp.float32)
    keep_own = lax.dynamic_slice_in_dim(keep_row, seq_place * places, places, 1)
    keep = jnp.broadcast_to(keep_own[:, None, :, None], (rows, 1, places, LANES)).reshape(rows, places, LANES)
    alive = jnp.min(keep_row.reshape(rows, seq_count, places), axis=2)

    (value_full, mix_full, expand_full, head_full), normed_window, start, ema_low, *made = gather_weights(
        (value_weight, mix_weight, expand_weight, head_weight),
        normed_low,
        keep,
        decay,
        gain,
        passed_on(alive, True),
        power,
        halo,
        chan_vectors[2] * normed,
        z_affine[2:3],
    )
    normed_window = normed_window.reshape(rows * window, width)
    value_full, mix_full, head_full, expand_full, shrink_late = lax.optimization_barrier(
        (value_full, mix_full, head_full, expand_full, shrink_weight)
    )
    shrink_full = lax.all_gather(shrink_late, BOTH, axis=0, tiled=True)

    premix = (ema_low.astype(jnp.float32) + chan_vectors[2] * normed).reshape(tokens, width)
    if made:
        values_low, value_slope = (item.reshape(rows, window, V) for item in made[:2])
        mixed_low = made[2].reshape(tokens, width)
        projected = made[3].reshape(tokens, made[3].shape[2])
        key_window = made[4].reshape(rows, window, Z)
        shared_pre = projected[:, :Z]
        shared = jax.nn.silu(shared_pre)
        queries_low = low(shared * z_affine[0] + z_affine[1]).reshape(rows, places, Z)
    else:
        mixed_low = low(jax.nn.silu(premix))
        value_pre = product(normed_window, value_full)
        values_low = low(jax.nn.silu(value_pre)).reshape(rows, window, V)
        value_slope = low(silu_slope(value_pre)).reshape(rows, window, V)
        projected = product(mixed_low, mix_full)
        shared_pre = projected[:, :Z]
        shared = jax.nn.silu(shared_pre)
        queries_low = low(shared * z_affine[0] + z_affine[1]).reshape(rows, places, Z)
        keys_low = low(shared * z_affine[2]).reshape(rows, places, Z)
        keys_sent = [shift_seq(keys_low, by) for by in range(halo, 0, -1)]
        key_window = jnp.concatenate(keys_sent + [keys_low], axis=1)
    reset_pre = projected[:, Z : Z + V]
    head_base = projected[:, Z + V : Z + V + width]
    update_pre = projected[:, Z + V + width :]
    reset_gate = jax.nn.silu(reset_pre)
    update_gate = jax.nn.sigmoid(update_pre)

    padded_docs = jnp.pad(doc_ids, ((0, 0), (halo * places, 0)), constant_values=-1)
    key_docs = lax.dynamic_slice_in_dim(padded_docs, seq_place * places, window, 1)
    docs_row, docs_column = key_docs[:, None, :], key_docs[:, :, None]
    gates = projected.reshape(rows, places, projected.shape[1])
    attended, gated_low = attend(queries_low, key_window, values_low, docs_row, docs_column, gates, halo)
    attended, gated_low = attended.reshape(tokens, V), gated_low.reshape(tokens, V)
    head_pre = head_base + product(gated_low, head_full)
    candidate = jax.nn.silu(head_pre)
    residual_in = inputs32.reshape(tokens, width)
    first = residual_in + update_gate * (candidate - residual_in)
    second, second_pull = jax.vjp(scaled_norm, first, chan_vectors[1])
    second_low = low(second)
    expand_pre = product(second_low, expand_full)
    expand_slope = silu_slope(expand_pre)
    hidden_low, expand_slope = lax.optimization_barrier((low(jax.nn.silu(expand_pre)), expand_slope))
    output = low(first + product(hidden_low, shrink_full)).reshape(rows, places, width)

    cot_low = cotangent.reshape(tokens, width)
    shrink_part = low(transposed(hidden_low, cot_low))
    d_expand = low(against(cot_low, shrink_full) * expand_slope)
    d_first_norm, d_gain_two = second_pull(against(d_expand, expand_full))
    d_first = cot_low.astype(jnp.float32) + d_first_norm
    d_update = d_first * (candidate - residual_in) * update_gate * (1.0 - update_gate)
    d_direct = d_first * (1.0 - update_gate)
    d_head = d_first * update_gate * silu_slope(head_pre)
    d_head_low = low(d_head)
    d_gated = against(d_head_low, head_full)
    d_reset = d_gated * attended * silu_slope(reset_pre)
    d_attended = low(d_gated * reset_gate).reshape(rows, places, V)
    d_queries, key_term, d_value_pre = attend_back(
        queries_low, key_window, values_low, value_slope, d_attended, docs_row, docs_column, halo
    )
    d_value_pre, second_late, gated_late = lax.optimization_barrier((d_value_pre, second_low, gated_low))
    expand_part = low(transposed(second_late, d_expand))
    head_part = low(transposed(gated_late, d_head_low))
    d_value_pre = d_value_pre.reshape(rows * window, V)
    d_keys = key_term[:, halo * places :]
    for by in range(1, halo + 1):
        begin = (halo - by) * places
        d_keys = d_keys + shift_seq(low(key_term[:, begin : begin + places]), -by).astype(jnp.float32)
    d_keys32 = low(d_keys).astype(jnp.float32).reshape(tokens, Z)
    value_part = low(transposed(normed_window, d_value_pre))
    value_term = against(d_value_pre, value_full).reshape(rows, halo + 1, places, width)
    terms = low(value_term[:, :halo])
    d_normed_value = value_term[:, halo]
    for by in range(1, halo + 1):
        d_normed_value = d_normed_value + shift_seq(terms[:, halo - by], -by).astype(jnp.float32)
    d_query_flat = d_queries.reshape(tokens, Z)
    d_shared = d_query_flat * z_affine[0] + d_keys32 * z_affine[2]
    affine_part = jnp.stack(
        [
            jnp.sum(d_query_flat * shared, axis=0),
            jnp.sum(d_query_flat, axis=0),
            jnp.sum(d_keys32 * shared, axis=0),
        ]
    )
    d_projected = low(
        jnp.concatenate([d_shared * silu_slope(shared_pre), d_reset, d_head, d_update], axis=1)
    )
    mix_part = low(transposed(mixed_low, d_projected))
    d_premix = against(d_projected, mix_full) * silu_slope(premix)
    omega_part = jnp.sum(d_premix * normed.reshape(tokens, width), axis=0)
    d_premix = d_premix.reshape(rows, places, width)
    d_ema = low(d_premix)
    known = d_premix * chan_vectors[2] + d_normed_value
    d_gain_one = jnp.sum(known * plain, axis=(0, 1))
    small_part = jnp.concatenate(
        [
            jnp.zeros((32, width), jnp.float32),
            jnp.stack([d_gain_one, d_gain_two, omega_part]),
            jnp.pad(affine_part.reshape(1, 3 * Z), ((0, 4), (0, width - 3 * Z))),
        ],
        axis=0,
    )
    (shrink_grad, expand_grad, value_grad, mix_grad, head_grad), small_sum, d_feed = scatter_grads(
        (shrink_part, expand_part, value_part, mix_part, head_part),
        small_part,
        normed_low,
        d_ema,
        keep,
        decay,
        gain,
        start,
        passed_on(alive, False),
        power,
    )
    d_normed = known + d_feed.astype(jnp.float32)
    pulled = d_normed * chan_vectors[0]
    pulled = pulled - jnp.mean(pulled, axis=-1, keepdims=True) - plain * jnp.mean(pulled * plain, axis=-1, keepdims=True)
    x_grad = d_direct.reshape(rows, places, width) + pulled * unit
    gain_sum = small_sum[:16]
    decay_sum = small_sum[16:32]
    chan_grad = small_sum[32:35].at[0].add(jnp.sum(gain * gain_sum, axis=0) / chan_vectors[0])
    affine_grad = small_sum[35, : 3 * Z].reshape(3, Z)
    d_gain = gain_sum.T
    d_decay = (decay_sum * gain).T
    d_weight_in = d_gain * weight_out
    coef_grad = jnp.stack([d_weight_in * rate, d_gain * weight_in])
    d_rate = d_weight_in * ema_beta_eta[0] - d_decay * damping
    d_damping = -d_decay * rate
    logits_grad = jnp.stack([d_rate * rate * (1.0 - rate), d_damping * damping * (1.0 - damping)])
    return (
        output,
        x_grad,
        mix_grad,
        value_grad,
        head_grad,
        expand_grad,
        shrink_grad,
        chan_grad,
        logits_grad,
        coef_grad,
        affine_grad,
    )


def solution(mesh):
    placed = (
        P("dp", "seq", None),
        P("dp", "seq", None),
        P("dp", None),
        P("dp", None),
        P(BOTH, None),
        P(BOTH, None),
        P(BOTH, None),
        P(BOTH, None),
        P(BOTH, None),
        P(),
        P(),
        P(),
        P(),
    )
    return jax.shard_map(
        on_device,
        mesh=mesh,
        in_specs=placed,
        out_specs=(
            P("dp", "seq", None),
            P("dp", "seq", None),
            P(BOTH, None),
            P(BOTH, None),
            P(BOTH, None),
            P(BOTH, None),
            P(BOTH, None),
            P(),
            P(),
            P(),
            P(),
        ),
        check_vma=False,
    )
```
